512 devices in a mesh: expert: 64 (over z, x), dp: 8 (over y, core).
Axes of the slice: x: 4, y: 4, z: 16, core: 2. Of those that a mesh axis runs over, the one named last changes fastest.
Arguments:
- tokens: bfloat16 [32768, 2048], P(('expert', 'dp')), may hold values from -6 to 6
- attn_partials: bfloat16 [8, 32768, 2048], P('dp', 'expert'), may hold values from -5 to 5
- expert_ids: int32 [32768], P(('expert', 'dp')), may hold values from 0 to 3, as said below
- gate: float32 [32768], P(('expert', 'dp')), may hold values from 0.2 to 1
- w_in: float32 [2048, 20480], P('dp', 'expert'), may hold values from -6 to 6
- w_out: float32 [2048, 20480], P('dp', 'expert'), may hold values from -6 to 6
Outputs:
- token_grad: bfloat16 [32768, 2048], P(('expert', 'dp'))
- new_w_in: float32 [2048, 20480], P('dp', 'expert')
- new_w_out: float32 [2048, 20480], P('dp', 'expert')
The draws below stay inside these ranges and needn't reach their ends.
Inputs may be any that keep to these rules, and one draw needn't show every extreme that they name: `expert_ids`: one expert, the same for all devices, is chosen by half of the 64 rows of every device; the other experts share the remaining rows of a device as evenly as whole numbers allow.
All inputs are finite; a program needn't handle non-finite values.
Results may differ from the reference program's by a relative error of at most 0.025.
Values may be sent and summed in bfloat16 or wider, within the bound.
A program may use at most 64 MiB of HBM per device.

```python
import jax
import jax.numpy as jnp
from jax import lax

D = 2048
FF = 5120
SHARDS = 16
TOK_DEV = 64
EXPERTS = 4
CAP = 10
TOKENS = 32768
N_EXPERT = 64
N_DP = 8


def draw_expert_ids(key, part):
    blocks = TOKENS // TOK_DEV
    spread = max(EXPERTS - 1, 1)
    popular = TOK_DEV // 2
    hot_key, shift_key, order_key = jax.random.split(key, 3)
    hot_expert = jax.random.randint(hot_key, (), 0, EXPERTS)
    shifts = jax.random.randint(shift_key, (blocks, 1), 0, spread)
    positions = jnp.arange(TOK_DEV)[None, :]
    others = (hot_expert + 1 + (positions - popular + shifts) % spread) % EXPERTS
    labels = jnp.where(positions < popular, hot_expert, others)
    block_keys = jax.random.split(order_key, blocks)
    shuffles = jax.vmap(lambda one_key: jax.random.permutation(one_key, TOK_DEV))(block_keys)
    shuffled_ids = jnp.take_along_axis(labels, shuffles, axis=1)
    return shuffled_ids.reshape(TOKENS).astype(jnp.int32)


def block_levels(own_key, dims, shards, low, largest):
    gain = 1.0
    for dim, parts in shards:
        heights = jax.random.uniform(jax.random.fold_in(jax.random.fold_in(own_key, 6), dim), (parts,), jnp.float32, low / len(shards), largest / len(shards))
        gain = gain * jnp.repeat(jnp.exp(heights), dims[dim] // parts).reshape((-1,) + (1,) * (len(dims) - 1 - dim))
    return gain


def gaussian(rng, shape, width, reach, pieces=(), kind=jnp.bfloat16):
    entries = width * jax.random.normal(rng, shape, jnp.float32)
    if pieces:
        entries = entries * block_levels(rng, shape, pieces, -0.22, 0.18)
    return jnp.clip(entries, -reach, reach).astype(kind)


def setup_inputs(seed: int = 0) -> dict:
    key_list = jax.random.split(jax.random.key(seed), 7)
    return {
        "tokens": gaussian(key_list[0], (TOKENS, D), 1.0, 6.0, ((0, 512),)),
        "attn_partials": gaussian(key_list[1], (N_DP, TOKENS, D), 0.35, 5.0, ((0, 8), (1, 64))),
        "expert_ids": draw_expert_ids(jax.random.fold_in(key_list[6], 71), 0),
        "gate": jnp.clip(0.2 + 0.8 * jax.random.uniform(key_list[3], (TOKENS,), jnp.float32) ** block_levels(key_list[3], (TOKENS,), ((0, 512),), -0.2, 0.2), 0.2, 1.0),
        "w_in": gaussian(key_list[4], (D, EXPERTS * FF), 1.0, 6.0, ((0, 8), (1, 64)), jnp.float32),
        "w_out": gaussian(key_list[5], (D, EXPERTS * FF), 1.0, 6.0, ((0, 8), (1, 64)), jnp.float32),
    }


gelu_coef = 0.7978845608028654
cubic_coef = 0.044715
step_rate = 0.5


def gelu_value(inputs):
    return 0.5 * inputs * (1.0 + jnp.tanh(gelu_coef * (inputs + cubic_coef * inputs * inputs * inputs)))


def gelu_slope(inputs):
    tangent = jnp.tanh(gelu_coef * (inputs + cubic_coef * inputs * inputs * inputs))
    return 0.5 * (1.0 + tangent) + 0.5 * inputs * (1.0 - tangent * tangent) * gelu_coef * (1.0 + 3.0 * cubic_coef * inputs * inputs)


def contract_rows(left, right):
    return lax.dot_general(left, right, (((0,), (0,)), ((), ())), preferred_element_type=jnp.float32)


def contract_cols(left, right):
    return lax.dot_general(left, right, (((1,), (1,)), ((), ())), preferred_element_type=jnp.float32)


def reference(tokens, attn_partials, expert_ids, gate, w_in, w_out):
    out_grad = jnp.sum(attn_partials, axis=0, dtype=jnp.float32)
    gated = (gate[:, None] * out_grad).astype(jnp.bfloat16)
    weights_in = w_in.astype(jnp.bfloat16)
    weights_out = w_out.astype(jnp.bfloat16)
    scale_in = D ** -0.5
    scale_out = FF ** -0.5
    window = N_EXPERT * CAP
    hidden_units = FF // SHARDS
    blocks = TOKENS // TOK_DEV
    id_blocks = expert_ids.astype(jnp.int32).reshape(blocks, TOK_DEV)
    expert_range = jnp.arange(EXPERTS, dtype=jnp.int32)
    member = (id_blocks[:, :, None] == expert_range[None, None, :]).astype(jnp.int32)
    ranks = jnp.sum(member * (jnp.cumsum(member, axis=1) - 1), axis=2).reshape(TOKENS)
    kept = ranks < CAP
    token_index = jnp.arange(TOKENS, dtype=jnp.int32)
    groups = (token_index // TOK_DEV) % N_DP
    segment = jnp.where(kept, expert_ids.astype(jnp.int32) * N_DP + groups, EXPERTS * N_DP).astype(jnp.int32)
    ordering = jnp.argsort(segment, stable=True).astype(jnp.int32)
    segment_range = jnp.arange(EXPERTS * N_DP, dtype=jnp.int32)
    counts = jnp.sum((segment[None, :] == segment_range[:, None]).astype(jnp.int32), axis=1)
    starts = (jnp.cumsum(counts) - counts).astype(jnp.int32)
    padded_order = jnp.concatenate([ordering, jnp.full((window,), TOKENS, jnp.int32)])
    padded_tokens = jnp.concatenate([tokens, jnp.zeros((1, D), jnp.bfloat16)])
    padded_gated = jnp.concatenate([gated, jnp.zeros((1, D), jnp.bfloat16)])

    def one_expert(expert):
        cols_in = lax.dynamic_slice_in_dim(weights_in, expert * FF, FF, 1)
        cols_out = lax.dynamic_slice_in_dim(weights_out, expert * FF, FF, 1)

        def one_group(totals, group):
            seg_index = expert * N_DP + group
            picked = lax.dynamic_slice_in_dim(padded_order, starts[seg_index], window, 0)
            live = jnp.arange(window, dtype=jnp.int32) < counts[seg_index]
            picked = jnp.where(live, picked, TOKENS).astype(jnp.int32)
            source_rows = jnp.take(padded_tokens, picked, axis=0)
            grad_rows = jnp.take(padded_gated, picked, axis=0)
            pre_act = jnp.dot(source_rows, cols_in, preferred_element_type=jnp.float32) * scale_in
            hidden = gelu_value(pre_act).astype(jnp.bfloat16)
            hidden_grad = jnp.dot(grad_rows, cols_out, preferred_element_type=jnp.float32) * scale_out
            pre_grad = (hidden_grad * gelu_slope(pre_act)).astype(jnp.bfloat16)
            x_total = jnp.zeros((window, D), jnp.float32)
            for shard in range(SHARDS):
                first = shard * hidden_units
                share = contract_cols(pre_grad[:, first:first + hidden_units], cols_in[:, first:first + hidden_units]) * scale_in
                x_total = x_total + share.astype(jnp.bfloat16).astype(jnp.float32)
            grad_in = (contract_rows(source_rows, pre_grad) * scale_in).astype(jnp.bfloat16)
            grad_out = (contract_rows(grad_rows, hidden) * scale_out).astype(jnp.bfloat16)
            totals = (totals[0] + grad_in.astype(jnp.float32), totals[1] + grad_out.astype(jnp.float32))
            return totals, (x_total.astype(jnp.bfloat16), picked)

        zeros_block = jnp.zeros((D, FF), jnp.float32)
        totals, outputs = lax.scan(one_group, (zeros_block, zeros_block), jnp.arange(N_DP, dtype=jnp.int32))
        return totals[0], totals[1], outputs[0], outputs[1]

    grads_in, grads_out, x_blocks, picks = lax.map(one_expert, jnp.arange(EXPERTS, dtype=jnp.int32))
    token_grad = jnp.zeros((TOKENS + 1, D), jnp.bfloat16)
    token_grad = token_grad.at[picks.reshape(-1)].set(x_blocks.reshape(-1, D))[:TOKENS]
    step_in = jnp.transpose(grads_in, (1, 0, 2)).reshape(D, EXPERTS * FF)
    step_out = jnp.transpose(grads_out, (1, 0, 2)).reshape(D, EXPERTS * FF)
    new_w_in = w_in - step_rate * step_in
    new_w_out = w_out - step_rate * step_out
    return token_grad, new_w_in, new_w_out
```

```python
import functools

import jax
import jax.numpy as jnp
from jax import lax
from jax.experimental import pallas as pl
from jax.experimental.pallas import tpu as pltpu
from jax.sharding import PartitionSpec as P

NX = 4
NY = 4
LINE = 4
BLOCKS = 4
CAP = 10
LANES = 128
MESH = pl.DeviceIdType.MESH

gelu_coef = 0.7978845608028654
cubic_coef = 0.044715
step_rate = 0.5
F32 = jnp.float32
BF16 = jnp.bfloat16


def add16(*terms):
    total = terms[0].astype(F32)
    for term in terms[1:]:
        total = total + term.astype(F32)
    return total.astype(BF16)


class Copies:
    def __init__(self, send_sems, recv_sems):
        self.send_sems = send_sems
        self.recv_sems = recv_sems
        self.count = 0
        self.started = []

    def start(self, src, dst, device):
        index = self.count
        self.count += 1
        copy = pltpu.make_async_remote_copy(
            src_ref=src,
            dst_ref=dst,
            send_sem=self.send_sems.at[index],
            recv_sem=self.recv_sems.at[index],
            device_id=device,
            device_id_type=MESH,
        )
        copy.start()
        self.started.append(copy)
        return copy

    def finish(self):
        for copy in self.started:
            copy.wait_send()


N_COPIES = 160


def kernel(
    dims,
    tok_ref, attn_ref, ids_ref, gate_ref, win_ref, wout_ref,
    tg_ref, nwin_ref, nwout_ref,
    pk_t, pk_g, x3, g3, x2, g2, perm, disp,
    wt, pre_slope, pg, hid, p2, p3,
    r1, m3, r3, r2, q3, rl, sb, slots,
    a_mate, a_sum, a_r1, a_m3, a_r3, a_r2,
    d_w, d_mate, d_sum, d_r1, d_m3, d_r3, d_r2,
    send_sems, recv_sems,
):
    width, hidden = dims
    scale_in = width ** (-0.5)
    scale_out = (hidden * NX * LINE) ** (-0.5)
    tiles = width // LANES
    expert = lax.axis_index("expert")
    dp = lax.axis_index("dp")
    z = expert // NX
    x = expert % NX
    block = z // LINE
    place = z % LINE
    y = dp // 2
    core = dp % 2
    rows_x = LINE * CAP
    rows_c = NX * rows_x

    right = (z * NX + (x + 1) % NX, dp)
    left = (z * NX + (x + NX - 1) % NX, dp)
    up = (expert, ((y + 1) % NY) * 2 + core)
    down = (expert, ((y + NY - 1) % NY) * 2 + core)
    mate = (expert, y * 2 + (1 - core))

    def line(r):
        return ((block * LINE + (place + r) % LINE) * NX + x, dp)

    def twin(j):
        return ((((block + j) % BLOCKS) * LINE + place) * NX + x, dp)

    barrier = pltpu.get_barrier_semaphore()
    partners = [right, left, up, down, mate]
    partners += [line(r) for r in range(1, LINE)] + [twin(j) for j in range(1, BLOCKS)]
    for device in partners:
        pl.semaphore_signal(barrier, inc=1, device_id=device, device_id_type=MESH)

    copies = Copies(send_sems, recv_sems)

    def at_row(c, xs, p):
        return c * rows_c + xs * rows_x + p * CAP

    row_i = lax.broadcasted_iota(jnp.int32, (256, 256), 0)
    col_i = lax.broadcasted_iota(jnp.int32, (256, 256), 1)
    perm[...] = jnp.where(col_i == (row_i % 16) * 16 + row_i // 16, 1.0, 0.0).astype(BF16)

    n_tok = tok_ref.shape[0]
    ids_row = ids_ref[...].astype(F32)
    eye_t = lax.broadcasted_iota(jnp.int32, (n_tok, n_tok), 0)
    eye_s = lax.broadcasted_iota(jnp.int32, (n_tok, n_tok), 1)
    spread_ids = jnp.broadcast_to(ids_row, (n_tok, n_tok))
    ids_col = jnp.sum(jnp.where(eye_t == eye_s, spread_ids, 0.0), axis=1, keepdims=True)
    earlier = jnp.where((ids_col == spread_ids) & (eye_t < eye_s), 1.0, 0.0)
    rank_row = jnp.sum(earlier, axis=0, keepdims=True)
    slot_row = jnp.where(rank_row < CAP, ids_row * CAP + rank_row, -1.0)
    n_slot = disp.shape[0]
    slot_i = lax.broadcasted_iota(jnp.int32, (n_slot, n_tok), 0).astype(F32)
    disp[...] = jnp.where(slot_i == jnp.broadcast_to(slot_row, (n_slot, n_tok)), 1.0, 0.0).astype(BF16)
    gate_col = jnp.sum(
        jnp.where(eye_t == eye_s, jnp.broadcast_to(gate_ref[...], (n_tok, n_tok)), 0.0),
        axis=1, keepdims=True,
    )

    def group_to_tiles(parts):
        return jnp.concatenate(parts, axis=0)

    def pack(rows, dst):
        packed = jnp.dot(disp[...], rows, preferred_element_type=F32).astype(BF16)
        for g in range(n_slot // 16):
            stacked = jnp.concatenate(
                [packed[g * 16:(g + 1) * 16, k * LANES:(k + 1) * LANES] for k in range(tiles)], axis=0
            )
            moved = jnp.dot(perm[...], stacked, preferred_element_type=F32).astype(BF16)
            dst[g * 16:(g + 1) * 16] = moved.reshape(16, tiles, LANES)

    def to_wide(src, dst, base, groups):
        def body(i, carry):
            first = base + i * 32
            pair = [src[pl.ds(first + h * 16, 16)].reshape(256, LANES) for h in range(2)]
            moved = jnp.dot(perm[...], jnp.concatenate(pair, axis=1), preferred_element_type=F32).astype(BF16)
            for h in range(2):
                at = pl.ds(pl.multiple_of(first + h * 16, 16), 16)
                for k in range(tiles):
                    dst[k // 2, at, (k % 2) * LANES:(k % 2 + 1) * LANES] = moved[
                        k * 16:(k + 1) * 16, h * LANES:(h + 1) * LANES
                    ]
            return carry

        lax.fori_loop(0, groups, body, 0)

    def to_narrow(src, dst, base, groups):
        def body(i, carry):
            pair = []
            for h in range(2):
                at = pl.ds(pl.multiple_of(i * 32 + h * 16, 16), 16)
                pair.append(jnp.concatenate(
                    [src[k // 2, at, (k % 2) * LANES:(k % 2 + 1) * LANES] for k in range(tiles)], axis=0
                ))
            moved = jnp.dot(perm[...], jnp.concatenate(pair, axis=1), preferred_element_type=F32).astype(BF16)
            for h in range(2):
                dst[pl.ds(base + i * 32 + h * 16, 16)] = moved[:, h * LANES:(h + 1) * LANES].reshape(16, tiles, LANES)
            return carry

        lax.fori_loop(0, groups, body, 0)

    pack(tok_ref[...], pk_t)
    own = at_row(block, x, place)
    x3[pl.ds(own, CAP)] = pk_t[pl.ds(block * CAP, CAP)]
    for half, source in ((0, win_ref), (1, wout_ref)):
        wt[dp, half * hidden:(half + 1) * hidden] = source[...].T.astype(BF16)
    slots[BLOCKS * CAP:] = jnp.zeros((slots.shape[0] - BLOCKS * CAP, tiles, LANES), BF16)

    pl.semaphore_wait(barrier, len(partners))

    def halves(count):
        return (pl.ds(0, count // 2), pl.ds(count // 2, count // 2))

    def pair_send(source, target):
        sent = {}
        for q in (2, 1, 3, 0):
            at = (y + q) % NY
            sent[q] = copies.start(source(at, 1 - core), target.at[at], mate)
        return sent

    def ring_begin(sent, source, mate_buf, sums, buf1, buf2, upper, lower):
        count = sums.shape[1]
        low, high = halves(count)
        started = {}
        for q in (2, 1, 3, 0):
            at = (y + q) % NY
            sent[q].wait_recv()
            sums[at] = add16(source(at, core)[...], mate_buf[at])
            if q == 2:
                started["u1"] = copies.start(sums.at[at, low], buf1.at[0], upper)
                started["d1"] = copies.start(sums.at[at, high], buf1.at[1], lower)
            elif q == 1:
                started["u2"] = copies.start(sums.at[at, high], buf2.at[0], upper)
            elif q == 3:
                started["d2"] = copies.start(sums.at[at, low], buf2.at[1], lower)
        return started

    def ring_middle(started, sums, buf1, mid, buf3, upper, lower):
        low, high = halves(sums.shape[1])
        started["u1"].wait_recv()
        mid[0] = add16(buf1[0], sums[(y + 1) % NY, low])
        started["u3"] = copies.start(mid.at[0], buf3.at[0], upper)
        started["d1"].wait_recv()
        mid[1] = add16(buf1[1], sums[(y + NY - 1) % NY, high])
        started["d3"] = copies.start(mid.at[1], buf3.at[1], lower)

    def ring_end(started, sums, buf2, buf3):
        low, high = halves(sums.shape[1])
        started["d2"].wait_recv()
        started["u3"].wait_recv()
        first = sums[y, low].astype(F32) + buf2[1].astype(F32) + buf3[0].astype(F32)
        started["u2"].wait_recv()
        started["d3"].wait_recv()
        second = sums[y, high].astype(F32) + buf2[0].astype(F32) + buf3[1].astype(F32)
        return first, second

    def attn_block(at, parity):
        return attn_ref.at[at, parity]

    def z_begin(packed, rows):
        spread = {0: [], }
        for r in range(1, LINE):
            spread[0].append(copies.start(packed.at[pl.ds(block * CAP, CAP)], rows.at[pl.ds(own, CAP)], line(r)))
        far = {}
        for j in (1, 3, 2):
            to = (block + j) % BLOCKS
            far[j] = copies.start(packed.at[pl.ds(to * CAP, CAP)], rows.at[pl.ds(own, CAP)], twin(j))
        return spread, far

    def chunk(j):
        return (block + BLOCKS - j) % BLOCKS

    def z_relay(state, rows, j):
        spread, far = state
        far[j].wait_recv()
        at = pl.ds(at_row(chunk(j), x, place), CAP)
        spread[j] = [copies.start(rows.at[at], rows.at[at], line(r)) for r in range(1, LINE)]

    def x_begin(state, rows, j):
        for copy in state[0][j]:
            copy.wait_recv()
        at = pl.ds(at_row(chunk(j), x, 0), rows_x)
        return [copies.start(rows.at[at], rows.at[at], device) for device in (right, left)]

    def x_forward(sent, rows, j):
        half = rows_x // 2
        sent[0].wait_recv()
        at = pl.ds(at_row(chunk(j), (x + NX - 1) % NX, 0), half)
        to_right = copies.start(rows.at[at], rows.at[at], right)
        sent[1].wait_recv()
        at = pl.ds(at_row(chunk(j), (x + 1) % NX, 0) + half, half)
        to_left = copies.start(rows.at[at], rows.at[at], left)
        return [to_right, to_left]

    def weights_begin():
        at = wt.at[dp]
        return [copies.start(at, at, device) for device in (up, down, mate)]

    def weights_middle(sent):
        low, high = halves(2 * hidden)
        below = ((y + NY - 1) % NY) * 2 + core
        above = ((y + 1) % NY) * 2 + core
        sent[0].wait_recv()
        to_up = copies.start(wt.at[below, low], wt.at[below, low], up)
        to_mate = [copies.start(wt.at[below], wt.at[below], mate)]
        sent[1].wait_recv()
        to_down = copies.start(wt.at[above, high], wt.at[above, high], down)
        to_mate.append(copies.start(wt.at[above], wt.at[above], mate))
        return [to_up, to_down], to_mate

    def weights_end(ends, to_mate):
        low, high = halves(2 * hidden)
        far = ((y + 2) % NY) * 2 + core
        for copy, part in zip(ends, (low, high)):
            copy.wait_recv()
            to_mate.append(copies.start(wt.at[far, part], wt.at[far, part], mate))

    def wide_dot(wide, rows, first):
        total = None
        for k in range(width // 256):
            term = lax.dot_general(
                wide[k, rows], wt[k, first:first + hidden],
                (((1,), (1,)), ((), ())), preferred_element_type=F32,
            )
            total = term if total is None else total + term
        return total

    def forward_chunk(j):
        base = chunk(j) * rows_c
        to_wide(x3, x2, base, rows_c // 32)
        rows = pl.ds(pl.multiple_of(base, 32), rows_c)
        pre = wide_dot(x2, rows, 0) * scale_in
        square = pre * pre
        tangent = jnp.tanh(gelu_coef * (pre + cubic_coef * square * pre))
        hid[rows] = (0.5 * pre * (1.0 + tangent)).astype(BF16)
        pre_slope[rows] = 0.5 * (1.0 + tangent) + 0.5 * pre * (1.0 - tangent * tangent) * gelu_coef * (
            1.0 + 3.0 * cubic_coef * square
        )

    def backward_chunk(j):
        base = chunk(j) * rows_c
        to_wide(g3, g2, base, rows_c // 32)
        rows = pl.ds(pl.multiple_of(base, 32), rows_c)
        grad = (wide_dot(g2, rows, hidden) * scale_out * pre_slope[rows]).astype(BF16)
        pg[rows] = grad
        for k in range(width // 256):
            p2[k] = (jnp.dot(grad, wt[k, 0:hidden], preferred_element_type=F32) * scale_in).astype(BF16)
        to_narrow(p2, p3, base, rows_c // 32)

    half = rows_x // 2

    def p_rows(j, xs, second, count):
        return pl.ds(at_row(chunk(j), xs % NX, 0) + second * half, count)

    def back_begin(j):
        out = {}
        out["r1"] = copies.start(p3.at[p_rows(j, x + 2, 0, half)], r1.at[j, 0], right)
        out["l1"] = copies.start(p3.at[p_rows(j, x + 2, 1, half)], r1.at[j, 1], left)
        out["r2"] = copies.start(p3.at[p_rows(j, x + 1, 1, half)], r2.at[j, 0], right)
        out["l2"] = copies.start(p3.at[p_rows(j, x + NX - 1, 0, half)], r2.at[j, 1], left)
        return out

    def back_middle(out, j):
        out["r1"].wait_recv()
        m3[j, 0] = add16(r1[j, 0], p3[p_rows(j, x + 1, 0, half)])
        out["r3"] = copies.start(m3.at[j, 0], r3.at[j, 0], right)
        out["l1"].wait_recv()
        m3[j, 1] = add16(r1[j, 1], p3[p_rows(j, x + NX - 1, 1, half)])
        out["l3"] = copies.start(m3.at[j, 1], r3.at[j, 1], left)

    def back_line(out, j):
        out["l2"].wait_recv()
        out["r3"].wait_recv()
        q3[j, 0:half] = add16(p3[p_rows(j, x, 0, half)], r3[j, 0], r2[j, 1])
        out["r2"].wait_recv()
        out["l3"].wait_recv()
        q3[j, half:rows_x] = add16(p3[p_rows(j, x, 1, half)], r2[j, 0], r3[j, 1])
        out["z"] = []
        for r in range(1, LINE):
            at = ((place + r) % LINE) * CAP
            out["z"].append(copies.start(q3.at[j, pl.ds(at, CAP)], rl.at[j, r - 1], line(r)))

    def back_far(out, j):
        for copy in out["z"]:
            copy.wait_recv()
        total = add16(q3[j, pl.ds(place * CAP, CAP)], rl[j, 0], rl[j, 1], rl[j, 2])
        at = pl.ds(block * CAP, CAP)
        if j == 0:
            slots[at] = total
        else:
            sb[j - 1] = total
            out["far"] = copies.start(sb.at[j - 1], slots.at[at], twin(BLOCKS - j))

    order = (0, 1, 3, 2)
    attn_sent = pair_send(attn_block, a_mate)
    t_state = z_begin(pk_t, x3)
    attn_ring = ring_begin(attn_sent, attn_block, a_mate, a_sum, a_r1, a_r2, up, down)
    w_first = weights_begin()
    t_x, t_f, g_x, g_f = {}, {}, {}, {}
    t_x[0] = x_begin(t_state, x3, 0)
    z_relay(t_state, x3, 1)
    ring_middle(attn_ring, a_sum, a_r1, a_m3, a_r3, up, down)
    z_relay(t_state, x3, 3)
    t_f[0] = x_forward(t_x[0], x3, 0)
    t_x[1] = x_begin(t_state, x3, 1)
    first, second = ring_end(attn_ring, a_sum, a_r2, a_r3)
    summed = jnp.concatenate([first, second], axis=0)
    pack((gate_col * summed).astype(BF16), pk_g)
    g3[pl.ds(own, CAP)] = pk_g[pl.ds(block * CAP, CAP)]
    g_state = z_begin(pk_g, g3)
    z_relay(t_state, x3, 2)
    t_x[3] = x_begin(t_state, x3, 3)
    t_f[1] = x_forward(t_x[1], x3, 1)
    w_ends, w_mate = weights_middle(w_first)
    t_x[2] = x_begin(t_state, x3, 2)
    t_f[3] = x_forward(t_x[3], x3, 3)
    g_x[0] = x_begin(g_state, g3, 0)
    z_relay(g_state, g3, 1)
    t_f[2] = x_forward(t_x[2], x3, 2)
    weights_end(w_ends, w_mate)
    z_relay(g_state, g3, 3)
    for copy in [w_first[2]] + w_mate:
        copy.wait_recv()
    g_x[1] = x_begin(g_state, g3, 1)
    z_relay(g_state, g3, 2)

    def arrive(copies_in):
        for copy in copies_in:
            copy.wait_recv()

    arrive(t_f[0])
    forward_chunk(0)
    g_f[0] = x_forward(g_x[0], g3, 0)
    g_x[3] = x_begin(g_state, g3, 3)
    arrive(t_f[1])
    forward_chunk(1)
    g_f[1] = x_forward(g_x[1], g3, 1)
    g_x[2] = x_begin(g_state, g3, 2)
    arrive(t_f[3])
    forward_chunk(3)
    g_f[3] = x_forward(g_x[3], g3, 3)
    arrive(t_f[2])
    forward_chunk(2)
    g_f[2] = x_forward(g_x[2], g3, 2)

    back = {}
    previous = None
    for j in order:
        arrive(g_f[j])
        backward_chunk(j)
        back[j] = back_begin(j)
        if previous is not None:
            back_middle(back[previous], previous)
        previous = j
    back_line(back[0], 0)
    back_middle(back[2], 2)
    back_line(back[1], 1)
    back_far(back[0], 0)

    grad_t = pg[...].T
    hid_t = hid[...].T

    def weight_grads(parity):
        def body(i, carry):
            k = i * 2 + parity
            d_w[i, parity, 0:hidden] = (
                jnp.dot(grad_t, x2[k], preferred_element_type=F32) * scale_in
            ).astype(BF16)
            d_w[i, parity, hidden:2 * hidden] = (
                jnp.dot(hid_t, g2[k], preferred_element_type=F32) * scale_out
            ).astype(BF16)
            return carry

        lax.fori_loop(0, NY, body, 0)

    def grad_block(at, parity):
        return d_w.at[at, parity]

    weight_grads(1 - core)
    d_sent = pair_send(grad_block, d_mate)
    back_line(back[3], 3)
    back_far(back[1], 1)
    weight_grads(core)
    d_ring = ring_begin(d_sent, grad_block, d_mate, d_sum, d_r1, d_r2, up, down)
    back_line(back[2], 2)
    back_far(back[3], 3)
    ring_middle(d_ring, d_sum, d_r1, d_m3, d_r3, up, down)
    back_far(back[2], 2)
    grad_in, grad_out = ring_end(d_ring, d_sum, d_r2, d_r3)
    nwin_ref[...] = win_ref[...] - step_rate * grad_in.T
    nwout_ref[...] = wout_ref[...] - step_rate * grad_out.T
    for j in (1, 3, 2):
        back[j]["far"].wait_recv()
    wide = []
    for g in range(n_slot // 16):
        moved = jnp.dot(
            perm[...], slots[g * 16:(g + 1) * 16].reshape(256, LANES), preferred_element_type=F32
        ).astype(BF16)
        wide.append(jnp.concatenate([moved[k * 16:(k + 1) * 16] for k in range(tiles)], axis=1))
    slots_wide = jnp.concatenate(wide, axis=0)
    tg_ref[...] = lax.dot_general(
        disp[...], slots_wide, (((0,), (0,)), ((), ())), preferred_element_type=F32
    ).astype(BF16)
    copies.finish()


def shards(tokens, attn_partials, expert_ids, gate, w_in, w_out):
    n_tok, width = tokens.shape
    hidden = w_in.shape[1]
    tiles = width // LANES
    rows = NX * LINE * BLOCKS * CAP
    rows_x = LINE * CAP
    half = rows_x // 2
    slot_rows = 48
    vmem = pl.BlockSpec(memory_space=pltpu.VMEM)

    def rows16(*lead):
        return pltpu.VMEM(lead + (tiles, LANES), BF16)

    def wide(*lead):
        return pltpu.VMEM(lead + (256,), BF16)

    parts = width // 256
    scratch = [
        rows16(slot_rows), rows16(slot_rows), rows16(rows), rows16(rows),
        wide(parts, rows), wide(parts, rows),
        pltpu.VMEM((256, 256), BF16), pltpu.VMEM((slot_rows, n_tok), BF16),
        wide(parts, 2 * hidden),
        pltpu.VMEM((rows, hidden), F32), pltpu.VMEM((rows, hidden), BF16), pltpu.VMEM((rows, hidden), BF16),
        wide(parts, rows // BLOCKS), rows16(rows),
        rows16(BLOCKS, 2, half), rows16(BLOCKS, 2, half), rows16(BLOCKS, 2, half), rows16(BLOCKS, 2, half),
        rows16(BLOCKS, rows_x), rows16(BLOCKS, LINE - 1, CAP), rows16(BLOCKS - 1, CAP), rows16(slot_rows),
        pltpu.VMEM((NY, n_tok, width), BF16), pltpu.VMEM((NY, n_tok, width), BF16),
    ]
    scratch += [pltpu.VMEM((2, n_tok // 2, width), BF16)] * 4
    scratch += [wide(NY, 2, 2 * hidden), wide(NY, 2 * hidden), wide(NY, 2 * hidden)]
    scratch += [wide(2, hidden)] * 4
    scratch += [pltpu.SemaphoreType.DMA((N_COPIES,)), pltpu.SemaphoreType.DMA((N_COPIES,))]
    return pl.pallas_call(
        functools.partial(kernel, (width, hidden)),
        out_shape=(
            jax.ShapeDtypeStruct((n_tok, width), BF16),
            jax.ShapeDtypeStruct(w_in.shape, F32),
            jax.ShapeDtypeStruct(w_out.shape, F32),
        ),
        in_specs=[vmem] * 6,
        out_specs=(vmem, vmem, vmem),
        scratch_shapes=scratch,
        compiler_params=pltpu.CompilerParams(
            collective_id=0, has_side_effects=True, vmem_limit_bytes=60 * 1024 * 1024
        ),
    )(
        tokens,
        attn_partials.reshape(NY, 2, n_tok, width),
        expert_ids.reshape(1, n_tok),
        gate.reshape(1, n_tok),
        w_in,
        w_out,
    )


def solution(mesh):
    in_specs = (
        P(("expert", "dp"), None),
        P("dp", "expert", None),
        P(("expert", "dp")),
        P(("expert", "dp")),
        P("dp", "expert"),
        P("dp", "expert"),
    )
    out_specs = (P(("expert", "dp"), None), P("dp", "expert"), P("dp", "expert"))
    return jax.shard_map(shards, mesh=mesh, in_specs=in_specs, out_specs=out_specs, check_vma=False)
```

```python
import functools

import jax
import jax.numpy as jnp
from jax import lax
from jax.experimental import pallas as pl
from jax.experimental.pallas import tpu as pltpu
from jax.sharding import PartitionSpec as P

NX = 4
NY = 4
LINE = 4
BLOCKS = 4
CAP = 10
LANES = 128
MESH = pl.DeviceIdType.MESH

gelu_coef = 0.7978845608028654
cubic_coef = 0.044715
step_rate = 0.5
F32 = jnp.float32
BF16 = jnp.bfloat16


def add16(*terms):
    total = terms[0].astype(F32)
    for term in terms[1:]:
        total = total + term.astype(F32)
    return total.astype(BF16)


class Copies:
    def __init__(self, send_sems, recv_sems):
        self.send_sems = send_sems
        self.recv_sems = recv_sems
        self.count = 0
        self.started = []

    def start(self, src, dst, device):
        index = self.count
        self.count += 1
        copy = pltpu.make_async_remote_copy(
            src_ref=src,
            dst_ref=dst,
            send_sem=self.send_sems.at[index],
            recv_sem=self.recv_sems.at[index],
            device_id=device,
            device_id_type=MESH,
        )
        copy.start()
        self.started.append(copy)
        return copy

    def finish(self):
        for copy in self.started:
            copy.wait_send()


N_COPIES = 192


def kernel(
    dims,
    tok_ref, attn_ref, ids_ref, gate_ref, win_ref, wout_ref,
    tg_ref, nwin_ref, nwout_ref,
    pk_t, pk_g, x3, g3, x2, g2, perm, disp,
    w_stage, w_in, w_out, pre_slope, pg, hid, p2, p3, p_mate,
    q3, rl, sb, slots,
    a_mate, a_sum, a_r1, a_m3, a_r3, a_r2,
    d_in, i_r1, i_m3, i_r3, i_r2, i_sum, is_r1, is_m3, is_r3, is_r2,
    d_out, o_r1, o_m3, o_r3, o_r2, o_sum, os_r1, os_m3, os_r3, os_r2,
    d_part, d_other,
    send_sems, recv_sems,
):
    width, hidden = dims
    scale_in = width ** (-0.5)
    scale_out = (hidden * NX * LINE) ** (-0.5)
    tiles = width // LANES
    share = hidden // 2
    units = NX * share
    depth = width // NY
    expert = lax.axis_index("expert")
    dp = lax.axis_index("dp")
    z = expert // NX
    x = expert % NX
    block = z // LINE
    place = z % LINE
    y = dp // 2
    core = dp % 2
    rows_b = LINE * CAP
    rows_d = BLOCKS * rows_b

    right = (z * NX + (x + 1) % NX, dp)
    left = (z * NX + (x + NX - 1) % NX, dp)
    up = (expert, ((y + 1) % NY) * 2 + core)
    down = (expert, ((y + NY - 1) % NY) * 2 + core)
    mate = (expert, y * 2 + (1 - core))

    def line(r):
        return ((block * LINE + (place + r) % LINE) * NX + x, dp)

    def twin(j):
        return ((((block + j) % BLOCKS) * LINE + place) * NX + x, dp)

    barrier = pltpu.get_barrier_semaphore()
    partners = [right, left, up, down, mate]
    partners += [line(r) for r in range(1, LINE)] + [twin(j) for j in range(1, BLOCKS)]
    for device in partners:
        pl.semaphore_signal(barrier, inc=1, device_id=device, device_id_type=MESH)

    copies = Copies(send_sems, recv_sems)

    def arrive(*waiting):
        for copy in waiting:
            copy.wait_recv()

    row_i = lax.broadcasted_iota(jnp.int32, (256, 256), 0)
    col_i = lax.broadcasted_iota(jnp.int32, (256, 256), 1)
    perm[...] = jnp.where(col_i == (row_i % 16) * 16 + row_i // 16, 1.0, 0.0).astype(BF16)

    n_tok = tok_ref.shape[0]
    ids_row = ids_ref[...].astype(F32)
    eye_t = lax.broadcasted_iota(jnp.int32, (n_tok, n_tok), 0)
    eye_s = lax.broadcasted_iota(jnp.int32, (n_tok, n_tok), 1)
    spread_ids = jnp.broadcast_to(ids_row, (n_tok, n_tok))
    ids_col = jnp.sum(jnp.where(eye_t == eye_s, spread_ids, 0.0), axis=1, keepdims=True)
    earlier = jnp.where((ids_col == spread_ids) & (eye_t < eye_s), 1.0, 0.0)
    rank_row = jnp.sum(earlier, axis=0, keepdims=True)
    slot_row = jnp.where(rank_row < CAP, ids_row * CAP + rank_row, -1.0)
    n_slot = disp.shape[0]
    slot_i = lax.broadcasted_iota(jnp.int32, (n_slot, n_tok), 0).astype(F32)
    disp[...] = jnp.where(slot_i == jnp.broadcast_to(slot_row, (n_slot, n_tok)), 1.0, 0.0).astype(BF16)
    gate_col = jnp.sum(
        jnp.where(eye_t == eye_s, jnp.broadcast_to(gate_ref[...], (n_tok, n_tok)), 0.0),
        axis=1, keepdims=True,
    )

    def pack(rows, dst):
        packed = jnp.dot(disp[...], rows, preferred_element_type=F32).astype(BF16)
        for g in range(n_slot // 16):
            stacked = jnp.concatenate(
                [packed[g * 16:(g + 1) * 16, k * LANES:(k + 1) * LANES] for k in range(tiles)], axis=0
            )
            moved = jnp.dot(perm[...], stacked, preferred_element_type=F32).astype(BF16)
            dst[g * 16:(g + 1) * 16] = moved.reshape(16, tiles, LANES)

    per = depth // LANES

    def to_wide(src, dst, half):
        def body(i, carry):
            pair = [src[half, pl.ds(i * 32 + h * 16, 16)].reshape(256, LANES) for h in range(2)]
            moved = jnp.dot(perm[...], jnp.concatenate(pair, axis=1), preferred_element_type=F32).astype(BF16)
            for h in range(2):
                at = pl.ds(pl.multiple_of(half * rows_d + i * 32 + h * 16, 16), 16)
                for k in range(tiles):
                    dst[k // per, at, (k % per) * LANES:(k % per + 1) * LANES] = moved[
                        k * 16:(k + 1) * 16, h * LANES:(h + 1) * LANES
                    ]
            return carry

        lax.fori_loop(0, rows_d // 32, body, 0)

    def to_narrow(src, dst, half):
        def body(i, carry):
            pair = []
            for h in range(2):
                at = pl.ds(pl.multiple_of(i * 32 + h * 16, 16), 16)
                pair.append(jnp.concatenate(
                    [src[k // per, at, (k % per) * LANES:(k % per + 1) * LANES] for k in range(tiles)], axis=0
                ))
            moved = jnp.dot(perm[...], jnp.concatenate(pair, axis=1), preferred_element_type=F32).astype(BF16)
            for h in range(2):
                dst[half, pl.ds(i * 32 + h * 16, 16)] = moved[:, h * LANES:(h + 1) * LANES].reshape(16, tiles, LANES)
            return carry

        lax.fori_loop(0, rows_d // 32, body, 0)

    pack(tok_ref[...], pk_t)

    def row_at(c, p):
        return c * rows_b + p * CAP

    own = row_at(block, place)
    x3[core, pl.ds(own, CAP)] = pk_t[pl.ds(block * CAP, CAP)]
    mine = pl.ds(pl.multiple_of(core * share, share), share)
    other = pl.ds(pl.multiple_of((1 - core) * share, share), share)
    lanes_mine = pl.ds(pl.multiple_of(core * (depth // 2), depth // 2), depth // 2)
    lanes_other = pl.ds(pl.multiple_of((1 - core) * (depth // 2), depth // 2), depth // 2)
    w_in[y, x, :, lanes_mine] = win_ref[mine].astype(BF16)
    w_out[x, y, :, lanes_mine] = wout_ref[mine].astype(BF16)
    w_stage[0] = win_ref[other].astype(BF16)
    w_stage[1] = wout_ref[other].astype(BF16)
    slots[BLOCKS * CAP:] = jnp.zeros((slots.shape[0] - BLOCKS * CAP, tiles, LANES), BF16)

    pl.semaphore_wait(barrier, len(partners))

    def halves(count):
        return pl.ds(0, count // 2), pl.ds(count // 2, count // 2)

    X_RING = (x, right, left)
    Y_RING = (y, up, down)

    def gather_first(blk, ring):
        pos, upper, lower = ring
        return [copies.start(blk(pos), blk(pos), device) for device in (upper, lower)]

    def gather_next(sent, blk, ring):
        pos, upper, lower = ring
        low, high = halves(share)
        below, above = (pos + 3) % 4, (pos + 1) % 4
        sent[0].wait_recv()
        to_up = copies.start(blk(below).at[low], blk(below).at[low], upper)
        sent[1].wait_recv()
        to_down = copies.start(blk(above).at[high], blk(above).at[high], lower)
        return [to_up, to_down]

    def scatter_first(blk, count, buf1, buf2, ring):
        pos, upper, lower = ring
        low, high = halves(count)
        far, above, below = (pos + 2) % 4, (pos + 1) % 4, (pos + 3) % 4
        return {
            "u1": copies.start(blk(far).at[low], buf1.at[0], upper),
            "d1": copies.start(blk(far).at[high], buf1.at[1], lower),
            "u2": copies.start(blk(above).at[high], buf2.at[0], upper),
            "d2": copies.start(blk(below).at[low], buf2.at[1], lower),
        }

    def scatter_middle(sent, blk, count, buf1, mid, buf3, ring):
        pos, upper, lower = ring
        low, high = halves(count)
        sent["u1"].wait_recv()
        mid[0] = add16(buf1[0], blk((pos + 1) % 4).at[low][...])
        sent["u3"] = copies.start(mid.at[0], buf3.at[0], upper)
        sent["d1"].wait_recv()
        mid[1] = add16(buf1[1], blk((pos + 3) % 4).at[high][...])
        sent["d3"] = copies.start(mid.at[1], buf3.at[1], lower)

    def scatter_end(sent, blk, count, buf2, buf3, ring):
        low, high = halves(count)
        pos = ring[0]
        arrive(sent["d2"], sent["u3"])
        first = blk(pos).at[low][...].astype(F32) + buf2[1].astype(F32) + buf3[0].astype(F32)
        arrive(sent["u2"], sent["d3"])
        second = blk(pos).at[high][...].astype(F32) + buf2[0].astype(F32) + buf3[1].astype(F32)
        return first, second

    def attn_begin(sent):
        low, high = halves(n_tok)
        out = {}
        for q in (2, 1, 3, 0):
            at = (y + q) % NY
            sent[q].wait_recv()
            a_sum[at] = add16(attn_ref[at, core], a_mate[at])
            if q == 2:
                out["u1"] = copies.start(a_sum.at[at, low], a_r1.at[0], up)
                out["d1"] = copies.start(a_sum.at[at, high], a_r1.at[1], down)
            elif q == 1:
                out["u2"] = copies.start(a_sum.at[at, high], a_r2.at[0], up)
            elif q == 3:
                out["d2"] = copies.start(a_sum.at[at, low], a_r2.at[1], down)
        return out

    def z_begin(packed, rows):
        at = pl.ds(block * CAP, CAP)
        spread = {0: [copies.start(packed.at[at], rows.at[core, pl.ds(own, CAP)], line(r)) for r in range(1, LINE)]}
        far = {}
        for j in (1, 3, 2):
            to = (block + j) % BLOCKS
            far[j] = copies.start(packed.at[pl.ds(to * CAP, CAP)], rows.at[core, pl.ds(own, CAP)], twin(j))
        return spread, far

    def chunk(j):
        return (block + BLOCKS - j) % BLOCKS

    def z_relay(state, rows, j):
        spread, far = state
        far[j].wait_recv()
        at = pl.ds(row_at(chunk(j), place), CAP)
        spread[j] = [copies.start(rows.at[core, at], rows.at[core, at], line(r)) for r in range(1, LINE)]

    def z_share(state, rows, j):
        arrive(*state[0][j])
        at = pl.ds(row_at(chunk(j), 0), rows_b)
        return copies.start(rows.at[core, at], rows.at[core, at], mate)

    def back_share(j):
        at = pl.ds(row_at(chunk(j), 0), rows_b)
        return {"m": copies.start(p3.at[1 - core, at], p_mate.at[at], mate)}

    def back_line(out, j):
        at = pl.ds(row_at(chunk(j), 0), rows_b)
        out["m"].wait_recv()
        q3[j] = add16(p3[core, at], p_mate[at])
        out["z"] = []
        for r in range(1, LINE):
            to = ((place + r) % LINE) * CAP
            out["z"].append(copies.start(q3.at[j, pl.ds(to, CAP)], rl.at[j, r - 1], line(r)))

    def back_far(out, j):
        arrive(*out["z"])
        total = add16(q3[j, pl.ds(place * CAP, CAP)], rl[j, 0], rl[j, 1], rl[j, 2])
        at = pl.ds(block * CAP, CAP)
        if j == 0:
            slots[at] = total
        else:
            sb[j - 1] = total
            out["far"] = copies.start(sb.at[j - 1], slots.at[at], twin(BLOCKS - j))

    def in_x(i):
        return w_in.at[y, i]

    def out_y(i):
        return w_out.at[x, i]

    def in_y(s):
        return lambda i: w_in.at[i, s]

    def out_x(s):
        return lambda i: w_out.at[i, s]

    w_pair = [
        copies.start(w_stage.at[0], w_in.at[y, x, :, lanes_mine], mate),
        copies.start(w_stage.at[1], w_out.at[x, y, :, lanes_mine], mate),
    ]
    attn_sent = {}
    for q in (2, 1, 3, 0):
        at = (y + q) % NY
        attn_sent[q] = copies.start(attn_ref.at[at, 1 - core], a_mate.at[at], mate)
    t_state = z_begin(pk_t, x3)
    arrive(w_pair[0])
    in_first = gather_first(in_x, X_RING)
    attn_ring = attn_begin(attn_sent)
    arrive(w_pair[1])
    out_first = gather_first(out_y, Y_RING)
    in_big, out_big = {}, {}
    in_big[0] = gather_first(in_y(x), Y_RING)
    out_big[0] = gather_first(out_x(y), X_RING)
    z_relay(t_state, x3, 1)
    in_next = gather_next(in_first, in_x, X_RING)
    for q in (1, 3):
        in_big[q] = gather_first(in_y((x + q) % NX), Y_RING)
    z_relay(t_state, x3, 3)
    a_low, a_high = halves(n_tok)
    scatter_middle(attn_ring, lambda i: a_sum.at[i], n_tok, a_r1, a_m3, a_r3, Y_RING)
    out_next = gather_next(out_first, out_y, Y_RING)
    for q in (1, 3):
        out_big[q] = gather_first(out_x((y + q) % NY), X_RING)
    z_relay(t_state, x3, 2)
    arrive(*in_next)
    in_big[2] = gather_first(in_y((x + 2) % NX), Y_RING)
    t_share = {0: z_share(t_state, x3, 0), 1: z_share(t_state, x3, 1)}
    first, second = scatter_end(attn_ring, lambda i: a_sum.at[i], n_tok, a_r2, a_r3, Y_RING)
    summed = jnp.concatenate([first, second], axis=0)
    pack((gate_col * summed).astype(BF16), pk_g)
    g3[core, pl.ds(own, CAP)] = pk_g[pl.ds(block * CAP, CAP)]
    g_state = z_begin(pk_g, g3)
    in_last, out_last = {}, {}
    in_last[0] = gather_next(in_big[0], in_y(x), Y_RING)
    arrive(*out_next)
    out_big[2] = gather_first(out_x((y + 2) % NY), X_RING)
    out_last[0] = gather_next(out_big[0], out_x(y), X_RING)
    t_share[3] = z_share(t_state, x3, 3)
    t_share[2] = z_share(t_state, x3, 2)
    for q in (1, 3):
        in_last[q] = gather_next(in_big[q], in_y((x + q) % NX), Y_RING)
        out_last[q] = gather_next(out_big[q], out_x((y + q) % NY), X_RING)
        z_relay(g_state, g3, q)
    in_last[2] = gather_next(in_big[2], in_y((x + 2) % NX), Y_RING)
    out_last[2] = gather_next(out_big[2], out_x((y + 2) % NY), X_RING)
    z_relay(g_state, g3, 2)
    g_share = {}
    g_share[0] = z_share(g_state, g3, 0)

    to_wide(x3, x2, core)
    arrive(*t_share.values())
    to_wide(x3, x2, 1 - core)
    for q in range(4):
        arrive(*in_last[q])
    pre = None
    for k in range(NY):
        term = lax.dot_general(
            x2[k], w_in[k].reshape(units, depth), (((1,), (1,)), ((), ())), preferred_element_type=F32
        )
        pre = term if pre is None else pre + term
    pre = pre * scale_in
    square = pre * pre
    tangent = jnp.tanh(gelu_coef * (pre + cubic_coef * square * pre))
    hid[...] = (0.5 * pre * (1.0 + tangent)).astype(BF16)
    pre_slope[...] = scale_out * (
        0.5 * (1.0 + tangent) + 0.5 * pre * (1.0 - tangent * tangent) * gelu_coef * (1.0 + 3.0 * cubic_coef * square)
    )
    for q in (1, 3, 2):
        g_share[q] = z_share(g_state, g3, q)
    hid_t = hid[...].T
    to_wide(g3, g2, core)
    arrive(*g_share.values())
    to_wide(g3, g2, 1 - core)

    for k in range(NY):
        grads = (jnp.dot(hid_t, g2[k], preferred_element_type=F32) * scale_out).astype(BF16)
        for i in range(NX):
            d_out[i, k] = grads[i * share:(i + 1) * share]
    out_ring = scatter_first(lambda i: d_out.at[i], NY, o_r1, o_r2, X_RING)

    for q in range(4):
        arrive(*out_last[q])
    total = None
    for k in range(NY):
        columns = jnp.concatenate([w_out[i, k] for i in range(NX)], axis=0)
        term = lax.dot_general(g2[k], columns, (((1,), (1,)), ((), ())), preferred_element_type=F32)
        total = term if total is None else total + term
    pg[...] = (total * pre_slope[...]).astype(BF16)

    back = {}
    order = (0, 1, 3, 2)
    for part in range(2):
        half = (1 - core) if part == 0 else core
        rows = pg[pl.ds(pl.multiple_of(half * rows_d, rows_d), rows_d)]
        for k in range(NY):
            p2[k] = (
                jnp.dot(rows, w_in[k].reshape(units, depth), preferred_element_type=F32) * scale_in
            ).astype(BF16)
        to_narrow(p2, p3, half)
        if part == 0:
            for j in order:
                back[j] = back_share(j)
    scatter_middle(out_ring, lambda i: d_out.at[i], NY, o_r1, o_m3, o_r3, X_RING)
    for j in order:
        back_line(back[j], j)
    pg_t = pg[...].T
    for k in range(NY):
        grads = (jnp.dot(pg_t, x2[k], preferred_element_type=F32) * scale_in).astype(BF16)
        d_in[k] = grads.reshape(NX, share, depth)
    in_ring = scatter_first(lambda i: d_in.at[i], NX, i_r1, i_r2, Y_RING)
    for j in order:
        back_far(back[j], j)
    scatter_middle(in_ring, lambda i: d_in.at[i], NX, i_r1, i_m3, i_r3, Y_RING)

    first, second = scatter_end(out_ring, lambda i: d_out.at[i], NY, o_r2, o_r3, X_RING)
    o_sum[0:2] = first.astype(BF16)
    o_sum[2:4] = second.astype(BF16)
    out_small = scatter_first(lambda i: o_sum.at[i], share, os_r1, os_r2, Y_RING)
    first, second = scatter_end(in_ring, lambda i: d_in.at[i], NX, i_r2, i_r3, Y_RING)
    i_sum[0:2] = first.astype(BF16)
    i_sum[2:4] = second.astype(BF16)
    in_small = scatter_first(lambda i: i_sum.at[i], share, is_r1, is_r2, X_RING)
    scatter_middle(out_small, lambda i: o_sum.at[i], share, os_r1, os_m3, os_r3, Y_RING)
    scatter_middle(in_small, lambda i: i_sum.at[i], share, is_r1, is_m3, is_r3, X_RING)
    pair = []
    for t, sent, sums, buf2, buf3, ring in (
        (1, out_small, o_sum, os_r2, os_r3, Y_RING), (0, in_small, i_sum, is_r2, is_r3, X_RING),
    ):
        low, high = halves(share)
        first, second = scatter_end(sent, lambda i: sums.at[i], share, buf2, buf3, ring)
        d_part[t, low] = first.astype(BF16)
        d_part[t, high] = second.astype(BF16)
        pair.append(copies.start(d_part.at[t, :, lanes_other], d_other.at[t], mate))

    arrive(back[1]["far"], back[3]["far"], back[2]["far"])
    wide = []
    for g in range(n_slot // 16):
        moved = jnp.dot(
            perm[...], slots[g * 16:(g + 1) * 16].reshape(256, LANES), preferred_element_type=F32
        ).astype(BF16)
        wide.append(jnp.concatenate([moved[k * 16:(k + 1) * 16] for k in range(tiles)], axis=1))
    slots_wide = jnp.concatenate(wide, axis=0)
    tg_ref[...] = lax.dot_general(
        disp[...], slots_wide, (((0,), (0,)), ((), ())), preferred_element_type=F32
    ).astype(BF16)

    for t, copy, old, new in ((1, pair[0], wout_ref, nwout_ref), (0, pair[1], win_ref, nwin_ref)):
        new[mine] = old[mine] - step_rate * d_part[t, :, lanes_mine].astype(F32)
        copy.wait_recv()
        new[other] = old[other] - step_rate * d_other[t].astype(F32)
    copies.finish()


def shards(tokens, attn_partials, expert_ids, gate, w_in, w_out):
    n_tok, width = tokens.shape
    w_in_t, w_out_t = w_in.T, w_out.T
    hidden = w_in_t.shape[0]
    tiles = width // LANES
    rows_b = LINE * CAP
    rows_d = BLOCKS * rows_b
    share = hidden // 2
    units = NX * share
    depth = width // NY
    slot_rows = 48
    vmem = pl.BlockSpec(memory_space=pltpu.VMEM)

    def bf16(*shape):
        return pltpu.VMEM(shape, BF16)

    def rows16(*lead):
        return bf16(*lead, tiles, LANES)

    scratch = [
        rows16(slot_rows), rows16(slot_rows), rows16(2, rows_d), rows16(2, rows_d),
        bf16(NY, 2 * rows_d, depth), bf16(NY, 2 * rows_d, depth),
        bf16(256, 256), bf16(slot_rows, n_tok),
        bf16(2, share, depth // 2), bf16(NY, NX, share, depth), bf16(NX, NY, share, depth),
        pltpu.VMEM((2 * rows_d, units), F32), bf16(2 * rows_d, units), bf16(2 * rows_d, units),
        bf16(NY, rows_d, depth), rows16(2, rows_d), rows16(rows_d),
        rows16(BLOCKS, rows_b), rows16(BLOCKS, LINE - 1, CAP), rows16(BLOCKS - 1, CAP), rows16(slot_rows),
        bf16(NY, n_tok, width), bf16(NY, n_tok, width),
    ]
    scratch += [bf16(2, n_tok // 2, width)] * 4
    for _ in range(2):
        scratch += [bf16(4, 4, share, depth)] + [bf16(2, 2, share, depth)] * 4
        scratch += [bf16(4, share, depth)] + [bf16(2, share // 2, depth)] * 4
    scratch += [bf16(2, share, depth), bf16(2, share, depth // 2)]
    scratch += [pltpu.SemaphoreType.DMA((N_COPIES,)), pltpu.SemaphoreType.DMA((N_COPIES,))]
    token_grad, new_in, new_out = pl.pallas_call(
        functools.partial(kernel, (width, hidden)),
        out_shape=(
            jax.ShapeDtypeStruct((n_tok, width), BF16),
            jax.ShapeDtypeStruct(w_in_t.shape, F32),
            jax.ShapeDtypeStruct(w_out_t.shape, F32),
        ),
        in_specs=[vmem] * 6,
        out_specs=(vmem, vmem, vmem),
        scratch_shapes=scratch,
        compiler_params=pltpu.CompilerParams(
            collective_id=0, has_side_effects=True, vmem_limit_bytes=60 * 1024 * 1024
        ),
    )(
        tokens,
        attn_partials.reshape(NY, 2, n_tok, width),
        expert_ids.reshape(1, n_tok),
        gate.reshape(1, n_tok),
        w_in_t,
        w_out_t,
    )
    return token_grad, new_in.T, new_out.T


def solution(mesh):
    in_specs = (
        P(("expert", "dp"), None),
        P("dp", "expert", None),
        P(("expert", "dp")),
        P(("expert", "dp")),
        P("dp", "expert"),
        P("dp", "expert"),
    )
    out_specs = (P(("expert", "dp"), None), P("dp", "expert"), P("dp", "expert"))
    return jax.shard_map(shards, mesh=mesh, in_specs=in_specs, out_specs=out_specs, check_vma=False)
```

```python
import functools

import jax
import jax.numpy as jnp
from jax import lax
from jax.experimental import pallas as pl
from jax.experimental.pallas import tpu as pltpu
from jax.sharding import PartitionSpec as P

NX = 4
NY = 4
LINE = 4
BLOCKS = 4
CAP = 10
LANES = 128
MESH = pl.DeviceIdType.MESH

gelu_coef = 0.7978845608028654
cubic_coef = 0.044715
step_rate = 0.5
F32 = jnp.float32
BF16 = jnp.bfloat16


def add16(*terms):
    total = terms[0].astype(F32)
    for term in terms[1:]:
        total = total + term.astype(F32)
    return total.astype(BF16)


class Copy:
    def __init__(self, copy, when):
        self.copy = copy
        self.when = when

    def wait_recv(self, when=None):
        guarded(when, self.copy.wait_recv)


def guarded(when, action):
    if when is None:
        action()
    else:
        pl.when(when)(action)


class Copies:
    def __init__(self, send_sems, recv_sems):
        self.send_sems = send_sems
        self.recv_sems = recv_sems
        self.sends = 0
        self.recvs = 0
        self.started = []

    def slots(self, count):
        first = self.recvs
        self.recvs += count
        return first

    def make(self, src, dst, device, recv=None, send=None):
        if recv is None:
            recv = self.slots(1)
        if send is None:
            send = self.sends
            self.sends += 1
        return pltpu.make_async_remote_copy(
            src_ref=src,
            dst_ref=dst,
            send_sem=self.send_sems.at[send],
            recv_sem=self.recv_sems.at[recv],
            device_id=device,
            device_id_type=MESH,
        )

    def start(self, src, dst, device, when=None, recv=None):
        copy = Copy(self.make(src, dst, device, recv), when)
        guarded(when, copy.copy.start)
        self.started.append(copy)
        return copy

    def finish(self):
        for copy in self.started:
            guarded(copy.when, copy.copy.wait_send)


N_COPIES = 384


def kernel(
    dims,
    tok_ref, attn_ref, ids_ref, gate_ref, win_ref, wout_ref,
    tg_ref, nwin_ref, nwout_ref,
    pk_t, pk_g, x3, g3, x2, g2, perm, disp,
    w_stage, w_in, w_out, pre_slope, grad_sum, pg, pg_t, hid, p2, p3, p_mate,
    q3, zr, zl, zs_r, zs_l, own_r, own_l, own_sr, own_sl, slots,
    a_mate, a_sum, a_r1, a_m3, a_r3, a_r2,
    d_in, i_r1, i_m3, i_r3, i_r2, i_sum, is_r1, is_m3, is_r3, is_r2,
    d_out, o_r1, o_m3, o_r3, o_r2, o_sum, os_r1, os_m3, os_r3, os_r2,
    d_part, d_other,
    send_sems, recv_sems,
):
    width, hidden = dims
    scale_in = width ** (-0.5)
    scale_out = (hidden * NX * LINE) ** (-0.5)
    tiles = width // LANES
    share = hidden // 2
    depth = width // NY
    expert = lax.axis_index("expert")
    dp = lax.axis_index("dp")
    z = expert // NX
    x = expert % NX
    block = z // LINE
    place = z % LINE
    y = dp // 2
    core = dp % 2
    rows_b = LINE * CAP
    rows_d = BLOCKS * rows_b

    right = (z * NX + (x + 1) % NX, dp)
    left = (z * NX + (x + NX - 1) % NX, dp)
    up = (expert, ((y + 1) % NY) * 2 + core)
    down = (expert, ((y + NY - 1) % NY) * 2 + core)
    mate = (expert, y * 2 + (1 - core))

    last = LINE - 1
    not_first, not_last = place > 0, place < last
    at_first, at_last = place == 0, place == last
    front = ((z + 1) % (BLOCKS * LINE) * NX + x, dp)
    back_z = ((z + BLOCKS * LINE - 1) % (BLOCKS * LINE) * NX + x, dp)

    def seat(step, at):
        return ((((block + step + BLOCKS) % BLOCKS) * LINE + at) * NX + x, dp)

    barrier = pltpu.get_barrier_semaphore()

    def greet(device, when=None):
        guarded(when, lambda: pl.semaphore_signal(barrier, inc=1, device_id=device, device_id_type=MESH))

    for device in (right, left, up, down, mate):
        greet(device)
    greet(front, not_last)
    greet(back_z, not_first)
    for step in (1, 2):
        greet(seat(step, 0))
        greet(seat(-step, last))
        for at in range(LINE):
            greet(seat(step, at), at_last)
            greet(seat(-step, at), at_first)
    edge = jnp.where(at_first | at_last, 2 * LINE - 1, 0)
    greetings = 5 + 2 + 4 + edge

    copies = Copies(send_sems, recv_sems)

    def arrive(*waiting):
        for copy in waiting:
            copy.wait_recv()

    row_i = lax.broadcasted_iota(jnp.int32, (256, 256), 0)
    col_i = lax.broadcasted_iota(jnp.int32, (256, 256), 1)
    perm[...] = jnp.where(col_i == (row_i % 16) * 16 + row_i // 16, 1.0, 0.0).astype(BF16)

    n_tok = tok_ref.shape[0]
    ids_row = ids_ref[...].astype(F32)
    eye_t = lax.broadcasted_iota(jnp.int32, (n_tok, n_tok), 0)
    eye_s = lax.broadcasted_iota(jnp.int32, (n_tok, n_tok), 1)
    spread_ids = jnp.broadcast_to(ids_row, (n_tok, n_tok))
    ids_col = jnp.sum(jnp.where(eye_t == eye_s, spread_ids, 0.0), axis=1, keepdims=True)
    earlier = jnp.where((ids_col == spread_ids) & (eye_t < eye_s), 1.0, 0.0)
    rank_row = jnp.sum(earlier, axis=0, keepdims=True)
    slot_row = jnp.where(rank_row < CAP, ids_row * CAP + rank_row, -1.0)
    n_slot = disp.shape[0]
    slot_i = lax.broadcasted_iota(jnp.int32, (n_slot, n_tok), 0).astype(F32)
    disp[...] = jnp.where(slot_i == jnp.broadcast_to(slot_row, (n_slot, n_tok)), 1.0, 0.0).astype(BF16)
    gate_col = jnp.sum(
        jnp.where(eye_t == eye_s, jnp.broadcast_to(gate_ref[...], (n_tok, n_tok)), 0.0),
        axis=1, keepdims=True,
    )

    def pack(rows, dst):
        packed = jnp.dot(disp[...], rows, preferred_element_type=F32).astype(BF16)
        for g in range(n_slot // 16):
            stacked = jnp.concatenate(
                [packed[g * 16:(g + 1) * 16, k * LANES:(k + 1) * LANES] for k in range(tiles)], axis=0
            )
            moved = jnp.dot(perm[...], stacked, preferred_element_type=F32).astype(BF16)
            dst[g * 16:(g + 1) * 16] = moved.reshape(16, tiles, LANES)

    per = depth // LANES

    def to_wide(src, dst, half):
        def body(i, carry):
            pair = [src[half, pl.ds(i * 32 + h * 16, 16)].reshape(256, LANES) for h in range(2)]
            moved = jnp.dot(perm[...], jnp.concatenate(pair, axis=1), preferred_element_type=F32).astype(BF16)
            for h in range(2):
                at = pl.ds(pl.multiple_of(half * rows_d + i * 32 + h * 16, 16), 16)
                for k in range(tiles):
                    dst[k // per, at, (k % per) * LANES:(k % per + 1) * LANES] = moved[
                        k * 16:(k + 1) * 16, h * LANES:(h + 1) * LANES
                    ]
            return carry

        lax.fori_loop(0, rows_d // 32, body, 0)

    def to_narrow(src, dst, half):
        def body(i, carry):
            pair = []
            for h in range(2):
                at = pl.ds(pl.multiple_of(i * 32 + h * 16, 16), 16)
                pair.append(jnp.concatenate(
                    [src[k // per, at, (k % per) * LANES:(k % per + 1) * LANES] for k in range(tiles)], axis=0
                ))
            moved = jnp.dot(perm[...], jnp.concatenate(pair, axis=1), preferred_element_type=F32).astype(BF16)
            for h in range(2):
                dst[half, pl.ds(i * 32 + h * 16, 16)] = moved[:, h * LANES:(h + 1) * LANES].reshape(16, tiles, LANES)
            return carry

        lax.fori_loop(0, rows_d // 32, body, 0)

    pack(tok_ref[...], pk_t)

    def row_at(c, p):
        return c * rows_b + p * CAP

    x3[core, pl.ds(row_at(block, place), CAP)] = pk_t[pl.ds(block * CAP, CAP)]
    mine = pl.ds(pl.multiple_of(core * share, share), share)
    other = pl.ds(pl.multiple_of((1 - core) * share, share), share)
    lanes_mine = pl.ds(pl.multiple_of(core * (depth // 2), depth // 2), depth // 2)
    lanes_other = pl.ds(pl.multiple_of((1 - core) * (depth // 2), depth // 2), depth // 2)
    w_in[y, x, :, lanes_mine] = win_ref[mine].astype(BF16)
    w_out[x, y, :, lanes_mine] = wout_ref[mine].astype(BF16)
    w_stage[0] = win_ref[other].astype(BF16)
    w_stage[1] = wout_ref[other].astype(BF16)
    @pl.when(at_first)
    def _():
        zr[...] = jnp.zeros_like(zr)
        own_r[...] = jnp.zeros_like(own_r)

    @pl.when(at_last)
    def _():
        zl[...] = jnp.zeros_like(zl)
        own_l[...] = jnp.zeros_like(own_l)

    slots[BLOCKS * CAP:] = jnp.zeros((slots.shape[0] - BLOCKS * CAP, tiles, LANES), BF16)

    pl.semaphore_wait(barrier, greetings)

    def halves(count):
        return pl.ds(0, count // 2), pl.ds(count // 2, count // 2)

    X_RING = (x, right, left)
    Y_RING = (y, up, down)

    def gather_first(blk, ring):
        pos, upper, lower = ring
        return [copies.start(blk(pos), blk(pos), device) for device in (upper, lower)]

    def gather_next(sent, blk, ring):
        pos, upper, lower = ring
        low, high = halves(share)
        below, above = (pos + 3) % 4, (pos + 1) % 4
        sent[0].wait_recv()
        to_up = copies.start(blk(below).at[low], blk(below).at[low], upper)
        sent[1].wait_recv()
        to_down = copies.start(blk(above).at[high], blk(above).at[high], lower)
        return [to_up, to_down]

    def scatter_first(blk, count, buf1, buf2, ring):
        pos, upper, lower = ring
        low, high = halves(count)
        far, above, below = (pos + 2) % 4, (pos + 1) % 4, (pos + 3) % 4
        return {
            "u1": copies.start(blk(far).at[low], buf1.at[0], upper),
            "d1": copies.start(blk(far).at[high], buf1.at[1], lower),
            "u2": copies.start(blk(above).at[high], buf2.at[0], upper),
            "d2": copies.start(blk(below).at[low], buf2.at[1], lower),
        }

    def scatter_middle(sent, blk, count, buf1, mid, buf3, ring):
        pos, upper, lower = ring
        low, high = halves(count)
        sent["u1"].wait_recv()
        mid[0] = add16(buf1[0], blk((pos + 1) % 4).at[low][...])
        sent["u3"] = copies.start(mid.at[0], buf3.at[0], upper)
        sent["d1"].wait_recv()
        mid[1] = add16(buf1[1], blk((pos + 3) % 4).at[high][...])
        sent["d3"] = copies.start(mid.at[1], buf3.at[1], lower)

    def scatter_end(sent, blk, count, buf2, buf3, ring):
        low, high = halves(count)
        pos = ring[0]
        arrive(sent["d2"], sent["u3"])
        first = blk(pos).at[low][...].astype(F32) + buf2[1].astype(F32) + buf3[0].astype(F32)
        arrive(sent["u2"], sent["d3"])
        second = blk(pos).at[high][...].astype(F32) + buf2[0].astype(F32) + buf3[1].astype(F32)
        return first, second

    def attn_begin(sent):
        low, high = halves(n_tok)
        out = {}
        for q in (2, 1, 3, 0):
            at = (y + q) % NY
            sent[q].wait_recv()
            a_sum[at] = add16(attn_ref[at, core], a_mate[at])
            if q == 2:
                out["u1"] = copies.start(a_sum.at[at, low], a_r1.at[0], up)
                out["d1"] = copies.start(a_sum.at[at, high], a_r1.at[1], down)
            elif q == 1:
                out["u2"] = copies.start(a_sum.at[at, high], a_r2.at[0], up)
            elif q == 3:
                out["d2"] = copies.start(a_sum.at[at, low], a_r2.at[1], down)
        return out

    part = CAP // 2

    def chunk(j):
        return (block + BLOCKS + j) % BLOCKS

    def z_begin(packed, rows):
        here = pl.ds(row_at(block, place), CAP)
        mine_at = pl.ds(block * CAP, CAP)
        state = {"rows": rows, "edge": {}, "relay": {}}
        state["r1"] = copies.start(packed.at[mine_at], rows.at[core, here], front, not_last)
        state["l1"] = copies.start(packed.at[mine_at], rows.at[core, here], back_z, not_first)
        for step in (1, 2):
            for sign in (1, -1):
                to = chunk(sign * step)
                skip = part if (step == 2 and sign == -1) else 0
                count = CAP if step == 1 else part
                first = copies.slots(LINE)
                src = packed.at[pl.ds(to * CAP + skip, count)]
                dst = rows.at[core, pl.ds(row_at(block, place) + skip, count)]
                copies.start(src, dst, seat(sign * step, 0 if sign == 1 else last), recv=first + place)
                state["edge"][sign * step] = (first, skip, count)
        return state

    def z_line(state, n):
        rows = state["rows"]
        for key, sign, ahead, came, go in (("r", 1, front, place >= n, not_last), ("l", -1, back_z, place + n <= last, not_first)):
            state[key + str(n)].wait_recv(came)
            if n < last:
                at = pl.ds(row_at(block, jnp.clip(place - sign * n, 0, last)), CAP)
                state[key + str(n + 1)] = copies.start(rows.at[core, at], rows.at[core, at], ahead, came & go)

    def z_edge(state, step):
        rows = state["rows"]
        for i in range(LINE):
            for sign, ahead, entry, inner, go in (
                (1, front, at_first, not_first, not_last), (-1, back_z, at_last, not_last, not_first),
            ):
                first, skip, count = state["edge"][sign * step]
                source = last - i if sign == 1 else i
                at = rows.at[core, pl.ds(row_at(chunk(-sign * step), source) + skip, count)]
                direct = copies.make(at, at, mate, recv=first + source, send=0)
                guarded(entry, direct.wait_recv)
                key = (sign * step, source)
                relay = copies.start(at, at, ahead, go & entry)
                state["relay"][key] = relay
                relay.wait_recv(inner)
                inside = Copy(relay.copy, go & inner)
                guarded(inside.when, inside.copy.start)
                copies.started.append(inside)

    def z_share(state, j):
        at = state["rows"].at[core, pl.ds(row_at(chunk(j), 0), rows_b)]
        return copies.start(at, at, mate)

    def back_share(j):
        at = pl.ds(row_at(chunk(j), 0), rows_b)
        return copies.start(p3.at[1 - core, at], p_mate.at[at], mate)

    def back_sum(copy, j):
        at = pl.ds(row_at(chunk(j), 0), rows_b)
        copy.wait_recv()
        q3[at] = add16(p3[core, at], p_mate[at])

    def back_chain(step):
        ends = []
        for sign in (1, -1):
            ends.append(copies.slots(1))
        for i in range(LINE):
            for sign, ahead, inner, go, leave, buf, out in (
                (1, front, not_first, not_last, at_last, zr, zs_r), (-1, back_z, not_last, not_first, at_first, zl, zs_l),
            ):
                skip = part if (step == 2 and sign == -1) else 0
                count = CAP if step == 1 else part
                source = last - i if sign == 1 else i
                slot = (step - 1) * LINE + source
                src = out.at[slot, pl.ds(0, count)]
                relay = copies.make(src, buf.at[slot, pl.ds(0, count)], ahead)
                guarded(inner, relay.wait_recv)
                at = pl.ds(row_at(chunk(sign * step), source) + skip, count)
                out[slot, 0:count] = add16(q3[at], buf[slot, 0:count])
                kept = Copy(relay, go)
                guarded(go, relay.start)
                copies.started.append(kept)
                end = ends[0 if sign == 1 else 1]
                copies.start(
                    src, slots.at[pl.ds(block * CAP + skip, count)], seat(sign * step, source), leave, recv=end
                )
        waits = []
        for sign, end in ((1, ends[0]), (-1, ends[1])):
            skip = part if (step == 2 and sign == -1) else 0
            count = CAP if step == 1 else part
            at = slots.at[pl.ds(chunk(-sign * step) * CAP + skip, count)]
            waits.append(copies.make(at, at, mate, recv=end, send=0))
        return waits

    def back_own():
        for n in (3, 2, 1):
            for key, sign, ahead, buf, out in (("r", 1, front, own_r, own_sr), ("l", -1, back_z, own_l, own_sl)):
                target = place + sign * n
                valid = (target >= 0) & (target <= last)
                at = pl.ds(row_at(block, jnp.clip(target, 0, last)), CAP)
                behind = (place - sign >= 0) & (place - sign <= last)
                if n < last:
                    own_state[key + str(n + 1)].wait_recv(valid & behind)
                out[n - 1] = add16(q3[at], buf[n])
                own_state[key + str(n)] = copies.start(out.at[n - 1], buf.at[n - 1], ahead, valid)

    def back_own_end():
        own_state["r1"].wait_recv(not_first)
        own_state["l1"].wait_recv(not_last)
        slots[pl.ds(block * CAP, CAP)] = add16(q3[pl.ds(row_at(block, place), CAP)], own_r[0], own_l[0])

    own_state = {}

    def in_x(i):
        return w_in.at[y, i]

    def out_y(i):
        return w_out.at[x, i]

    def in_y(s):
        return lambda i: w_in.at[i, s]

    def out_x(s):
        return lambda i: w_out.at[i, s]

    def forward(i):
        pre = None
        for k in range(NY):
            term = lax.dot_general(
                x2[k], w_in[k, i], (((1,), (1,)), ((), ())), preferred_element_type=F32
            )
            pre = term if pre is None else pre + term
        pre = pre * scale_in
        square = pre * pre
        tangent = jnp.tanh(gelu_coef * (pre + cubic_coef * square * pre))
        hid[i] = (0.5 * pre * (1.0 + tangent)).astype(BF16).T
        pre_slope[i] = scale_out * (
            0.5 * (1.0 + tangent) + 0.5 * pre * (1.0 - tangent * tangent) * gelu_coef * (1.0 + 3.0 * cubic_coef * square)
        )

    def out_grads(i):
        for k in range(NY):
            d_out[i, k] = (jnp.dot(hid[i], g2[k], preferred_element_type=F32) * scale_out).astype(BF16)

    def hidden_grads(k, begin):
        for i in range(NX):
            term = lax.dot_general(
                g2[k], w_out[i, k], (((1,), (1,)), ((), ())), preferred_element_type=F32
            )
            grad_sum[i] = term if begin else grad_sum[i] + term

    def in_grads(k):
        for i in range(NX):
            d_in[k, i] = (jnp.dot(pg_t[i], x2[k], preferred_element_type=F32) * scale_in).astype(BF16)

    order = (0, 1, 3, 2)
    w_pair = [
        copies.start(w_stage.at[0], w_in.at[y, x, :, lanes_mine], mate),
        copies.start(w_stage.at[1], w_out.at[x, y, :, lanes_mine], mate),
    ]
    t_state = z_begin(pk_t, x3)
    attn_sent = {}
    for q in (2, 1, 3, 0):
        at = (y + q) % NY
        attn_sent[q] = copies.start(attn_ref.at[at, 1 - core], a_mate.at[at], mate)
    arrive(w_pair[0])
    in_first = gather_first(in_x, X_RING)
    arrive(w_pair[1])
    attn_ring = attn_begin(attn_sent)
    out_first = gather_first(out_y, Y_RING)
    in_big, out_big = {}, {}
    in_big[0] = gather_first(in_y(x), Y_RING)
    out_big[0] = gather_first(out_x(y), X_RING)
    z_line(t_state, 1)
    in_next = gather_next(in_first, in_x, X_RING)
    z_edge(t_state, 1)
    for q in (1, 3):
        in_big[q] = gather_first(in_y((x + q) % NX), Y_RING)
    z_line(t_state, 2)
    scatter_middle(attn_ring, lambda i: a_sum.at[i], n_tok, a_r1, a_m3, a_r3, Y_RING)
    out_next = gather_next(out_first, out_y, Y_RING)
    for q in (1, 3):
        out_big[q] = gather_first(out_x((y + q) % NY), X_RING)
    z_edge(t_state, 2)
    arrive(*in_next)
    in_big[2] = gather_first(in_y((x + 2) % NX), Y_RING)
    z_line(t_state, 3)
    first, second = scatter_end(attn_ring, lambda i: a_sum.at[i], n_tok, a_r2, a_r3, Y_RING)
    summed = jnp.concatenate([first, second], axis=0)
    pack((gate_col * summed).astype(BF16), pk_g)
    g3[core, pl.ds(row_at(block, place), CAP)] = pk_g[pl.ds(block * CAP, CAP)]
    g_state = z_begin(pk_g, g3)
    t_share = [z_share(t_state, j) for j in range(4)]
    arrive(*out_next)
    out_big[2] = gather_first(out_x((y + 2) % NY), X_RING)
    in_last, out_last = {}, {}
    in_last[0] = gather_next(in_big[0], in_y(x), Y_RING)
    out_last[0] = gather_next(out_big[0], out_x(y), X_RING)
    to_wide(x3, x2, core)
    z_line(g_state, 1)
    z_edge(g_state, 1)
    arrive(*t_share)
    to_wide(x3, x2, 1 - core)
    z_line(g_state, 2)
    for q in (1, 3):
        in_last[q] = gather_next(in_big[q], in_y((x + q) % NX), Y_RING)
        out_last[q] = gather_next(out_big[q], out_x((y + q) % NY), X_RING)
    arrive(*in_last[0])
    forward(x)
    z_edge(g_state, 2)
    z_line(g_state, 3)
    g_share = [z_share(g_state, j) for j in range(4)]
    to_wide(g3, g2, core)
    in_last[2] = gather_next(in_big[2], in_y((x + 2) % NX), Y_RING)
    out_last[2] = gather_next(out_big[2], out_x((y + 2) % NY), X_RING)
    arrive(*g_share)
    to_wide(g3, g2, 1 - core)
    out_grads(x)
    arrive(*out_last[0])
    hidden_grads(y, True)
    for q in (1, 3):
        arrive(*in_last[q])
        forward((x + q) % NX)
        out_grads((x + q) % NX)
        arrive(*out_last[q])
        hidden_grads((y + q) % NY, False)
    arrive(*in_last[2])
    forward((x + 2) % NX)
    out_grads((x + 2) % NX)
    out_ring = scatter_first(lambda i: d_out.at[i], NY, o_r1, o_r2, X_RING)
    arrive(*out_last[2])
    hidden_grads((y + 2) % NY, False)
    for i in range(NX):
        grad = (grad_sum[i] * pre_slope[i]).astype(BF16)
        pg[i] = grad
        pg_t[i] = grad.T
    for q in (2, 1, 3):
        in_grads((y + q) % NY)
    in_ring = scatter_first(lambda i: d_in.at[i], NX, i_r1, i_r2, Y_RING)

    back = {}
    for part_i in range(2):
        half = (1 - core) if part_i == 0 else core
        for k in range(NY):
            term = None
            for i in range(NX):
                add = jnp.dot(
                    pg[i, pl.ds(pl.multiple_of(half * rows_d, rows_d), rows_d)], w_in[k, i],
                    preferred_element_type=F32,
                )
                term = add if term is None else term + add
            p2[k] = (term * scale_in).astype(BF16)
        to_narrow(p2, p3, half)
        if part_i == 0:
            for j in order:
                back[j] = back_share(j)
            scatter_middle(out_ring, lambda i: d_out.at[i], NY, o_r1, o_m3, o_r3, X_RING)
    for j in order:
        back_sum(back[j], j)
    back_own()
    ends = back_chain(1)
    in_grads(y)
    scatter_middle(in_ring, lambda i: d_in.at[i], NX, i_r1, i_m3, i_r3, Y_RING)
    ends += back_chain(2)
    back_own_end()

    first, second = scatter_end(out_ring, lambda i: d_out.at[i], NY, o_r2, o_r3, X_RING)
    o_sum[0:2] = first.astype(BF16)
    o_sum[2:4] = second.astype(BF16)
    out_small = scatter_first(lambda i: o_sum.at[i], share, os_r1, os_r2, Y_RING)
    first, second = scatter_end(in_ring, lambda i: d_in.at[i], NX, i_r2, i_r3, Y_RING)
    i_sum[0:2] = first.astype(BF16)
    i_sum[2:4] = second.astype(BF16)
    in_small = scatter_first(lambda i: i_sum.at[i], share, is_r1, is_r2, X_RING)
    scatter_middle(out_small, lambda i: o_sum.at[i], share, os_r1, os_m3, os_r3, Y_RING)
    scatter_middle(in_small, lambda i: i_sum.at[i], share, is_r1, is_m3, is_r3, X_RING)
    pair = []
    for t, sent, sums, buf2, buf3, ring in (
        (1, out_small, o_sum, os_r2, os_r3, Y_RING), (0, in_small, i_sum, is_r2, is_r3, X_RING),
    ):
        low, high = halves(share)
        first, second = scatter_end(sent, lambda i: sums.at[i], share, buf2, buf3, ring)
        d_part[t, low] = first.astype(BF16)
        d_part[t, high] = second.astype(BF16)
        pair.append(copies.start(d_part.at[t, :, lanes_other], d_other.at[t], mate))

    for copy in ends:
        copy.wait_recv()
    wide = []
    for g in range(n_slot // 16):
        moved = jnp.dot(
            perm[...], slots[g * 16:(g + 1) * 16].reshape(256, LANES), preferred_element_type=F32
        ).astype(BF16)
        wide.append(jnp.concatenate([moved[k * 16:(k + 1) * 16] for k in range(tiles)], axis=1))
    slots_wide = jnp.concatenate(wide, axis=0)
    tg_ref[...] = lax.dot_general(
        disp[...], slots_wide, (((0,), (0,)), ((), ())), preferred_element_type=F32
    ).astype(BF16)

    for t, copy, old, new in ((1, pair[0], wout_ref, nwout_ref), (0, pair[1], win_ref, nwin_ref)):
        new[mine] = old[mine] - step_rate * d_part[t, :, lanes_mine].astype(F32)
        copy.wait_recv()
        new[other] = old[other] - step_rate * d_other[t].astype(F32)
    copies.finish()


def shards(tokens, attn_partials, expert_ids, gate, w_in, w_out):
    n_tok, width = tokens.shape
    w_in_t, w_out_t = w_in.T, w_out.T
    hidden = w_in_t.shape[0]
    tiles = width // LANES
    rows_b = LINE * CAP
    rows_d = BLOCKS * rows_b
    share = hidden // 2
    depth = width // NY
    slot_rows = 48
    vmem = pl.BlockSpec(memory_space=pltpu.VMEM)

    def bf16(*shape):
        return pltpu.VMEM(shape, BF16)

    def rows16(*lead):
        return bf16(*lead, tiles, LANES)

    scratch = [
        rows16(slot_rows), rows16(slot_rows), rows16(2, rows_d), rows16(2, rows_d),
        bf16(NY, 2 * rows_d, depth), bf16(NY, 2 * rows_d, depth),
        bf16(256, 256), bf16(slot_rows, n_tok),
        bf16(2, share, depth // 2), bf16(NY, NX, share, depth), bf16(NX, NY, share, depth),
        pltpu.VMEM((NX, 2 * rows_d, share), F32), pltpu.VMEM((NX, 2 * rows_d, share), F32),
        bf16(NX, 2 * rows_d, share), bf16(NX, share, 2 * rows_d), bf16(NX, share, 2 * rows_d),
        bf16(NY, rows_d, depth), rows16(2, rows_d), rows16(rows_d),
        rows16(rows_d), rows16(2 * LINE, CAP), rows16(2 * LINE, CAP), rows16(2 * LINE, CAP), rows16(2 * LINE, CAP),
        rows16(LINE, CAP), rows16(LINE, CAP), rows16(LINE, CAP), rows16(LINE, CAP), rows16(slot_rows),
        bf16(NY, n_tok, width), bf16(NY, n_tok, width),
    ]
    scratch += [bf16(2, n_tok // 2, width)] * 4
    for _ in range(2):
        scratch += [bf16(4, 4, share, depth)] + [bf16(2, 2, share, depth)] * 4
        scratch += [bf16(4, share, depth)] + [bf16(2, share // 2, depth)] * 4
    scratch += [bf16(2, share, depth), bf16(2, share, depth // 2)]
    scratch += [pltpu.SemaphoreType.DMA((N_COPIES,)), pltpu.SemaphoreType.DMA((N_COPIES,))]
    token_grad, new_in, new_out = pl.pallas_call(
        functools.partial(kernel, (width, hidden)),
        out_shape=(
            jax.ShapeDtypeStruct((n_tok, width), BF16),
            jax.ShapeDtypeStruct(w_in_t.shape, F32),
            jax.ShapeDtypeStruct(w_out_t.shape, F32),
        ),
        in_specs=[vmem] * 6,
        out_specs=(vmem, vmem, vmem),
        scratch_shapes=scratch,
        compiler_params=pltpu.CompilerParams(
            collective_id=0, has_side_effects=True, vmem_limit_bytes=60 * 1024 * 1024
        ),
    )(
        tokens,
        attn_partials.reshape(NY, 2, n_tok, width),
        expert_ids.reshape(1, n_tok),
        gate.reshape(1, n_tok),
        w_in_t,
        w_out_t,
    )
    return token_grad, new_in.T, new_out.T


def solution(mesh):
    in_specs = (
        P(("expert", "dp"), None),
        P("dp", "expert", None),
        P(("expert", "dp")),
        P(("expert", "dp")),
        P("dp", "expert"),
        P("dp", "expert"),
    )
    out_specs = (P(("expert", "dp"), None), P("dp", "expert"), P("dp", "expert"))
    return jax.shard_map(shards, mesh=mesh, in_specs=in_specs, out_specs=out_specs, check_vma=False)
```

```python
import functools

import jax
import jax.numpy as jnp
from jax import lax
from jax.experimental import pallas as pl
from jax.experimental.pallas import tpu as pltpu
from jax.sharding import PartitionSpec as P

NX = 4
NY = 4
LINE = 4
BLOCKS = 4
CAP = 10
LANES = 128
MESH = pl.DeviceIdType.MESH

gelu_coef = 0.7978845608028654
cubic_coef = 0.044715
step_rate = 0.5
F32 = jnp.float32
BF16 = jnp.bfloat16


def add16(*terms):
    total = terms[0].astype(F32)
    for term in terms[1:]:
        total = total + term.astype(F32)
    return total.astype(BF16)


class Copy:
    def __init__(self, copy, when):
        self.copy = copy
        self.when = when

    def wait_recv(self, when=None):
        guarded(when, self.copy.wait_recv)


def guarded(when, action):
    if when is None:
        action()
    else:
        pl.when(when)(action)


class Copies:
    def __init__(self, send_sems, recv_sems):
        self.send_sems = send_sems
        self.recv_sems = recv_sems
        self.sends = 0
        self.recvs = 0
        self.started = []

    def slots(self, count):
        first = self.recvs
        self.recvs += count
        return first

    def send_slots(self, count):
        first = self.sends
        self.sends += count
        return first

    def make(self, src, dst, device, recv=None, send=None):
        if recv is None:
            recv = self.slots(1)
        if send is None:
            send = self.sends
            self.sends += 1
        return pltpu.make_async_remote_copy(
            src_ref=src,
            dst_ref=dst,
            send_sem=self.send_sems.at[send],
            recv_sem=self.recv_sems.at[recv],
            device_id=device,
            device_id_type=MESH,
        )

    def start(self, src, dst, device, when=None, recv=None):
        copy = Copy(self.make(src, dst, device, recv), when)
        guarded(when, copy.copy.start)
        self.started.append(copy)
        return copy

    def finish(self):
        for copy in self.started:
            guarded(copy.when, copy.copy.wait_send)


N_COPIES = 384
CHAIN = 3
LAG = 2


def kernel(
    dims,
    tok_ref, attn_ref, ids_ref, gate_ref, win_ref, wout_ref,
    tg_ref, nwin_ref, nwout_ref,
    pk_t, pk_g, x3, g3, x2, g2, perm, disp,
    w_stage, w_in, w_out, pre_slope, grad_sum, pg, pg_t, hid, p2, p3, p_mate,
    q3, zr, zl, zs_r, zs_l, own_r, own_l, own_sr, own_sl, slots,
    a_mate, a_sum, a_r1, a_m3, a_r3, a_r2,
    d_in, i_r1, i_m3, i_r3, i_r2, i_sum, is_r1, is_m3, is_r3, is_r2,
    d_out, o_r1, o_m3, o_r3, o_r2, o_sum, os_r1, os_m3, os_r3, os_r2,
    d_part, d_other,
    send_sems, recv_sems,
):
    width, hidden = dims
    scale_in = width ** (-0.5)
    scale_out = (hidden * NX * LINE) ** (-0.5)
    tiles = width // LANES
    share = hidden // 2
    depth = width // NY
    expert = lax.axis_index("expert")
    dp = lax.axis_index("dp")
    z = expert // NX
    x = expert % NX
    block = z // LINE
    place = z % LINE
    y = dp // 2
    core = dp % 2
    rows_b = LINE * CAP
    rows_d = BLOCKS * rows_b

    right = (z * NX + (x + 1) % NX, dp)
    left = (z * NX + (x + NX - 1) % NX, dp)
    up = (expert, ((y + 1) % NY) * 2 + core)
    down = (expert, ((y + NY - 1) % NY) * 2 + core)
    mate = (expert, y * 2 + (1 - core))

    last = LINE - 1
    not_first, not_last = place > 0, place < last
    at_first, at_last = place == 0, place == last
    front = ((z + 1) % (BLOCKS * LINE) * NX + x, dp)
    back_z = ((z + BLOCKS * LINE - 1) % (BLOCKS * LINE) * NX + x, dp)

    def seat(step, at):
        return ((((block + step + BLOCKS) % BLOCKS) * LINE + at) * NX + x, dp)

    barrier = pltpu.get_barrier_semaphore()

    def greet(device, when=None):
        guarded(when, lambda: pl.semaphore_signal(barrier, inc=1, device_id=device, device_id_type=MESH))

    for device in (right, left, up, down, mate):
        greet(device)
    greet(front, not_last)
    greet(back_z, not_first)
    for step in (1, 2):
        greet(seat(step, 0))
        greet(seat(-step, last))
        for at in range(LINE):
            greet(seat(step, at), at_last)
            greet(seat(-step, at), at_first)
    edge = jnp.where(at_first | at_last, 2 * LINE - 1, 0)
    greetings = 5 + 2 + 4 + edge

    copies = Copies(send_sems, recv_sems)

    def arrive(*waiting):
        for copy in waiting:
            copy.wait_recv()

    row_i = lax.broadcasted_iota(jnp.int32, (256, 256), 0)
    col_i = lax.broadcasted_iota(jnp.int32, (256, 256), 1)
    perm[...] = jnp.where(col_i == (row_i % 16) * 16 + row_i // 16, 1.0, 0.0).astype(BF16)

    n_tok = tok_ref.shape[0]
    ids_row = ids_ref[...].astype(F32)
    eye_t = lax.broadcasted_iota(jnp.int32, (n_tok, n_tok), 0)
    eye_s = lax.broadcasted_iota(jnp.int32, (n_tok, n_tok), 1)
    spread_ids = jnp.broadcast_to(ids_row, (n_tok, n_tok))
    ids_col = jnp.sum(jnp.where(eye_t == eye_s, spread_ids, 0.0), axis=1, keepdims=True)
    earlier = jnp.where((ids_col == spread_ids) & (eye_t < eye_s), 1.0, 0.0)
    rank_row = jnp.sum(earlier, axis=0, keepdims=True)
    slot_row = jnp.where(rank_row < CAP, ids_row * CAP + rank_row, -1.0)
    n_slot = disp.shape[0]
    slot_i = lax.broadcasted_iota(jnp.int32, (n_slot, n_tok), 0).astype(F32)
    disp[...] = jnp.where(slot_i == jnp.broadcast_to(slot_row, (n_slot, n_tok)), 1.0, 0.0).astype(BF16)
    gate_col = jnp.sum(
        jnp.where(eye_t == eye_s, jnp.broadcast_to(gate_ref[...], (n_tok, n_tok)), 0.0),
        axis=1, keepdims=True,
    )

    def pack(rows, dst):
        packed = jnp.dot(disp[...], rows, preferred_element_type=F32).astype(BF16)
        for g in range(n_slot // 16):
            stacked = jnp.concatenate(
                [packed[g * 16:(g + 1) * 16, k * LANES:(k + 1) * LANES] for k in range(tiles)], axis=0
            )
            moved = jnp.dot(perm[...], stacked, preferred_element_type=F32).astype(BF16)
            dst[g * 16:(g + 1) * 16] = moved.reshape(16, tiles, LANES)

    per = depth // LANES

    def to_wide(src, dst, half):
        def body(i, carry):
            pair = [src[half, pl.ds(i * 32 + h * 16, 16)].reshape(256, LANES) for h in range(2)]
            moved = jnp.dot(perm[...], jnp.concatenate(pair, axis=1), preferred_element_type=F32).astype(BF16)
            for h in range(2):
                at = pl.ds(pl.multiple_of(half * rows_d + i * 32 + h * 16, 16), 16)
                for k in range(tiles):
                    dst[k // per, at, (k % per) * LANES:(k % per + 1) * LANES] = moved[
                        k * 16:(k + 1) * 16, h * LANES:(h + 1) * LANES
                    ]
            return carry

        lax.fori_loop(0, rows_d // 32, body, 0)

    def to_narrow(src, dst, half):
        def body(i, carry):
            pair = []
            for h in range(2):
                at = pl.ds(pl.multiple_of(i * 32 + h * 16, 16), 16)
                pair.append(jnp.concatenate(
                    [src[k // per, at, (k % per) * LANES:(k % per + 1) * LANES] for k in range(tiles)], axis=0
                ))
            moved = jnp.dot(perm[...], jnp.concatenate(pair, axis=1), preferred_element_type=F32).astype(BF16)
            for h in range(2):
                dst[half, pl.ds(i * 32 + h * 16, 16)] = moved[:, h * LANES:(h + 1) * LANES].reshape(16, tiles, LANES)
            return carry

        lax.fori_loop(0, rows_d // 32, body, 0)

    pack(tok_ref[...], pk_t)

    def row_at(c, p):
        return c * rows_b + p * CAP

    x3[core, pl.ds(row_at(block, place), CAP)] = pk_t[pl.ds(block * CAP, CAP)]
    mine = pl.ds(pl.multiple_of(core * share, share), share)
    other = pl.ds(pl.multiple_of((1 - core) * share, share), share)
    lanes_mine = pl.ds(pl.multiple_of(core * (depth // 2), depth // 2), depth // 2)
    lanes_other = pl.ds(pl.multiple_of((1 - core) * (depth // 2), depth // 2), depth // 2)
    w_in[y, x, :, lanes_mine] = win_ref[mine].astype(BF16)
    w_out[x, y, :, lanes_mine] = wout_ref[mine].astype(BF16)
    w_stage[0] = win_ref[other].astype(BF16)
    w_stage[1] = wout_ref[other].astype(BF16)
    @pl.when(at_first)
    def _():
        zr[...] = jnp.zeros_like(zr)
        own_r[...] = jnp.zeros_like(own_r)

    @pl.when(at_last)
    def _():
        zl[...] = jnp.zeros_like(zl)
        own_l[...] = jnp.zeros_like(own_l)

    slots[BLOCKS * CAP:] = jnp.zeros((slots.shape[0] - BLOCKS * CAP, tiles, LANES), BF16)

    pl.semaphore_wait(barrier, greetings)

    def halves(count):
        return pl.ds(0, count // 2), pl.ds(count // 2, count // 2)

    X_RING = (x, right, left)
    Y_RING = (y, up, down)

    def gather_first(blk, ring):
        pos, upper, lower = ring
        return [copies.start(blk(pos), blk(pos), device) for device in (upper, lower)]

    def gather_next(sent, blk, ring):
        pos, upper, lower = ring
        low, high = halves(share)
        below, above = (pos + 3) % 4, (pos + 1) % 4
        sent[0].wait_recv()
        to_up = copies.start(blk(below).at[low], blk(below).at[low], upper)
        sent[1].wait_recv()
        to_down = copies.start(blk(above).at[high], blk(above).at[high], lower)
        return [to_up, to_down]

    def scatter_first(blk, count, buf1, buf2, ring):
        pos, upper, lower = ring
        low, high = halves(count)
        far, above, below = (pos + 2) % 4, (pos + 1) % 4, (pos + 3) % 4
        return {
            "u1": copies.start(blk(far).at[low], buf1.at[0], upper),
            "d1": copies.start(blk(far).at[high], buf1.at[1], lower),
            "u2": copies.start(blk(above).at[high], buf2.at[0], upper),
            "d2": copies.start(blk(below).at[low], buf2.at[1], lower),
        }

    def scatter_middle(sent, blk, count, buf1, mid, buf3, ring):
        pos, upper, lower = ring
        low, high = halves(count)
        sent["u1"].wait_recv()
        mid[0] = add16(buf1[0], blk((pos + 1) % 4).at[low][...])
        sent["u3"] = copies.start(mid.at[0], buf3.at[0], upper)
        sent["d1"].wait_recv()
        mid[1] = add16(buf1[1], blk((pos + 3) % 4).at[high][...])
        sent["d3"] = copies.start(mid.at[1], buf3.at[1], lower)

    def scatter_end(sent, blk, count, buf2, buf3, ring):
        low, high = halves(count)
        pos = ring[0]
        arrive(sent["d2"], sent["u3"])
        first = blk(pos).at[low][...].astype(F32) + buf2[1].astype(F32) + buf3[0].astype(F32)
        arrive(sent["u2"], sent["d3"])
        second = blk(pos).at[high][...].astype(F32) + buf2[0].astype(F32) + buf3[1].astype(F32)
        return first, second

    def attn_begin(sent):
        low, high = halves(n_tok)
        out = {}
        for q in (2, 1, 3, 0):
            at = (y + q) % NY
            sent[q].wait_recv()
            a_sum[at] = add16(attn_ref[at, core], a_mate[at])
            if q == 2:
                out["u1"] = copies.start(a_sum.at[at, low], a_r1.at[0], up)
                out["d1"] = copies.start(a_sum.at[at, high], a_r1.at[1], down)
            elif q == 1:
                out["u2"] = copies.start(a_sum.at[at, high], a_r2.at[0], up)
            elif q == 3:
                out["d2"] = copies.start(a_sum.at[at, low], a_r2.at[1], down)
        return out

    def chunk(j):
        return (block + BLOCKS + j) % BLOCKS

    def z_begin(packed, rows):
        here = pl.ds(row_at(block, place), CAP)
        mine_at = pl.ds(block * CAP, CAP)
        state = {"rows": rows, "edge": {}, "relay": {}}
        state["r1"] = copies.start(packed.at[mine_at], rows.at[core, here], front, not_last)
        state["l1"] = copies.start(packed.at[mine_at], rows.at[core, here], back_z, not_first)
        for step in (1, 2):
            for sign in (1, -1):
                first = copies.slots(LINE)
                sends = None if step == 1 else (place >= 2 if sign == 1 else place < 2)
                copies.start(
                    packed.at[pl.ds(chunk(sign * step) * CAP, CAP)], rows.at[core, here],
                    seat(sign * step, 0 if sign == 1 else last), sends, recv=first + place,
                )
                state["edge"][sign * step] = first
        for sign in (1, -1):
            state["relay"][sign] = (copies.slots(CHAIN), copies.send_slots(CHAIN))
        return state

    def z_line(state, n):
        rows = state["rows"]
        for key, sign, ahead, came, go in (("r", 1, front, place >= n, not_last), ("l", -1, back_z, place + n <= last, not_first)):
            state[key + str(n)].wait_recv(came)
            if n < last:
                at = pl.ds(row_at(block, jnp.clip(place - sign * n, 0, last)), CAP)
                state[key + str(n + 1)] = copies.start(rows.at[core, at], rows.at[core, at], ahead, came & go)

    directions = (
        (1, front, at_first, not_first, not_last, place), (-1, back_z, at_last, not_last, not_first, last - place),
    )

    def pair_place(sign, k):
        return 2 * (1 - k % 2) if sign == 1 else 2 * (k % 2)

    def z_chain(state, *times):
        rows = state["rows"]

        def view(sign, k):
            from_block = (block + BLOCKS - sign * (1 + k // 2)) % BLOCKS
            return rows.at[core, pl.ds(row_at(from_block, pair_place(sign, k)), 2 * CAP)]

        for t in times:
            for sign, ahead, entry, inner, go, rank in directions:
                recv, send = state["relay"][sign]
                if t < CHAIN:
                    at = view(sign, t)
                    first = state["edge"][sign * (1 + t // 2)] + pair_place(sign, t)
                    start = copies.make(at, at, ahead, recv + t, send + t)
                    half_at = rows.at[core, pl.ds(row_at(0, 0), CAP)]
                    arrivals = [copies.make(half_at, half_at, mate, first + n, 0) for n in range(2)]

                    def enter(start=start, arrivals=arrivals):
                        for copy in arrivals:
                            copy.wait_recv()
                        start.start()

                    pl.when(entry)(enter)
                k = t - LAG * rank
                safe = jnp.clip(k, 0, CHAIN - 1)
                at = view(sign, safe)
                relay = copies.make(at, at, ahead, recv + safe, send + safe)

                def pass_on(relay=relay, go=go):
                    relay.wait_recv()
                    pl.when(go)(relay.start)

                pl.when(inner & (k >= 0) & (k < CHAIN))(pass_on)
                if t == CHAIN - 1 + LAG * last:
                    for n in range(CHAIN):
                        sent = copies.make(view(sign, n), view(sign, n), ahead, recv + n, send + n)
                        copies.started.append(Copy(sent, go))

    def z_share(state, j):
        at = state["rows"].at[core, pl.ds(row_at(chunk(j), 0), rows_b)]
        return copies.start(at, at, mate)

    def back_share(j):
        at = pl.ds(row_at(chunk(j), 0), rows_b)
        return copies.start(p3.at[1 - core, at], p_mate.at[at], mate)

    def back_sum(copy, j):
        at = pl.ds(row_at(chunk(j), 0), rows_b)
        copy.wait_recv()
        q3[at] = add16(p3[core, at], p_mate[at])

    def back_chain(state, *times):
        if not state:
            for sign in (1, -1):
                state[sign] = (copies.slots(CHAIN), copies.send_slots(CHAIN), copies.slots(2), copies.send_slots(2 * CHAIN))
        for t in times:
            for (sign, ahead, entry, inner, go, rank), buf, out in zip(directions, (zr, zl), (zs_r, zs_l)):
                recv, send, end, send_end = state[sign]
                k = t - LAG * rank
                safe = jnp.clip(k, 0, CHAIN - 1)
                step = 1 + safe // 2
                to_block = (block + BLOCKS + sign * step) % BLOCKS
                first = pair_place(-sign, safe)
                relay = copies.make(out.at[safe], buf.at[safe], ahead, recv + safe, send + safe)
                leaving = [
                    copies.make(
                        out.at[safe, pl.ds(n * CAP, CAP)], slots.at[pl.ds(block * CAP, CAP)],
                        ((to_block * LINE + first + n) * NX + x, dp), end + safe // 2, send_end + 2 * safe + n,
                    )
                    for n in range(2)
                ]

                def pass_on(
                    relay=relay, leaving=leaving, inner=inner, go=go, buf=buf, out=out, safe=safe,
                    at=pl.ds(row_at(to_block, first), 2 * CAP),
                ):
                    pl.when(inner)(relay.wait_recv)
                    out[safe] = add16(q3[at], buf[safe])
                    pl.when(go)(relay.start)

                    @pl.when(jnp.logical_not(go))
                    def _():
                        for copy in leaving:
                            copy.start()

                pl.when((k >= 0) & (k < CHAIN))(pass_on)
                if t == CHAIN - 1 + LAG * last:
                    for n in range(CHAIN):
                        sent = copies.make(out.at[n], buf.at[n], ahead, recv + n, send + n)
                        copies.started.append(Copy(sent, go))
                    for n in range(2 * CHAIN):
                        at = out.at[n // 2, pl.ds(0, CAP)]
                        sent = copies.make(at, at, ahead, end, send_end + n)
                        copies.started.append(Copy(sent, jnp.logical_not(go)))

    def back_chain_end(state):
        at = slots.at[pl.ds(0, CAP)]
        for sign in (1, -1):
            end = state[sign][2]
            for n, came in ((0, None), (1, place < 2 if sign == 1 else place >= 2)):
                guarded(came, copies.make(at, at, mate, end + n, 0).wait_recv)

    def back_own():
        for n in (3, 2, 1):
            for key, sign, ahead, buf, out in (("r", 1, front, own_r, own_sr), ("l", -1, back_z, own_l, own_sl)):
                target = place + sign * n
                valid = (target >= 0) & (target <= last)
                at = pl.ds(row_at(block, jnp.clip(target, 0, last)), CAP)
                behind = (place - sign >= 0) & (place - sign <= last)
                if n < last:
                    own_state[key + str(n + 1)].wait_recv(valid & behind)
                out[n - 1] = add16(q3[at], buf[n])
                own_state[key + str(n)] = copies.start(out.at[n - 1], buf.at[n - 1], ahead, valid)

    def back_own_end():
        own_state["r1"].wait_recv(not_first)
        own_state["l1"].wait_recv(not_last)
        slots[pl.ds(block * CAP, CAP)] = add16(q3[pl.ds(row_at(block, place), CAP)], own_r[0], own_l[0])

    own_state = {}

    def in_x(i):
        return w_in.at[y, i]

    def out_y(i):
        return w_out.at[x, i]

    def in_y(s):
        return lambda i: w_in.at[i, s]

    def out_x(s):
        return lambda i: w_out.at[i, s]

    def forward(i):
        pre = None
        for k in range(NY):
            term = lax.dot_general(
                x2[k], w_in[k, i], (((1,), (1,)), ((), ())), preferred_element_type=F32
            )
            pre = term if pre is None else pre + term
        pre = pre * scale_in
        square = pre * pre
        tangent = jnp.tanh(gelu_coef * (pre + cubic_coef * square * pre))
        hid[i] = (0.5 * pre * (1.0 + tangent)).astype(BF16).T
        pre_slope[i] = scale_out * (
            0.5 * (1.0 + tangent) + 0.5 * pre * (1.0 - tangent * tangent) * gelu_coef * (1.0 + 3.0 * cubic_coef * square)
        )

    def out_grads(i):
        for k in range(NY):
            d_out[i, k] = (jnp.dot(hid[i], g2[k], preferred_element_type=F32) * scale_out).astype(BF16)

    def hidden_grads(k, begin):
        for i in range(NX):
            term = lax.dot_general(
                g2[k], w_out[i, k], (((1,), (1,)), ((), ())), preferred_element_type=F32
            )
            grad_sum[i] = term if begin else grad_sum[i] + term

    def in_grads(k):
        for i in range(NX):
            d_in[k, i] = (jnp.dot(pg_t[i], x2[k], preferred_element_type=F32) * scale_in).astype(BF16)

    order = (0, 1, 3, 2)
    w_pair = [
        copies.start(w_stage.at[0], w_in.at[y, x, :, lanes_mine], mate),
        copies.start(w_stage.at[1], w_out.at[x, y, :, lanes_mine], mate),
    ]
    t_state = z_begin(pk_t, x3)
    attn_sent = {}
    for q in (2, 1, 3, 0):
        at = (y + q) % NY
        attn_sent[q] = copies.start(attn_ref.at[at, 1 - core], a_mate.at[at], mate)
    arrive(*w_pair)
    in_first = gather_first(in_x, X_RING)
    in_big, out_big, in_last, out_last = {}, {}, {}, {}
    out_big[0] = gather_first(out_x(y), X_RING)
    attn_ring = attn_begin(attn_sent)
    z_line(t_state, 1)
    z_chain(t_state, 0, 1)
    scatter_middle(attn_ring, lambda i: a_sum.at[i], n_tok, a_r1, a_m3, a_r3, Y_RING)
    in_big[0] = gather_first(in_y(x), Y_RING)
    out_first = gather_first(out_y, Y_RING)
    z_chain(t_state, 2, 3)
    z_line(t_state, 2)
    in_next = gather_next(in_first, in_x, X_RING)
    for q in (1, 3):
        in_big[q] = gather_first(in_y((x + q) % NX), Y_RING)
    z_chain(t_state, 4, 5)
    first, second = scatter_end(attn_ring, lambda i: a_sum.at[i], n_tok, a_r2, a_r3, Y_RING)
    summed = jnp.concatenate([first, second], axis=0)
    pack((gate_col * summed).astype(BF16), pk_g)
    g3[core, pl.ds(row_at(block, place), CAP)] = pk_g[pl.ds(block * CAP, CAP)]
    g_state = z_begin(pk_g, g3)
    z_line(t_state, 3)
    z_chain(t_state, 6, 7)
    arrive(*in_next)
    in_big[2] = gather_first(in_y((x + 2) % NX), Y_RING)
    out_next = gather_next(out_first, out_y, Y_RING)
    for q in (1, 3):
        out_big[q] = gather_first(out_x((y + q) % NY), X_RING)
    z_chain(t_state, 8)
    t_share = [z_share(t_state, j) for j in range(4)]
    z_line(g_state, 1)
    z_chain(g_state, 0, 1)
    to_wide(x3, x2, core)
    in_last[0] = gather_next(in_big[0], in_y(x), Y_RING)
    out_last[0] = gather_next(out_big[0], out_x(y), X_RING)
    z_chain(g_state, 2)
    z_line(g_state, 2)
    arrive(*t_share)
    to_wide(x3, x2, 1 - core)
    z_chain(g_state, 3, 4)
    arrive(*out_next)
    out_big[2] = gather_first(out_x((y + 2) % NY), X_RING)
    in_last[1] = gather_next(in_big[1], in_y((x + 1) % NX), Y_RING)
    in_last[3] = gather_next(in_big[3], in_y((x + 3) % NX), Y_RING)
    z_chain(g_state, 5)
    z_line(g_state, 3)
    arrive(*in_last[0])
    forward(x)
    z_chain(g_state, 6, 7)
    out_last[1] = gather_next(out_big[1], out_x((y + 1) % NY), X_RING)
    out_last[3] = gather_next(out_big[3], out_x((y + 3) % NY), X_RING)
    z_chain(g_state, 8)
    g_share = [z_share(g_state, j) for j in range(4)]
    to_wide(g3, g2, core)
    in_last[2] = gather_next(in_big[2], in_y((x + 2) % NX), Y_RING)
    out_last[2] = gather_next(out_big[2], out_x((y + 2) % NY), X_RING)
    arrive(*g_share)
    to_wide(g3, g2, 1 - core)
    out_grads(x)
    arrive(*out_last[0])
    hidden_grads(y, True)
    for q in (1, 3):
        arrive(*in_last[q])
        forward((x + q) % NX)
        out_grads((x + q) % NX)
        arrive(*out_last[q])
        hidden_grads((y + q) % NY, False)
    arrive(*in_last[2])
    forward((x + 2) % NX)
    out_grads((x + 2) % NX)
    out_ring = scatter_first(lambda i: d_out.at[i], NY, o_r1, o_r2, X_RING)
    arrive(*out_last[2])
    hidden_grads((y + 2) % NY, False)
    for i in range(NX):
        grad = (grad_sum[i] * pre_slope[i]).astype(BF16)
        pg[i] = grad
        pg_t[i] = grad.T
    for q in (2, 1, 3):
        in_grads((y + q) % NY)
    in_ring = scatter_first(lambda i: d_in.at[i], NX, i_r1, i_r2, Y_RING)

    back = {}
    for part_i in range(2):
        half = (1 - core) if part_i == 0 else core
        for k in range(NY):
            term = None
            for i in range(NX):
                add = jnp.dot(
                    pg[i, pl.ds(pl.multiple_of(half * rows_d, rows_d), rows_d)], w_in[k, i],
                    preferred_element_type=F32,
                )
                term = add if term is None else term + add
            p2[k] = (term * scale_in).astype(BF16)
        to_narrow(p2, p3, half)
        if part_i == 0:
            for j in order:
                back[j] = back_share(j)
            scatter_middle(out_ring, lambda i: d_out.at[i], NY, o_r1, o_m3, o_r3, X_RING)
    for j in order:
        back_sum(back[j], j)
    ends = {}
    back_chain(ends, 0)
    back_own()
    back_chain(ends, 1, 2)
    in_grads(y)
    back_chain(ends, 3, 4)
    scatter_middle(in_ring, lambda i: d_in.at[i], NX, i_r1, i_m3, i_r3, Y_RING)
    back_chain(ends, 5, 6, 7, 8)
    back_own_end()

    first, second = scatter_end(out_ring, lambda i: d_out.at[i], NY, o_r2, o_r3, X_RING)
    o_sum[0:2] = first.astype(BF16)
    o_sum[2:4] = second.astype(BF16)
    out_small = scatter_first(lambda i: o_sum.at[i], share, os_r1, os_r2, Y_RING)
    first, second = scatter_end(in_ring, lambda i: d_in.at[i], NX, i_r2, i_r3, Y_RING)
    i_sum[0:2] = first.astype(BF16)
    i_sum[2:4] = second.astype(BF16)
    in_small = scatter_first(lambda i: i_sum.at[i], share, is_r1, is_r2, X_RING)
    scatter_middle(out_small, lambda i: o_sum.at[i], share, os_r1, os_m3, os_r3, Y_RING)
    scatter_middle(in_small, lambda i: i_sum.at[i], share, is_r1, is_m3, is_r3, X_RING)
    pair = []
    for t, sent, sums, buf2, buf3, ring in (
        (1, out_small, o_sum, os_r2, os_r3, Y_RING), (0, in_small, i_sum, is_r2, is_r3, X_RING),
    ):
        low, high = halves(share)
        first, second = scatter_end(sent, lambda i: sums.at[i], share, buf2, buf3, ring)
        d_part[t, low] = first.astype(BF16)
        d_part[t, high] = second.astype(BF16)
        pair.append(copies.start(d_part.at[t, :, lanes_other], d_other.at[t], mate))

    back_chain_end(ends)
    wide = []
    for g in range(n_slot // 16):
        moved = jnp.dot(
            perm[...], slots[g * 16:(g + 1) * 16].reshape(256, LANES), preferred_element_type=F32
        ).astype(BF16)
        wide.append(jnp.concatenate([moved[k * 16:(k + 1) * 16] for k in range(tiles)], axis=1))
    slots_wide = jnp.concatenate(wide, axis=0)
    tg_ref[...] = lax.dot_general(
        disp[...], slots_wide, (((0,), (0,)), ((), ())), preferred_element_type=F32
    ).astype(BF16)

    for t, copy, old, new in ((1, pair[0], wout_ref, nwout_ref), (0, pair[1], win_ref, nwin_ref)):
        new[mine] = old[mine] - step_rate * d_part[t, :, lanes_mine].astype(F32)
        copy.wait_recv()
        new[other] = old[other] - step_rate * d_other[t].astype(F32)
    copies.finish()


def shards(tokens, attn_partials, expert_ids, gate, w_in, w_out):
    n_tok, width = tokens.shape
    w_in_t, w_out_t = w_in.T, w_out.T
    hidden = w_in_t.shape[0]
    tiles = width // LANES
    rows_b = LINE * CAP
    rows_d = BLOCKS * rows_b
    share = hidden // 2
    depth = width // NY
    slot_rows = 48
    vmem = pl.BlockSpec(memory_space=pltpu.VMEM)

    def bf16(*shape):
        return pltpu.VMEM(shape, BF16)

    def rows16(*lead):
        return bf16(*lead, tiles, LANES)

    scratch = [
        rows16(slot_rows), rows16(slot_rows), rows16(2, rows_d), rows16(2, rows_d),
        bf16(NY, 2 * rows_d, depth), bf16(NY, 2 * rows_d, depth),
        bf16(256, 256), bf16(slot_rows, n_tok),
        bf16(2, share, depth // 2), bf16(NY, NX, share, depth), bf16(NX, NY, share, depth),
        pltpu.VMEM((NX, 2 * rows_d, share), F32), pltpu.VMEM((NX, 2 * rows_d, share), F32),
        bf16(NX, 2 * rows_d, share), bf16(NX, share, 2 * rows_d), bf16(NX, share, 2 * rows_d),
        bf16(NY, rows_d, depth), rows16(2, rows_d), rows16(rows_d),
        rows16(rows_d), rows16(CHAIN, 2 * CAP), rows16(CHAIN, 2 * CAP), rows16(CHAIN, 2 * CAP), rows16(CHAIN, 2 * CAP),
        rows16(LINE, CAP), rows16(LINE, CAP), rows16(LINE, CAP), rows16(LINE, CAP), rows16(slot_rows),
        bf16(NY, n_tok, width), bf16(NY, n_tok, width),
    ]
    scratch += [bf16(2, n_tok // 2, width)] * 4
    for _ in range(2):
        scratch += [bf16(4, 4, share, depth)] + [bf16(2, 2, share, depth)] * 4
        scratch += [bf16(4, share, depth)] + [bf16(2, share // 2, depth)] * 4
    scratch += [bf16(2, share, depth), bf16(2, share, depth // 2)]
    scratch += [pltpu.SemaphoreType.DMA((N_COPIES,)), pltpu.SemaphoreType.DMA((N_COPIES,))]
    token_grad, new_in, new_out = pl.pallas_call(
        functools.partial(kernel, (width, hidden)),
        out_shape=(
            jax.ShapeDtypeStruct((n_tok, width), BF16),
            jax.ShapeDtypeStruct(w_in_t.shape, F32),
            jax.ShapeDtypeStruct(w_out_t.shape, F32),
        ),
        in_specs=[vmem] * 6,
        out_specs=(vmem, vmem, vmem),
        scratch_shapes=scratch,
        compiler_params=pltpu.CompilerParams(
            collective_id=0, has_side_effects=True, vmem_limit_bytes=60 * 1024 * 1024
        ),
    )(
        tokens,
        attn_partials.reshape(NY, 2, n_tok, width),
        expert_ids.reshape(1, n_tok),
        gate.reshape(1, n_tok),
        w_in_t,
        w_out_t,
    )
    return token_grad, new_in.T, new_out.T


def solution(mesh):
    in_specs = (
        P(("expert", "dp"), None),
        P("dp", "expert", None),
        P(("expert", "dp")),
        P(("expert", "dp")),
        P("dp", "expert"),
        P("dp", "expert"),
    )
    out_specs = (P(("expert", "dp"), None), P("dp", "expert"), P("dp", "expert"))
    return jax.shard_map(shards, mesh=mesh, in_specs=in_specs, out_specs=out_specs, check_vma=False)
```

```python
import functools

import jax
import jax.numpy as jnp
from jax import lax
from jax.experimental import pallas as pl
from jax.experimental.pallas import tpu as pltpu
from jax.sharding import PartitionSpec as P

NX = 4
NY = 4
LINE = 4
BLOCKS = 4
CAP = 10
LANES = 128
MESH = pl.DeviceIdType.MESH

gelu_coef = 0.7978845608028654
cubic_coef = 0.044715
step_rate = 0.5
F32 = jnp.float32
BF16 = jnp.bfloat16


def add16(*terms):
    total = terms[0].astype(F32)
    for term in terms[1:]:
        total = total + term.astype(F32)
    return total.astype(BF16)


class Copy:
    def __init__(self, copy, when):
        self.copy = copy
        self.when = when

    def wait_recv(self, when=None):
        guarded(when, self.copy.wait_recv)


def guarded(when, action):
    if when is None:
        action()
    else:
        pl.when(when)(action)


class Copies:
    def __init__(self, send_sems, recv_sems):
        self.send_sems = send_sems
        self.recv_sems = recv_sems
        self.sends = 0
        self.recvs = 0
        self.started = []

    def slots(self, count):
        first = self.recvs
        self.recvs += count
        return first

    def send_slots(self, count):
        first = self.sends
        self.sends += count
        return first

    def make(self, src, dst, device, recv=None, send=None):
        if recv is None:
            recv = self.slots(1)
        if send is None:
            send = self.sends
            self.sends += 1
        return pltpu.make_async_remote_copy(
            src_ref=src,
            dst_ref=dst,
            send_sem=self.send_sems.at[send],
            recv_sem=self.recv_sems.at[recv],
            device_id=device,
            device_id_type=MESH,
        )

    def start(self, src, dst, device, when=None, recv=None):
        copy = Copy(self.make(src, dst, device, recv), when)
        guarded(when, copy.copy.start)
        self.started.append(copy)
        return copy

    def finish(self):
        for copy in self.started:
            guarded(copy.when, copy.copy.wait_send)


N_COPIES = 384
CHAIN = 3
LAG = 2


def kernel(
    dims,
    tok_ref, attn_ref, ids_ref, gate_ref, win_ref, wout_ref,
    tg_ref, nwin_ref, nwout_ref,
    pk_t, pk_g, x3, g3, x2, g2, perm, disp,
    w_stage, w_in, w_out, pre_slope, grad_sum, pg, pg_t, hid, p2, p3, p_mate,
    q3, zr, zl, zs_r, zs_l, own_r, own_l, own_sr, own_sl, slots,
    a_mate, a_sum, a_r1, a_m3, a_r3, a_r2,
    d_in, i_r1, i_m3, i_r3, i_r2, i_sum, is_r1, is_m3, is_r3, is_r2,
    d_out, o_r1, o_m3, o_r3, o_r2, o_sum, os_r1, os_m3, os_r3, os_r2,
    d_part, d_other,
    send_sems, recv_sems, reach_sems,
):
    width, hidden = dims
    scale_in = width ** (-0.5)
    scale_out = (hidden * NX * LINE) ** (-0.5)
    tiles = width // LANES
    share = hidden // 2
    depth = width // NY
    expert = lax.axis_index("expert")
    dp = lax.axis_index("dp")
    z = expert // NX
    x = expert % NX
    block = z // LINE
    place = z % LINE
    y = dp // 2
    core = dp % 2
    rows_b = LINE * CAP
    rows_d = BLOCKS * rows_b

    right = (z * NX + (x + 1) % NX, dp)
    left = (z * NX + (x + NX - 1) % NX, dp)
    up = (expert, ((y + 1) % NY) * 2 + core)
    down = (expert, ((y + NY - 1) % NY) * 2 + core)
    mate = (expert, y * 2 + (1 - core))

    last = LINE - 1
    not_first, not_last = place > 0, place < last
    at_first, at_last = place == 0, place == last
    front = ((z + 1) % (BLOCKS * LINE) * NX + x, dp)
    back_z = ((z + BLOCKS * LINE - 1) % (BLOCKS * LINE) * NX + x, dp)

    def seat(step, at):
        return ((((block + step + BLOCKS) % BLOCKS) * LINE + at) * NX + x, dp)

    def z_step(step):
        return ((z + step + BLOCKS * LINE) % (BLOCKS * LINE) * NX + x, dp)

    barrier = pltpu.get_barrier_semaphore()
    near = (right, left, up, down, mate, front, back_z)
    for device in near:
        pl.semaphore_signal(barrier, inc=1, device_id=device, device_id_type=MESH)

    def reach(round_index):
        for step in ((1, -1), (2, -2), (4, -4))[round_index]:
            pl.semaphore_signal(
                reach_sems.at[round_index], inc=1, device_id=z_step(step), device_id_type=MESH
            )

    def reached(round_index):
        pl.semaphore_wait(reach_sems.at[round_index], 2)

    copies = Copies(send_sems, recv_sems)

    def arrive(*waiting):
        for copy in waiting:
            copy.wait_recv()

    n_tok = tok_ref.shape[0]

    def pack(rows, dst):
        n_slot = disp.shape[0]
        packed = jnp.dot(disp[...], rows, preferred_element_type=F32).astype(BF16)
        for g in range(n_slot // 16):
            stacked = jnp.concatenate(
                [packed[g * 16:(g + 1) * 16, k * LANES:(k + 1) * LANES] for k in range(tiles)], axis=0
            )
            moved = jnp.dot(perm[...], stacked, preferred_element_type=F32).astype(BF16)
            dst[g * 16:(g + 1) * 16] = moved.reshape(16, tiles, LANES)

    per = depth // LANES

    def to_wide(src, dst, half):
        def body(i, carry):
            pair = [src[half, pl.ds(i * 32 + h * 16, 16)].reshape(256, LANES) for h in range(2)]
            moved = jnp.dot(perm[...], jnp.concatenate(pair, axis=1), preferred_element_type=F32).astype(BF16)
            for h in range(2):
                at = pl.ds(pl.multiple_of(half * rows_d + i * 32 + h * 16, 16), 16)
                for k in range(tiles):
                    dst[k // per, at, (k % per) * LANES:(k % per + 1) * LANES] = moved[
                        k * 16:(k + 1) * 16, h * LANES:(h + 1) * LANES
                    ]
            return carry

        lax.fori_loop(0, rows_d // 32, body, 0)

    def to_narrow(src, dst, half):
        def body(i, carry):
            pair = []
            for h in range(2):
                at = pl.ds(pl.multiple_of(i * 32 + h * 16, 16), 16)
                pair.append(jnp.concatenate(
                    [src[k // per, at, (k % per) * LANES:(k % per + 1) * LANES] for k in range(tiles)], axis=0
                ))
            moved = jnp.dot(perm[...], jnp.concatenate(pair, axis=1), preferred_element_type=F32).astype(BF16)
            for h in range(2):
                dst[half, pl.ds(i * 32 + h * 16, 16)] = moved[:, h * LANES:(h + 1) * LANES].reshape(16, tiles, LANES)
            return carry

        lax.fori_loop(0, rows_d // 32, body, 0)

    def row_at(c, p):
        return c * rows_b + p * CAP

    mine = pl.ds(pl.multiple_of(core * share, share), share)
    other = pl.ds(pl.multiple_of((1 - core) * share, share), share)
    lanes_mine = pl.ds(pl.multiple_of(core * (depth // 2), depth // 2), depth // 2)
    lanes_other = pl.ds(pl.multiple_of((1 - core) * (depth // 2), depth // 2), depth // 2)
    w_in[y, x, :, lanes_mine] = win_ref[mine].astype(BF16)
    w_out[x, y, :, lanes_mine] = wout_ref[mine].astype(BF16)
    w_stage[0] = win_ref[other].astype(BF16)
    w_stage[1] = wout_ref[other].astype(BF16)
    pl.semaphore_wait(barrier, len(near))
    reach(0)

    def halves(count):
        return pl.ds(0, count // 2), pl.ds(count // 2, count // 2)

    X_RING = (x, right, left)
    Y_RING = (y, up, down)

    def gather_first(blk, ring):
        pos, upper, lower = ring
        return [copies.start(blk(pos), blk(pos), device) for device in (upper, lower)]

    def gather_next(sent, blk, ring):
        pos, upper, lower = ring
        low, high = halves(share)
        below, above = (pos + 3) % 4, (pos + 1) % 4
        sent[0].wait_recv()
        to_up = copies.start(blk(below).at[low], blk(below).at[low], upper)
        sent[1].wait_recv()
        to_down = copies.start(blk(above).at[high], blk(above).at[high], lower)
        return [to_up, to_down]

    def scatter_first(blk, count, buf1, buf2, ring):
        pos, upper, lower = ring
        low, high = halves(count)
        far, above, below = (pos + 2) % 4, (pos + 1) % 4, (pos + 3) % 4
        return {
            "u1": copies.start(blk(far).at[low], buf1.at[0], upper),
            "d1": copies.start(blk(far).at[high], buf1.at[1], lower),
            "u2": copies.start(blk(above).at[high], buf2.at[0], upper),
            "d2": copies.start(blk(below).at[low], buf2.at[1], lower),
        }

    def scatter_middle(sent, blk, count, buf1, mid, buf3, ring):
        pos, upper, lower = ring
        low, high = halves(count)
        sent["u1"].wait_recv()
        mid[0] = add16(buf1[0], blk((pos + 1) % 4).at[low][...])
        sent["u3"] = copies.start(mid.at[0], buf3.at[0], upper)
        sent["d1"].wait_recv()
        mid[1] = add16(buf1[1], blk((pos + 3) % 4).at[high][...])
        sent["d3"] = copies.start(mid.at[1], buf3.at[1], lower)

    def scatter_end(sent, blk, count, buf2, buf3, ring):
        low, high = halves(count)
        pos = ring[0]
        arrive(sent["d2"], sent["u3"])
        first = blk(pos).at[low][...].astype(F32) + buf2[1].astype(F32) + buf3[0].astype(F32)
        arrive(sent["u2"], sent["d3"])
        second = blk(pos).at[high][...].astype(F32) + buf2[0].astype(F32) + buf3[1].astype(F32)
        return first, second

    def attn_begin(sent):
        low, high = halves(n_tok)
        out = {}
        for q in (2, 1, 3, 0):
            at = (y + q) % NY
            sent[q].wait_recv()
            a_sum[at] = add16(attn_ref[at, core], a_mate[at])
            if q == 2:
                out["u1"] = copies.start(a_sum.at[at, low], a_r1.at[0], up)
                out["d1"] = copies.start(a_sum.at[at, high], a_r1.at[1], down)
            elif q == 1:
                out["u2"] = copies.start(a_sum.at[at, high], a_r2.at[0], up)
            elif q == 3:
                out["d2"] = copies.start(a_sum.at[at, low], a_r2.at[1], down)
        return out

    def chunk(j):
        return (block + BLOCKS + j) % BLOCKS

    def z_begin(packed, rows):
        here = pl.ds(row_at(block, place), CAP)
        mine_at = pl.ds(block * CAP, CAP)
        state = {"rows": rows, "edge": {}, "relay": {}}
        state["r1"] = copies.start(packed.at[mine_at], rows.at[core, here], front, not_last)
        state["l1"] = copies.start(packed.at[mine_at], rows.at[core, here], back_z, not_first)
        for step in (1, 2):
            for sign in (1, -1):
                first = copies.slots(LINE)
                sends = None if step == 1 else (place >= 2 if sign == 1 else place < 2)
                copies.start(
                    packed.at[pl.ds(chunk(sign * step) * CAP, CAP)], rows.at[core, here],
                    seat(sign * step, 0 if sign == 1 else last), sends, recv=first + place,
                )
                state["edge"][sign * step] = first
        for sign in (1, -1):
            state["relay"][sign] = (copies.slots(CHAIN), copies.send_slots(CHAIN))
        return state

    def z_line(state, n):
        rows = state["rows"]
        for key, sign, ahead, came, go in (("r", 1, front, place >= n, not_last), ("l", -1, back_z, place + n <= last, not_first)):
            state[key + str(n)].wait_recv(came)
            if n < last:
                at = pl.ds(row_at(block, jnp.clip(place - sign * n, 0, last)), CAP)
                state[key + str(n + 1)] = copies.start(rows.at[core, at], rows.at[core, at], ahead, came & go)

    directions = (
        (1, front, at_first, not_first, not_last, place), (-1, back_z, at_last, not_last, not_first, last - place),
    )

    def pair_place(sign, k):
        return 2 * (1 - k % 2) if sign == 1 else 2 * (k % 2)

    def z_chain(state, *times):
        rows = state["rows"]

        def view(sign, k):
            from_block = (block + BLOCKS - sign * (1 + k // 2)) % BLOCKS
            return rows.at[core, pl.ds(row_at(from_block, pair_place(sign, k)), 2 * CAP)]

        for t in times:
            for sign, ahead, entry, inner, go, rank in directions:
                recv, send = state["relay"][sign]
                if t < CHAIN:
                    at = view(sign, t)
                    first = state["edge"][sign * (1 + t // 2)] + pair_place(sign, t)
                    start = copies.make(at, at, ahead, recv + t, send + t)
                    half_at = rows.at[core, pl.ds(row_at(0, 0), CAP)]
                    arrivals = [copies.make(half_at, half_at, mate, first + n, 0) for n in range(2)]

                    def enter(start=start, arrivals=arrivals):
                        for copy in arrivals:
                            copy.wait_recv()
                        start.start()

                    pl.when(entry)(enter)
                k = t - LAG * rank
                safe = jnp.clip(k, 0, CHAIN - 1)
                at = view(sign, safe)
                relay = copies.make(at, at, ahead, recv + safe, send + safe)

                def pass_on(relay=relay, go=go):
                    relay.wait_recv()
                    pl.when(go)(relay.start)

                pl.when(inner & (k >= 0) & (k < CHAIN))(pass_on)
                if t == CHAIN - 1 + LAG * last:
                    for n in range(CHAIN):
                        sent = copies.make(view(sign, n), view(sign, n), ahead, recv + n, send + n)
                        copies.started.append(Copy(sent, go))

    def z_share(state, j):
        at = state["rows"].at[core, pl.ds(row_at(chunk(j), 0), rows_b)]
        return copies.start(at, at, mate)

    def back_share(j):
        at = pl.ds(row_at(chunk(j), 0), rows_b)
        return copies.start(p3.at[1 - core, at], p_mate.at[at], mate)

    def back_sum(copy, j):
        at = pl.ds(row_at(chunk(j), 0), rows_b)
        copy.wait_recv()
        q3[at] = add16(p3[core, at], p_mate[at])

    def back_chain(state, *times):
        if not state:
            for sign in (1, -1):
                state[sign] = (copies.slots(CHAIN), copies.send_slots(CHAIN), copies.slots(2), copies.send_slots(2 * CHAIN))
        for t in times:
            for (sign, ahead, entry, inner, go, rank), buf, out in zip(directions, (zr, zl), (zs_r, zs_l)):
                recv, send, end, send_end = state[sign]
                k = t - LAG * rank
                safe = jnp.clip(k, 0, CHAIN - 1)
                step = 1 + safe // 2
                to_block = (block + BLOCKS + sign * step) % BLOCKS
                first = pair_place(-sign, safe)
                relay = copies.make(out.at[safe], buf.at[safe], ahead, recv + safe, send + safe)
                leaving = [
                    copies.make(
                        out.at[safe, pl.ds(n * CAP, CAP)], slots.at[pl.ds(block * CAP, CAP)],
                        ((to_block * LINE + first + n) * NX + x, dp), end + safe // 2, send_end + 2 * safe + n,
                    )
                    for n in range(2)
                ]

                def pass_on(
                    relay=relay, leaving=leaving, inner=inner, go=go, buf=buf, out=out, safe=safe,
                    at=pl.ds(row_at(to_block, first), 2 * CAP),
                ):
                    pl.when(inner)(relay.wait_recv)
                    out[safe] = add16(q3[at], buf[safe])
                    pl.when(go)(relay.start)

                    @pl.when(jnp.logical_not(go))
                    def _():
                        for copy in leaving:
                            copy.start()

                pl.when((k >= 0) & (k < CHAIN))(pass_on)
                if t == CHAIN - 1 + LAG * last:
                    for n in range(CHAIN):
                        sent = copies.make(out.at[n], buf.at[n], ahead, recv + n, send + n)
                        copies.started.append(Copy(sent, go))
                    for n in range(2 * CHAIN):
                        at = out.at[n // 2, pl.ds(0, CAP)]
                        sent = copies.make(at, at, ahead, end, send_end + n)
                        copies.started.append(Copy(sent, jnp.logical_not(go)))

    def back_chain_end(state):
        at = slots.at[pl.ds(0, CAP)]
        for sign in (1, -1):
            end = state[sign][2]
            for n, came in ((0, None), (1, place < 2 if sign == 1 else place >= 2)):
                guarded(came, copies.make(at, at, mate, end + n, 0).wait_recv)

    def back_own():
        for n in (3, 2, 1):
            for key, sign, ahead, buf, out in (("r", 1, front, own_r, own_sr), ("l", -1, back_z, own_l, own_sl)):
                target = place + sign * n
                valid = (target >= 0) & (target <= last)
                at = pl.ds(row_at(block, jnp.clip(target, 0, last)), CAP)
                behind = (place - sign >= 0) & (place - sign <= last)
                if n < last:
                    own_state[key + str(n + 1)].wait_recv(valid & behind)
                out[n - 1] = add16(q3[at], buf[n])
                own_state[key + str(n)] = copies.start(out.at[n - 1], buf.at[n - 1], ahead, valid)

    def back_own_end():
        own_state["r1"].wait_recv(not_first)
        own_state["l1"].wait_recv(not_last)
        slots[pl.ds(block * CAP, CAP)] = add16(q3[pl.ds(row_at(block, place), CAP)], own_r[0], own_l[0])

    own_state = {}

    def in_x(i):
        return w_in.at[y, i]

    def out_y(i):
        return w_out.at[x, i]

    def in_y(s):
        return lambda i: w_in.at[i, s]

    def out_x(s):
        return lambda i: w_out.at[i, s]

    def forward(i):
        pre = None
        for k in range(NY):
            term = lax.dot_general(
                x2[k], w_in[k, i], (((1,), (1,)), ((), ())), preferred_element_type=F32
            )
            pre = term if pre is None else pre + term
        pre = pre * scale_in
        square = pre * pre
        tangent = jnp.tanh(gelu_coef * (pre + cubic_coef * square * pre))
        hid[i] = (0.5 * pre * (1.0 + tangent)).astype(BF16).T
        pre_slope[i] = scale_out * (
            0.5 * (1.0 + tangent) + 0.5 * pre * (1.0 - tangent * tangent) * gelu_coef * (1.0 + 3.0 * cubic_coef * square)
        )

    def out_grads(i):
        for k in range(NY):
            d_out[i, k] = (jnp.dot(hid[i], g2[k], preferred_element_type=F32) * scale_out).astype(BF16)

    def hidden_grads(k, begin):
        for i in range(NX):
            term = lax.dot_general(
                g2[k], w_out[i, k], (((1,), (1,)), ((), ())), preferred_element_type=F32
            )
            grad_sum[i] = term if begin else grad_sum[i] + term

    def in_grads(k):
        for i in range(NX):
            d_in[k, i] = (jnp.dot(pg_t[i], x2[k], preferred_element_type=F32) * scale_in).astype(BF16)

    order = (0, 1, 3, 2)
    w_pair = [
        copies.start(w_stage.at[0], w_in.at[y, x, :, lanes_mine], mate),
        copies.start(w_stage.at[1], w_out.at[x, y, :, lanes_mine], mate),
    ]
    attn_sent = {}
    for q in (2, 1, 3, 0):
        at = (y + q) % NY
        attn_sent[q] = copies.start(attn_ref.at[at, 1 - core], a_mate.at[at], mate)
    reached(0)
    reach(1)
    row_i = lax.broadcasted_iota(jnp.int32, (256, 256), 0)
    col_i = lax.broadcasted_iota(jnp.int32, (256, 256), 1)
    perm[...] = jnp.where(col_i == (row_i % 16) * 16 + row_i // 16, 1.0, 0.0).astype(BF16)

    ids_row = ids_ref[...].astype(F32)
    eye_t = lax.broadcasted_iota(jnp.int32, (n_tok, n_tok), 0)
    eye_s = lax.broadcasted_iota(jnp.int32, (n_tok, n_tok), 1)
    spread_ids = jnp.broadcast_to(ids_row, (n_tok, n_tok))
    ids_col = jnp.sum(jnp.where(eye_t == eye_s, spread_ids, 0.0), axis=1, keepdims=True)
    earlier = jnp.where((ids_col == spread_ids) & (eye_t < eye_s), 1.0, 0.0)
    rank_row = jnp.sum(earlier, axis=0, keepdims=True)
    slot_row = jnp.where(rank_row < CAP, ids_row * CAP + rank_row, -1.0)
    n_slot = disp.shape[0]
    slot_i = lax.broadcasted_iota(jnp.int32, (n_slot, n_tok), 0).astype(F32)
    disp[...] = jnp.where(slot_i == jnp.broadcast_to(slot_row, (n_slot, n_tok)), 1.0, 0.0).astype(BF16)
    gate_col = jnp.sum(
        jnp.where(eye_t == eye_s, jnp.broadcast_to(gate_ref[...], (n_tok, n_tok)), 0.0),
        axis=1, keepdims=True,
    )

    reached(1)
    reach(2)
    arrive(*w_pair)
    in_first = gather_first(in_x, X_RING)
    in_big, out_big, in_last, out_last = {}, {}, {}, {}
    out_big[0] = gather_first(out_x(y), X_RING)
    pack(tok_ref[...], pk_t)
    x3[core, pl.ds(row_at(block, place), CAP)] = pk_t[pl.ds(block * CAP, CAP)]
    reached(2)
    t_state = z_begin(pk_t, x3)
    attn_ring = attn_begin(attn_sent)
    @pl.when(at_first)
    def _():
        zr[...] = jnp.zeros_like(zr)
        own_r[...] = jnp.zeros_like(own_r)

    @pl.when(at_last)
    def _():
        zl[...] = jnp.zeros_like(zl)
        own_l[...] = jnp.zeros_like(own_l)

    slots[BLOCKS * CAP:] = jnp.zeros((slots.shape[0] - BLOCKS * CAP, tiles, LANES), BF16)

    z_line(t_state, 1)
    z_chain(t_state, 0, 1)
    scatter_middle(attn_ring, lambda i: a_sum.at[i], n_tok, a_r1, a_m3, a_r3, Y_RING)
    in_big[0] = gather_first(in_y(x), Y_RING)
    out_first = gather_first(out_y, Y_RING)
    z_chain(t_state, 2, 3)
    z_line(t_state, 2)
    in_next = gather_next(in_first, in_x, X_RING)
    for q in (1, 3):
        in_big[q] = gather_first(in_y((x + q) % NX), Y_RING)
    z_chain(t_state, 4, 5)
    first, second = scatter_end(attn_ring, lambda i: a_sum.at[i], n_tok, a_r2, a_r3, Y_RING)
    summed = jnp.concatenate([first, second], axis=0)
    pack((gate_col * summed).astype(BF16), pk_g)
    g3[core, pl.ds(row_at(block, place), CAP)] = pk_g[pl.ds(block * CAP, CAP)]
    g_state = z_begin(pk_g, g3)
    z_line(t_state, 3)
    z_chain(t_state, 6, 7)
    arrive(*in_next)
    in_big[2] = gather_first(in_y((x + 2) % NX), Y_RING)
    out_next = gather_next(out_first, out_y, Y_RING)
    for q in (1, 3):
        out_big[q] = gather_first(out_x((y + q) % NY), X_RING)
    z_chain(t_state, 8)
    t_share = [z_share(t_state, j) for j in range(4)]
    z_line(g_state, 1)
    z_chain(g_state, 0, 1)
    to_wide(x3, x2, core)
    in_last[0] = gather_next(in_big[0], in_y(x), Y_RING)
    out_last[0] = gather_next(out_big[0], out_x(y), X_RING)
    z_chain(g_state, 2)
    z_line(g_state, 2)
    arrive(*t_share)
    to_wide(x3, x2, 1 - core)
    z_chain(g_state, 3, 4)
    arrive(*out_next)
    out_big[2] = gather_first(out_x((y + 2) % NY), X_RING)
    in_last[1] = gather_next(in_big[1], in_y((x + 1) % NX), Y_RING)
    in_last[3] = gather_next(in_big[3], in_y((x + 3) % NX), Y_RING)
    z_chain(g_state, 5)
    z_line(g_state, 3)
    arrive(*in_last[0])
    forward(x)
    z_chain(g_state, 6, 7)
    out_last[1] = gather_next(out_big[1], out_x((y + 1) % NY), X_RING)
    out_last[3] = gather_next(out_big[3], out_x((y + 3) % NY), X_RING)
    arrive(*in_last[1], *in_last[3])
    z_chain(g_state, 8)
    g_share = [z_share(g_state, j) for j in range(4)]
    in_last[2] = gather_next(in_big[2], in_y((x + 2) % NX), Y_RING)
    out_last[2] = gather_next(out_big[2], out_x((y + 2) % NY), X_RING)
    forward((x + 1) % NX)
    forward((x + 3) % NX)
    to_wide(g3, g2, core)
    arrive(*g_share)
    to_wide(g3, g2, 1 - core)
    out_grads(x)
    arrive(*out_last[0])
    hidden_grads(y, True)
    for q in (1, 3):
        out_grads((x + q) % NX)
        arrive(*out_last[q])
        hidden_grads((y + q) % NY, False)
    arrive(*in_last[2])
    forward((x + 2) % NX)
    out_grads((x + 2) % NX)
    out_ring = scatter_first(lambda i: d_out.at[i], NY, o_r1, o_r2, X_RING)
    arrive(*out_last[2])
    hidden_grads((y + 2) % NY, False)
    for i in range(NX):
        grad = (grad_sum[i] * pre_slope[i]).astype(BF16)
        pg[i] = grad
        pg_t[i] = grad.T
    for q in (2, 1, 3):
        in_grads((y + q) % NY)
    in_ring = scatter_first(lambda i: d_in.at[i], NX, i_r1, i_r2, Y_RING)

    back = {}
    for part_i in range(2):
        half = (1 - core) if part_i == 0 else core
        for k in range(NY):
            term = None
            for i in range(NX):
                add = jnp.dot(
                    pg[i, pl.ds(pl.multiple_of(half * rows_d, rows_d), rows_d)], w_in[k, i],
                    preferred_element_type=F32,
                )
                term = add if term is None else term + add
            p2[k] = (term * scale_in).astype(BF16)
        to_narrow(p2, p3, half)
        if part_i == 0:
            for j in order:
                back[j] = back_share(j)
            scatter_middle(out_ring, lambda i: d_out.at[i], NY, o_r1, o_m3, o_r3, X_RING)
    for j in order:
        back_sum(back[j], j)
    ends = {}
    back_chain(ends, 0)
    back_own()
    back_chain(ends, 1, 2)
    in_grads(y)
    back_chain(ends, 3, 4)
    scatter_middle(in_ring, lambda i: d_in.at[i], NX, i_r1, i_m3, i_r3, Y_RING)
    back_chain(ends, 5, 6, 7, 8)
    back_own_end()

    first, second = scatter_end(out_ring, lambda i: d_out.at[i], NY, o_r2, o_r3, X_RING)
    o_sum[0:2] = first.astype(BF16)
    o_sum[2:4] = second.astype(BF16)
    out_small = scatter_first(lambda i: o_sum.at[i], share, os_r1, os_r2, Y_RING)
    first, second = scatter_end(in_ring, lambda i: d_in.at[i], NX, i_r2, i_r3, Y_RING)
    i_sum[0:2] = first.astype(BF16)
    i_sum[2:4] = second.astype(BF16)
    in_small = scatter_first(lambda i: i_sum.at[i], share, is_r1, is_r2, X_RING)
    scatter_middle(out_small, lambda i: o_sum.at[i], share, os_r1, os_m3, os_r3, Y_RING)
    scatter_middle(in_small, lambda i: i_sum.at[i], share, is_r1, is_m3, is_r3, X_RING)
    pair = []
    for t, sent, sums, buf2, buf3, ring in (
        (1, out_small, o_sum, os_r2, os_r3, Y_RING), (0, in_small, i_sum, is_r2, is_r3, X_RING),
    ):
        low, high = halves(share)
        first, second = scatter_end(sent, lambda i: sums.at[i], share, buf2, buf3, ring)
        d_part[t, low] = first.astype(BF16)
        d_part[t, high] = second.astype(BF16)
        pair.append(copies.start(d_part.at[t, :, lanes_other], d_other.at[t], mate))

    back_chain_end(ends)
    wide = []
    for g in range(n_slot // 16):
        moved = jnp.dot(
            perm[...], slots[g * 16:(g + 1) * 16].reshape(256, LANES), preferred_element_type=F32
        ).astype(BF16)
        wide.append(jnp.concatenate([moved[k * 16:(k + 1) * 16] for k in range(tiles)], axis=1))
    slots_wide = jnp.concatenate(wide, axis=0)
    tg_ref[...] = lax.dot_general(
        disp[...], slots_wide, (((0,), (0,)), ((), ())), preferred_element_type=F32
    ).astype(BF16)

    for t, copy, old, new in ((1, pair[0], wout_ref, nwout_ref), (0, pair[1], win_ref, nwin_ref)):
        new[mine] = old[mine] - step_rate * d_part[t, :, lanes_mine].astype(F32)
        copy.wait_recv()
        new[other] = old[other] - step_rate * d_other[t].astype(F32)
    copies.finish()


def hand_over(*refs):
    for source, target in zip(refs[:3], refs[3:]):
        target[...] = source[...]


def shards(tokens, attn_partials, expert_ids, gate, w_in, w_out):
    n_tok, width = tokens.shape
    w_in_t, w_out_t = w_in.T, w_out.T
    hidden = w_in_t.shape[0]
    tiles = width // LANES
    rows_b = LINE * CAP
    rows_d = BLOCKS * rows_b
    share = hidden // 2
    depth = width // NY
    slot_rows = 48
    vmem = pl.BlockSpec(memory_space=pltpu.VMEM)

    def bf16(*shape):
        return pltpu.VMEM(shape, BF16)

    def rows16(*lead):
        return bf16(*lead, tiles, LANES)

    scratch = [
        rows16(slot_rows), rows16(slot_rows), rows16(2, rows_d), rows16(2, rows_d),
        bf16(NY, 2 * rows_d, depth), bf16(NY, 2 * rows_d, depth),
        bf16(256, 256), bf16(slot_rows, n_tok),
        bf16(2, share, depth // 2), bf16(NY, NX, share, depth), bf16(NX, NY, share, depth),
        pltpu.VMEM((NX, 2 * rows_d, share), F32), pltpu.VMEM((NX, 2 * rows_d, share), F32),
        bf16(NX, 2 * rows_d, share), bf16(NX, share, 2 * rows_d), bf16(NX, share, 2 * rows_d),
        bf16(NY, rows_d, depth), rows16(2, rows_d), rows16(rows_d),
        rows16(rows_d), rows16(CHAIN, 2 * CAP), rows16(CHAIN, 2 * CAP), rows16(CHAIN, 2 * CAP), rows16(CHAIN, 2 * CAP),
        rows16(LINE, CAP), rows16(LINE, CAP), rows16(LINE, CAP), rows16(LINE, CAP), rows16(slot_rows),
        bf16(NY, n_tok, width), bf16(NY, n_tok, width),
    ]
    scratch += [bf16(2, n_tok // 2, width)] * 4
    for _ in range(2):
        scratch += [bf16(4, 4, share, depth)] + [bf16(2, 2, share, depth)] * 4
        scratch += [bf16(4, share, depth)] + [bf16(2, share // 2, depth)] * 4
    scratch += [bf16(2, share, depth), bf16(2, share, depth // 2)]
    scratch += [pltpu.SemaphoreType.DMA((N_COPIES,)), pltpu.SemaphoreType.DMA((N_COPIES,))]
    scratch += [pltpu.SemaphoreType.REGULAR((3,))]
    token_grad, new_in, new_out = pl.pallas_call(
        functools.partial(kernel, (width, hidden)),
        out_shape=(
            jax.ShapeDtypeStruct((n_tok, width), BF16),
            jax.ShapeDtypeStruct(w_in_t.shape, F32),
            jax.ShapeDtypeStruct(w_out_t.shape, F32),
        ),
        in_specs=[vmem] * 6,
        out_specs=(vmem, vmem, vmem),
        scratch_shapes=scratch,
        compiler_params=pltpu.CompilerParams(
            collective_id=0, has_side_effects=True, vmem_limit_bytes=60 * 1024 * 1024
        ),
    )(
        tokens,
        attn_partials.reshape(NY, 2, n_tok, width),
        expert_ids.reshape(1, n_tok),
        gate.reshape(1, n_tok),
        w_in_t,
        w_out_t,
    )
    results = (token_grad, new_in, new_out)
    token_grad, new_in, new_out = pl.pallas_call(
        hand_over,
        out_shape=tuple(jax.ShapeDtypeStruct(r.shape, r.dtype) for r in results),
        in_specs=[vmem] * 3,
        out_specs=(vmem, vmem, vmem),
    )(*results)
    return token_grad, new_in.T, new_out.T


def solution(mesh):
    in_specs = (
        P(("expert", "dp"), None),
        P("dp", "expert", None),
        P(("expert", "dp")),
        P(("expert", "dp")),
        P("dp", "expert"),
        P("dp", "expert"),
    )
    out_specs = (P(("expert", "dp"), None), P("dp", "expert"), P("dp", "expert"))
    return jax.shard_map(shards, mesh=mesh, in_specs=in_specs, out_specs=out_specs, check_vma=False)
```

```python
import functools

import jax
import jax.numpy as jnp
from jax import lax
from jax.experimental import pallas as pl
from jax.experimental.pallas import tpu as pltpu
from jax.sharding import PartitionSpec as P

NX = 4
NY = 4
LINE = 4
BLOCKS = 4
CAP = 10
LANES = 128
MESH = pl.DeviceIdType.MESH

gelu_coef = 0.7978845608028654
cubic_coef = 0.044715
step_rate = 0.5
F32 = jnp.float32
BF16 = jnp.bfloat16


def add16(*terms):
    total = terms[0].astype(F32)
    for term in terms[1:]:
        total = total + term.astype(F32)
    return total.astype(BF16)


class Copy:
    def __init__(self, copy, when):
        self.copy = copy
        self.when = when

    def wait_recv(self, when=None):
        guarded(when, self.copy.wait_recv)


def guarded(when, action):
    if when is None:
        action()
    else:
        pl.when(when)(action)


class Copies:
    def __init__(self, send_sems, recv_sems):
        self.send_sems = send_sems
        self.recv_sems = recv_sems
        self.sends = 0
        self.recvs = 0
        self.started = []

    def slots(self, count):
        first = self.recvs
        self.recvs += count
        return first

    def send_slots(self, count):
        first = self.sends
        self.sends += count
        return first

    def make(self, src, dst, device, recv=None, send=None):
        if recv is None:
            recv = self.slots(1)
        if send is None:
            send = self.sends
            self.sends += 1
        return pltpu.make_async_remote_copy(
            src_ref=src,
            dst_ref=dst,
            send_sem=self.send_sems.at[send],
            recv_sem=self.recv_sems.at[recv],
            device_id=device,
            device_id_type=MESH,
        )

    def start(self, src, dst, device, when=None, recv=None):
        copy = Copy(self.make(src, dst, device, recv), when)
        guarded(when, copy.copy.start)
        self.started.append(copy)
        return copy

    def finish(self):
        for copy in self.started:
            guarded(copy.when, copy.copy.wait_send)


N_COPIES = 384
CHAIN = 3
LAG = 2


def kernel(
    dims,
    tok_ref, attn_ref, ids_ref, gate_ref, win_ref, wout_ref,
    tg_ref, nwin_ref, nwout_ref,
    pk_t, pk_g, x3, g3, x2, g2, perm, disp,
    w_stage, w_in, w_out, pre_slope, grad_sum, pg, pg_t, hid, p2, p3, p_mate,
    q3, zr, zl, zs_r, zs_l, own_r, own_l, own_sr, own_sl, slots,
    a_mate, a_sum, a_r1, a_m3, a_r3, a_r2,
    d_in, i_r1, i_m3, i_r3, i_r2, i_sum, is_r1, is_m3, is_r3, is_r2,
    d_out, o_r1, o_m3, o_r3, o_r2, o_sum, os_r1, os_m3, os_r3, os_r2,
    d_part, d_other,
    send_sems, recv_sems, reach_sems,
):
    width, hidden = dims
    scale_in = width ** (-0.5)
    scale_out = (hidden * NX * LINE) ** (-0.5)
    tiles = width // LANES
    share = hidden // 2
    depth = width // NY
    expert = lax.axis_index("expert")
    dp = lax.axis_index("dp")
    z = expert // NX
    x = expert % NX
    block = z // LINE
    place = z % LINE
    y = dp // 2
    core = dp % 2
    rows_b = LINE * CAP
    rows_d = BLOCKS * rows_b

    right = (z * NX + (x + 1) % NX, dp)
    left = (z * NX + (x + NX - 1) % NX, dp)
    up = (expert, ((y + 1) % NY) * 2 + core)
    down = (expert, ((y + NY - 1) % NY) * 2 + core)
    mate = (expert, y * 2 + (1 - core))

    last = LINE - 1
    not_first, not_last = place > 0, place < last
    at_first, at_last = place == 0, place == last
    front = ((z + 1) % (BLOCKS * LINE) * NX + x, dp)
    back_z = ((z + BLOCKS * LINE - 1) % (BLOCKS * LINE) * NX + x, dp)

    def seat(step, at):
        return ((((block + step + BLOCKS) % BLOCKS) * LINE + at) * NX + x, dp)

    def z_step(step):
        return ((z + step + BLOCKS * LINE) % (BLOCKS * LINE) * NX + x, dp)

    barrier = pltpu.get_barrier_semaphore()
    near = (right, left, up, down, mate, front, back_z)
    for device in near:
        pl.semaphore_signal(barrier, inc=1, device_id=device, device_id_type=MESH)

    def reach(round_index):
        for step in ((1, -1), (2, -2), (4, -4))[round_index]:
            pl.semaphore_signal(
                reach_sems.at[round_index], inc=1, device_id=z_step(step), device_id_type=MESH
            )

    def reached(round_index):
        pl.semaphore_wait(reach_sems.at[round_index], 2)

    copies = Copies(send_sems, recv_sems)

    def arrive(*waiting):
        for copy in waiting:
            copy.wait_recv()

    n_tok = tok_ref.shape[0]

    def pack(rows, dst):
        n_slot = disp.shape[0]
        packed = jnp.dot(disp[...], rows, preferred_element_type=F32).astype(BF16)
        for g in range(n_slot // 16):
            stacked = jnp.concatenate(
                [packed[g * 16:(g + 1) * 16, k * LANES:(k + 1) * LANES] for k in range(tiles)], axis=0
            )
            moved = jnp.dot(perm[...], stacked, preferred_element_type=F32).astype(BF16)
            dst[g * 16:(g + 1) * 16] = moved.reshape(16, tiles, LANES)

    per = depth // LANES

    def to_wide(src, dst, half):
        def body(i, carry):
            pair = [src[half, pl.ds(i * 32 + h * 16, 16)].reshape(256, LANES) for h in range(2)]
            moved = jnp.dot(perm[...], jnp.concatenate(pair, axis=1), preferred_element_type=F32).astype(BF16)
            for h in range(2):
                at = pl.ds(pl.multiple_of(half * rows_d + i * 32 + h * 16, 16), 16)
                for k in range(tiles):
                    dst[k // per, at, (k % per) * LANES:(k % per + 1) * LANES] = moved[
                        k * 16:(k + 1) * 16, h * LANES:(h + 1) * LANES
                    ]
            return carry

        lax.fori_loop(0, rows_d // 32, body, 0, unroll=True)

    def to_narrow(src, dst, half):
        def body(i, carry):
            pair = []
            for h in range(2):
                at = pl.ds(pl.multiple_of(i * 32 + h * 16, 16), 16)
                pair.append(jnp.concatenate(
                    [src[k // per, at, (k % per) * LANES:(k % per + 1) * LANES] for k in range(tiles)], axis=0
                ))
            moved = jnp.dot(perm[...], jnp.concatenate(pair, axis=1), preferred_element_type=F32).astype(BF16)
            for h in range(2):
                dst[half, pl.ds(i * 32 + h * 16, 16)] = moved[:, h * LANES:(h + 1) * LANES].reshape(16, tiles, LANES)
            return carry

        lax.fori_loop(0, rows_d // 32, body, 0, unroll=True)

    def row_at(c, p):
        return c * rows_b + p * CAP

    mine = pl.ds(pl.multiple_of(core * share, share), share)
    other = pl.ds(pl.multiple_of((1 - core) * share, share), share)
    lanes_mine = pl.ds(pl.multiple_of(core * (depth // 2), depth // 2), depth // 2)
    lanes_other = pl.ds(pl.multiple_of((1 - core) * (depth // 2), depth // 2), depth // 2)
    w_in[y, x, :, lanes_mine] = win_ref[mine].astype(BF16)
    w_out[x, y, :, lanes_mine] = wout_ref[mine].astype(BF16)
    w_stage[0] = win_ref[other].astype(BF16)
    w_stage[1] = wout_ref[other].astype(BF16)
    pl.semaphore_wait(barrier, len(near))
    reach(0)

    def halves(count):
        return pl.ds(0, count // 2), pl.ds(count // 2, count // 2)

    X_RING = (x, right, left)
    Y_RING = (y, up, down)

    def gather_first(blk, ring):
        pos, upper, lower = ring
        return [copies.start(blk(pos), blk(pos), device) for device in (upper, lower)]

    def gather_next(sent, blk, ring):
        pos, upper, lower = ring
        low, high = halves(share)
        below, above = (pos + 3) % 4, (pos + 1) % 4
        sent[0].wait_recv()
        to_up = copies.start(blk(below).at[low], blk(below).at[low], upper)
        sent[1].wait_recv()
        to_down = copies.start(blk(above).at[high], blk(above).at[high], lower)
        return [to_up, to_down]

    def scatter_first(blk, count, buf1, buf2, ring):
        pos, upper, lower = ring
        low, high = halves(count)
        far, above, below = (pos + 2) % 4, (pos + 1) % 4, (pos + 3) % 4
        return {
            "u1": copies.start(blk(far).at[low], buf1.at[0], upper),
            "d1": copies.start(blk(far).at[high], buf1.at[1], lower),
            "u2": copies.start(blk(above).at[high], buf2.at[0], upper),
            "d2": copies.start(blk(below).at[low], buf2.at[1], lower),
        }

    def scatter_middle(sent, blk, count, buf1, mid, buf3, ring):
        pos, upper, lower = ring
        low, high = halves(count)
        sent["u1"].wait_recv()
        mid[0] = add16(buf1[0], blk((pos + 1) % 4).at[low][...])
        sent["u3"] = copies.start(mid.at[0], buf3.at[0], upper)
        sent["d1"].wait_recv()
        mid[1] = add16(buf1[1], blk((pos + 3) % 4).at[high][...])
        sent["d3"] = copies.start(mid.at[1], buf3.at[1], lower)

    def scatter_end(sent, blk, count, buf2, buf3, ring):
        low, high = halves(count)
        pos = ring[0]
        arrive(sent["d2"], sent["u3"])
        first = blk(pos).at[low][...].astype(F32) + buf2[1].astype(F32) + buf3[0].astype(F32)
        arrive(sent["u2"], sent["d3"])
        second = blk(pos).at[high][...].astype(F32) + buf2[0].astype(F32) + buf3[1].astype(F32)
        return first, second

    def attn_begin(sent):
        low, high = halves(n_tok)
        out = {}
        for q in (2, 1, 3, 0):
            at = (y + q) % NY
            sent[q].wait_recv()
            a_sum[at] = add16(attn_ref[at, core], a_mate[at])
            if q == 2:
                out["u1"] = copies.start(a_sum.at[at, low], a_r1.at[0], up)
                out["d1"] = copies.start(a_sum.at[at, high], a_r1.at[1], down)
            elif q == 1:
                out["u2"] = copies.start(a_sum.at[at, high], a_r2.at[0], up)
            elif q == 3:
                out["d2"] = copies.start(a_sum.at[at, low], a_r2.at[1], down)
        return out

    def chunk(j):
        return (block + BLOCKS + j) % BLOCKS

    def z_begin(packed, rows):
        here = pl.ds(row_at(block, place), CAP)
        mine_at = pl.ds(block * CAP, CAP)
        state = {"rows": rows, "edge": {}, "relay": {}}
        state["r1"] = copies.start(packed.at[mine_at], rows.at[core, here], front, not_last)
        state["l1"] = copies.start(packed.at[mine_at], rows.at[core, here], back_z, not_first)
        for step in (1, 2):
            for sign in (1, -1):
                first = copies.slots(LINE)
                sends = None if step == 1 else (place >= 2 if sign == 1 else place < 2)
                copies.start(
                    packed.at[pl.ds(chunk(sign * step) * CAP, CAP)], rows.at[core, here],
                    seat(sign * step, 0 if sign == 1 else last), sends, recv=first + place,
                )
                state["edge"][sign * step] = first
        for sign in (1, -1):
            state["relay"][sign] = (copies.slots(CHAIN), copies.send_slots(CHAIN))
        return state

    def z_line(state, n):
        rows = state["rows"]
        for key, sign, ahead, came, go in (("r", 1, front, place >= n, not_last), ("l", -1, back_z, place + n <= last, not_first)):
            state[key + str(n)].wait_recv(came)
            if n < last:
                at = pl.ds(row_at(block, jnp.clip(place - sign * n, 0, last)), CAP)
                state[key + str(n + 1)] = copies.start(rows.at[core, at], rows.at[core, at], ahead, came & go)

    directions = (
        (1, front, at_first, not_first, not_last, place), (-1, back_z, at_last, not_last, not_first, last - place),
    )

    def pair_place(sign, k):
        return 2 * (1 - k % 2) if sign == 1 else 2 * (k % 2)

    def z_chain(state, *times):
        rows = state["rows"]

        def view(sign, k):
            from_block = (block + BLOCKS - sign * (1 + k // 2)) % BLOCKS
            return rows.at[core, pl.ds(row_at(from_block, pair_place(sign, k)), 2 * CAP)]

        for t in times:
            for sign, ahead, entry, inner, go, rank in directions:
                recv, send = state["relay"][sign]
                if t < CHAIN:
                    at = view(sign, t)
                    first = state["edge"][sign * (1 + t // 2)] + pair_place(sign, t)
                    start = copies.make(at, at, ahead, recv + t, send + t)
                    half_at = rows.at[core, pl.ds(row_at(0, 0), CAP)]
                    arrivals = [copies.make(half_at, half_at, mate, first + n, 0) for n in range(2)]

                    def enter(start=start, arrivals=arrivals):
                        for copy in arrivals:
                            copy.wait_recv()
                        start.start()

                    pl.when(entry)(enter)
                k = t - LAG * rank
                safe = jnp.clip(k, 0, CHAIN - 1)
                at = view(sign, safe)
                relay = copies.make(at, at, ahead, recv + safe, send + safe)

                def pass_on(relay=relay, go=go):
                    relay.wait_recv()
                    pl.when(go)(relay.start)

                pl.when(inner & (k >= 0) & (k < CHAIN))(pass_on)
                if t == CHAIN - 1 + LAG * last:
                    for n in range(CHAIN):
                        sent = copies.make(view(sign, n), view(sign, n), ahead, recv + n, send + n)
                        copies.started.append(Copy(sent, go))

    def z_share(state, j):
        at = state["rows"].at[core, pl.ds(row_at(chunk(j), 0), rows_b)]
        return copies.start(at, at, mate)

    def back_share(j):
        at = pl.ds(row_at(chunk(j), 0), rows_b)
        return copies.start(p3.at[1 - core, at], p_mate.at[at], mate)

    def back_sum(copy, j):
        at = pl.ds(row_at(chunk(j), 0), rows_b)
        copy.wait_recv()
        q3[at] = add16(p3[core, at], p_mate[at])

    def back_chain(state, *times):
        if not state:
            for sign in (1, -1):
                state[sign] = (copies.slots(CHAIN), copies.send_slots(CHAIN), copies.slots(2), copies.send_slots(2 * CHAIN))
        for t in times:
            for (sign, ahead, entry, inner, go, rank), buf, out in zip(directions, (zr, zl), (zs_r, zs_l)):
                recv, send, end, send_end = state[sign]
                k = t - LAG * rank
                safe = jnp.clip(k, 0, CHAIN - 1)
                step = 1 + safe // 2
                to_block = (block + BLOCKS + sign * step) % BLOCKS
                first = pair_place(-sign, safe)
                relay = copies.make(out.at[safe], buf.at[safe], ahead, recv + safe, send + safe)
                leaving = [
                    copies.make(
                        out.at[safe, pl.ds(n * CAP, CAP)], slots.at[pl.ds(block * CAP, CAP)],
                        ((to_block * LINE + first + n) * NX + x, dp), end + safe // 2, send_end + 2 * safe + n,
                    )
                    for n in range(2)
                ]

                def pass_on(
                    relay=relay, leaving=leaving, inner=inner, go=go, buf=buf, out=out, safe=safe,
                    at=pl.ds(row_at(to_block, first), 2 * CAP),
                ):
                    pl.when(inner)(relay.wait_recv)
                    out[safe] = add16(q3[at], buf[safe])
                    pl.when(go)(relay.start)

                    @pl.when(jnp.logical_not(go))
                    def _():
                        for copy in leaving:
                            copy.start()

                pl.when((k >= 0) & (k < CHAIN))(pass_on)
                if t == CHAIN - 1 + LAG * last:
                    for n in range(CHAIN):
                        sent = copies.make(out.at[n], buf.at[n], ahead, recv + n, send + n)
                        copies.started.append(Copy(sent, go))
                    for n in range(2 * CHAIN):
                        at = out.at[n // 2, pl.ds(0, CAP)]
                        sent = copies.make(at, at, ahead, end, send_end + n)
                        copies.started.append(Copy(sent, jnp.logical_not(go)))

    def back_chain_end(state):
        at = slots.at[pl.ds(0, CAP)]
        for sign in (1, -1):
            end = state[sign][2]
            for n, came in ((0, None), (1, place < 2 if sign == 1 else place >= 2)):
                guarded(came, copies.make(at, at, mate, end + n, 0).wait_recv)

    def back_own():
        for n in (3, 2, 1):
            for key, sign, ahead, buf, out in (("r", 1, front, own_r, own_sr), ("l", -1, back_z, own_l, own_sl)):
                target = place + sign * n
                valid = (target >= 0) & (target <= last)
                at = pl.ds(row_at(block, jnp.clip(target, 0, last)), CAP)
                behind = (place - sign >= 0) & (place - sign <= last)
                if n < last:
                    own_state[key + str(n + 1)].wait_recv(valid & behind)
                out[n - 1] = add16(q3[at], buf[n])
                own_state[key + str(n)] = copies.start(out.at[n - 1], buf.at[n - 1], ahead, valid)

    def back_own_end():
        own_state["r1"].wait_recv(not_first)
        own_state["l1"].wait_recv(not_last)
        slots[pl.ds(block * CAP, CAP)] = add16(q3[pl.ds(row_at(block, place), CAP)], own_r[0], own_l[0])

    own_state = {}

    def in_x(i):
        return w_in.at[y, i]

    def out_y(i):
        return w_out.at[x, i]

    def in_y(s):
        return lambda i: w_in.at[i, s]

    def out_x(s):
        return lambda i: w_out.at[i, s]

    def forward(i):
        pre = None
        for k in range(NY):
            term = lax.dot_general(
                x2[k], w_in[k, i], (((1,), (1,)), ((), ())), preferred_element_type=F32
            )
            pre = term if pre is None else pre + term
        pre = pre * scale_in
        square = pre * pre
        tangent = jnp.tanh(gelu_coef * (pre + cubic_coef * square * pre))
        hid[i] = (0.5 * pre * (1.0 + tangent)).astype(BF16).T
        pre_slope[i] = scale_out * (
            0.5 * (1.0 + tangent) + 0.5 * pre * (1.0 - tangent * tangent) * gelu_coef * (1.0 + 3.0 * cubic_coef * square)
        )

    def out_grads(i):
        for k in range(NY):
            d_out[i, k] = (jnp.dot(hid[i], g2[k], preferred_element_type=F32) * scale_out).astype(BF16)

    def hidden_grads(k, begin):
        for i in range(NX):
            term = lax.dot_general(
                g2[k], w_out[i, k], (((1,), (1,)), ((), ())), preferred_element_type=F32
            )
            grad_sum[i] = term if begin else grad_sum[i] + term

    def in_grads(k):
        for i in range(NX):
            d_in[k, i] = (jnp.dot(pg_t[i], x2[k], preferred_element_type=F32) * scale_in).astype(BF16)

    order = (0, 1, 3, 2)
    w_pair = [
        copies.start(w_stage.at[0], w_in.at[y, x, :, lanes_mine], mate),
        copies.start(w_stage.at[1], w_out.at[x, y, :, lanes_mine], mate),
    ]
    attn_sent = {}
    for q in (2, 1, 3, 0):
        at = (y + q) % NY
        attn_sent[q] = copies.start(attn_ref.at[at, 1 - core], a_mate.at[at], mate)
    reached(0)
    reach(1)
    arrive(*w_pair)
    in_big, out_big, in_last, out_last = {}, {}, {}, {}
    in_first = gather_first(in_x, X_RING)
    in_big[0] = gather_first(in_y(x), Y_RING)
    out_big[0] = gather_first(out_x(y), X_RING)
    reached(1)
    reach(2)
    row_i = lax.broadcasted_iota(jnp.int32, (256, 256), 0)
    col_i = lax.broadcasted_iota(jnp.int32, (256, 256), 1)
    perm[...] = jnp.where(col_i == ((row_i & 15) << 4) + (row_i >> 4), 1.0, 0.0).astype(BF16)

    ids_row = ids_ref[...].astype(F32)
    eye_t = lax.broadcasted_iota(jnp.int32, (n_tok, n_tok), 0)
    eye_s = lax.broadcasted_iota(jnp.int32, (n_tok, n_tok), 1)
    spread_ids = jnp.broadcast_to(ids_row, (n_tok, n_tok))
    ids_col = jnp.sum(jnp.where(eye_t == eye_s, spread_ids, 0.0), axis=1, keepdims=True)
    earlier = jnp.where((ids_col == spread_ids) & (eye_t < eye_s), 1.0, 0.0)
    rank_row = jnp.sum(earlier, axis=0, keepdims=True)
    slot_row = jnp.where(rank_row < CAP, ids_row * CAP + rank_row, -1.0)
    n_slot = disp.shape[0]
    slot_i = lax.broadcasted_iota(jnp.int32, (n_slot, n_tok), 0).astype(F32)
    disp[...] = jnp.where(slot_i == jnp.broadcast_to(slot_row, (n_slot, n_tok)), 1.0, 0.0).astype(BF16)
    gate_col = jnp.sum(
        jnp.where(eye_t == eye_s, jnp.broadcast_to(gate_ref[...], (n_tok, n_tok)), 0.0),
        axis=1, keepdims=True,
    )

    attn_ring = attn_begin(attn_sent)
    out_first = gather_first(out_y, Y_RING)
    pack(tok_ref[...], pk_t)
    x3[core, pl.ds(row_at(block, place), CAP)] = pk_t[pl.ds(block * CAP, CAP)]
    reached(2)
    t_state = z_begin(pk_t, x3)
    @pl.when(at_first)
    def _():
        zr[...] = jnp.zeros_like(zr)
        own_r[...] = jnp.zeros_like(own_r)

    @pl.when(at_last)
    def _():
        zl[...] = jnp.zeros_like(zl)
        own_l[...] = jnp.zeros_like(own_l)

    slots[BLOCKS * CAP:] = jnp.zeros((slots.shape[0] - BLOCKS * CAP, tiles, LANES), BF16)

    z_line(t_state, 1)
    scatter_middle(attn_ring, lambda i: a_sum.at[i], n_tok, a_r1, a_m3, a_r3, Y_RING)
    z_chain(t_state, 0, 1)
    in_next = gather_next(in_first, in_x, X_RING)
    for q in (1, 3):
        in_big[q] = gather_first(in_y((x + q) % NX), Y_RING)
    z_chain(t_state, 2, 3)
    z_line(t_state, 2)
    z_chain(t_state, 4)
    first, second = scatter_end(attn_ring, lambda i: a_sum.at[i], n_tok, a_r2, a_r3, Y_RING)
    summed = jnp.concatenate([first, second], axis=0)
    pack((gate_col * summed).astype(BF16), pk_g)
    g3[core, pl.ds(row_at(block, place), CAP)] = pk_g[pl.ds(block * CAP, CAP)]
    g_state = z_begin(pk_g, g3)
    z_chain(t_state, 5, 6)
    z_line(t_state, 3)
    arrive(*in_next)
    in_big[2] = gather_first(in_y((x + 2) % NX), Y_RING)
    out_next = gather_next(out_first, out_y, Y_RING)
    for q in (1, 3):
        out_big[q] = gather_first(out_x((y + q) % NY), X_RING)
    z_chain(t_state, 7, 8)
    t_share = [z_share(t_state, j) for j in range(4)]
    z_line(g_state, 1)
    z_chain(g_state, 0, 1)
    to_wide(x3, x2, core)
    in_last[0] = gather_next(in_big[0], in_y(x), Y_RING)
    out_last[0] = gather_next(out_big[0], out_x(y), X_RING)
    z_chain(g_state, 2)
    z_line(g_state, 2)
    arrive(*t_share)
    to_wide(x3, x2, 1 - core)
    z_chain(g_state, 3, 4)
    arrive(*out_next)
    out_big[2] = gather_first(out_x((y + 2) % NY), X_RING)
    in_last[1] = gather_next(in_big[1], in_y((x + 1) % NX), Y_RING)
    in_last[3] = gather_next(in_big[3], in_y((x + 3) % NX), Y_RING)
    z_chain(g_state, 5)
    z_line(g_state, 3)
    arrive(*in_last[0])
    forward(x)
    z_chain(g_state, 6, 7)
    out_last[1] = gather_next(out_big[1], out_x((y + 1) % NY), X_RING)
    out_last[3] = gather_next(out_big[3], out_x((y + 3) % NY), X_RING)
    arrive(*in_last[1], *in_last[3])
    z_chain(g_state, 8)
    g_share = [z_share(g_state, j) for j in range(4)]
    in_last[2] = gather_next(in_big[2], in_y((x + 2) % NX), Y_RING)
    out_last[2] = gather_next(out_big[2], out_x((y + 2) % NY), X_RING)
    forward((x + 1) % NX)
    forward((x + 3) % NX)
    to_wide(g3, g2, core)
    arrive(*g_share)
    to_wide(g3, g2, 1 - core)
    out_grads(x)
    arrive(*out_last[0])
    hidden_grads(y, True)
    for q in (1, 3):
        out_grads((x + q) % NX)
        arrive(*out_last[q])
        hidden_grads((y + q) % NY, False)
    arrive(*in_last[2])
    forward((x + 2) % NX)
    out_grads((x + 2) % NX)
    out_ring = scatter_first(lambda i: d_out.at[i], NY, o_r1, o_r2, X_RING)
    arrive(*out_last[2])
    hidden_grads((y + 2) % NY, False)
    for i in range(NX):
        grad = (grad_sum[i] * pre_slope[i]).astype(BF16)
        pg[i] = grad
        pg_t[i] = grad.T
    for q in (2, 1, 3):
        in_grads((y + q) % NY)
    in_ring = scatter_first(lambda i: d_in.at[i], NX, i_r1, i_r2, Y_RING)

    back = {}
    for part_i in range(2):
        half = (1 - core) if part_i == 0 else core
        for k in range(NY):
            term = None
            for i in range(NX):
                add = jnp.dot(
                    pg[i, pl.ds(pl.multiple_of(half * rows_d, rows_d), rows_d)], w_in[k, i],
                    preferred_element_type=F32,
                )
                term = add if term is None else term + add
            p2[k] = (term * scale_in).astype(BF16)
        to_narrow(p2, p3, half)
        if part_i == 0:
            for j in order:
                back[j] = back_share(j)
            scatter_middle(out_ring, lambda i: d_out.at[i], NY, o_r1, o_m3, o_r3, X_RING)
    for j in order:
        back_sum(back[j], j)
    ends = {}
    back_chain(ends, 0)
    back_own()
    back_chain(ends, 1, 2)
    in_grads(y)
    back_chain(ends, 3, 4)
    scatter_middle(in_ring, lambda i: d_in.at[i], NX, i_r1, i_m3, i_r3, Y_RING)
    back_chain(ends, 5, 6, 7, 8)
    back_own_end()

    first, second = scatter_end(out_ring, lambda i: d_out.at[i], NY, o_r2, o_r3, X_RING)
    o_sum[0:2] = first.astype(BF16)
    o_sum[2:4] = second.astype(BF16)
    out_small = scatter_first(lambda i: o_sum.at[i], share, os_r1, os_r2, Y_RING)
    first, second = scatter_end(in_ring, lambda i: d_in.at[i], NX, i_r2, i_r3, Y_RING)
    i_sum[0:2] = first.astype(BF16)
    i_sum[2:4] = second.astype(BF16)
    in_small = scatter_first(lambda i: i_sum.at[i], share, is_r1, is_r2, X_RING)
    scatter_middle(out_small, lambda i: o_sum.at[i], share, os_r1, os_m3, os_r3, Y_RING)
    scatter_middle(in_small, lambda i: i_sum.at[i], share, is_r1, is_m3, is_r3, X_RING)
    pair = []
    for t, sent, sums, buf2, buf3, ring in (
        (1, out_small, o_sum, os_r2, os_r3, Y_RING), (0, in_small, i_sum, is_r2, is_r3, X_RING),
    ):
        low, high = halves(share)
        first, second = scatter_end(sent, lambda i: sums.at[i], share, buf2, buf3, ring)
        d_part[t, low] = first.astype(BF16)
        d_part[t, high] = second.astype(BF16)
        pair.append(copies.start(d_part.at[t, :, lanes_other], d_other.at[t], mate))

    back_chain_end(ends)
    wide = []
    for g in range(n_slot // 16):
        moved = jnp.dot(
            perm[...], slots[g * 16:(g + 1) * 16].reshape(256, LANES), preferred_element_type=F32
        ).astype(BF16)
        wide.append(jnp.concatenate([moved[k * 16:(k + 1) * 16] for k in range(tiles)], axis=1))
    slots_wide = jnp.concatenate(wide, axis=0)
    tg_ref[...] = lax.dot_general(
        disp[...], slots_wide, (((0,), (0,)), ((), ())), preferred_element_type=F32
    ).astype(BF16)

    for t, copy, old, new in ((1, pair[0], wout_ref, nwout_ref), (0, pair[1], win_ref, nwin_ref)):
        new[mine] = old[mine] - step_rate * d_part[t, :, lanes_mine].astype(F32)
        copy.wait_recv()
        new[other] = old[other] - step_rate * d_other[t].astype(F32)
    copies.finish()


def hand_over(*refs):
    for source, target in zip(refs[:3], refs[3:]):
        target[...] = source[...]


def shards(tokens, attn_partials, expert_ids, gate, w_in, w_out):
    n_tok, width = tokens.shape
    w_in_t, w_out_t = w_in.T, w_out.T
    hidden = w_in_t.shape[0]
    tiles = width // LANES
    rows_b = LINE * CAP
    rows_d = BLOCKS * rows_b
    share = hidden // 2
    depth = width // NY
    slot_rows = 48
    vmem = pl.BlockSpec(memory_space=pltpu.VMEM)

    def bf16(*shape):
        return pltpu.VMEM(shape, BF16)

    def rows16(*lead):
        return bf16(*lead, tiles, LANES)

    scratch = [
        rows16(slot_rows), rows16(slot_rows), rows16(2, rows_d), rows16(2, rows_d),
        bf16(NY, 2 * rows_d, depth), bf16(NY, 2 * rows_d, depth),
        bf16(256, 256), bf16(slot_rows, n_tok),
        bf16(2, share, depth // 2), bf16(NY, NX, share, depth), bf16(NX, NY, share, depth),
        pltpu.VMEM((NX, 2 * rows_d, share), F32), pltpu.VMEM((NX, 2 * rows_d, share), F32),
        bf16(NX, 2 * rows_d, share), bf16(NX, share, 2 * rows_d), bf16(NX, share, 2 * rows_d),
        bf16(NY, rows_d, depth), rows16(2, rows_d), rows16(rows_d),
        rows16(rows_d), rows16(CHAIN, 2 * CAP), rows16(CHAIN, 2 * CAP), rows16(CHAIN, 2 * CAP), rows16(CHAIN, 2 * CAP),
        rows16(LINE, CAP), rows16(LINE, CAP), rows16(LINE, CAP), rows16(LINE, CAP), rows16(slot_rows),
        bf16(NY, n_tok, width), bf16(NY, n_tok, width),
    ]
    scratch += [bf16(2, n_tok // 2, width)] * 4
    for _ in range(2):
        scratch += [bf16(4, 4, share, depth)] + [bf16(2, 2, share, depth)] * 4
        scratch += [bf16(4, share, depth)] + [bf16(2, share // 2, depth)] * 4
    scratch += [bf16(2, share, depth), bf16(2, share, depth // 2)]
    scratch += [pltpu.SemaphoreType.DMA((N_COPIES,)), pltpu.SemaphoreType.DMA((N_COPIES,))]
    scratch += [pltpu.SemaphoreType.REGULAR((3,))]
    token_grad, new_in, new_out = pl.pallas_call(
        functools.partial(kernel, (width, hidden)),
        out_shape=(
            jax.ShapeDtypeStruct((n_tok, width), BF16),
            jax.ShapeDtypeStruct(w_in_t.shape, F32),
            jax.ShapeDtypeStruct(w_out_t.shape, F32),
        ),
        in_specs=[vmem] * 6,
        out_specs=(vmem, vmem, vmem),
        scratch_shapes=scratch,
        compiler_params=pltpu.CompilerParams(
            collective_id=0, has_side_effects=True, vmem_limit_bytes=60 * 1024 * 1024
        ),
    )(
        tokens,
        attn_partials.reshape(NY, 2, n_tok, width),
        expert_ids.reshape(1, n_tok),
        gate.reshape(1, n_tok),
        w_in_t,
        w_out_t,
    )
    results = (token_grad, new_in, new_out)
    token_grad, new_in, new_out = pl.pallas_call(
        hand_over,
        out_shape=tuple(jax.ShapeDtypeStruct(r.shape, r.dtype) for r in results),
        in_specs=[vmem] * 3,
        out_specs=(vmem, vmem, vmem),
    )(*results)
    return token_grad, new_in.T, new_out.T


def solution(mesh):
    in_specs = (
        P(("expert", "dp"), None),
        P("dp", "expert", None),
        P(("expert", "dp")),
        P(("expert", "dp")),
        P("dp", "expert"),
        P("dp", "expert"),
    )
    out_specs = (P(("expert", "dp"), None), P("dp", "expert"), P("dp", "expert"))
    return jax.shard_map(shards, mesh=mesh, in_specs=in_specs, out_specs=out_specs, check_vma=False)
```

```python
import functools

import jax
import jax.numpy as jnp
from jax import lax
from jax.experimental import pallas as pl
from jax.experimental.pallas import tpu as pltpu
from jax.sharding import PartitionSpec as P

NX = 4
NY = 4
LINE = 4
BLOCKS = 4
CAP = 10
LANES = 128
MESH = pl.DeviceIdType.MESH

gelu_coef = 0.7978845608028654
cubic_coef = 0.044715
step_rate = 0.5
F32 = jnp.float32
BF16 = jnp.bfloat16


def add16(*terms):
    total = terms[0].astype(F32)
    for term in terms[1:]:
        total = total + term.astype(F32)
    return total.astype(BF16)


class Copy:
    def __init__(self, copy, when):
        self.copy = copy
        self.when = when

    def wait_recv(self, when=None):
        guarded(when, self.copy.wait_recv)


def guarded(when, action):
    if when is None:
        action()
    else:
        pl.when(when)(action)


class Copies:
    def __init__(self, send_sems, recv_sems):
        self.send_sems = send_sems
        self.recv_sems = recv_sems
        self.sends = 0
        self.recvs = 0
        self.started = []

    def slots(self, count):
        first = self.recvs
        self.recvs += count
        return first

    def send_slots(self, count):
        first = self.sends
        self.sends += count
        return first

    def make(self, src, dst, device, recv=None, send=None):
        if recv is None:
            recv = self.slots(1)
        if send is None:
            send = self.sends
            self.sends += 1
        return pltpu.make_async_remote_copy(
            src_ref=src,
            dst_ref=dst,
            send_sem=self.send_sems.at[send],
            recv_sem=self.recv_sems.at[recv],
            device_id=device,
            device_id_type=MESH,
        )

    def start(self, src, dst, device, when=None, recv=None):
        copy = Copy(self.make(src, dst, device, recv), when)
        guarded(when, copy.copy.start)
        self.started.append(copy)
        return copy

    def finish(self):
        for copy in self.started:
            guarded(copy.when, copy.copy.wait_send)


N_COPIES = 384
CHAIN = 3
LAG = 2


def kernel(
    dims,
    tok_ref, attn_ref, ids_ref, gate_ref, win_ref, wout_ref,
    tg_ref, nwin_ref, nwout_ref,
    pk_t, pk_g, x3, g3, x2, g2, perm, disp,
    w_stage, w_in, w_out, pre_slope, grad_sum, pg, pg_t, hid, p2, p3, p_mate,
    q3, zr, zl, zs_r, zs_l, own_r, own_l, own_sr, own_sl, slots,
    a_mate, a_sum, a_r1, a_m3, a_r3, a_r2,
    d_in, i_r1, i_m3, i_r3, i_r2, i_sum, is_r1, is_m3, is_r3, is_r2,
    d_out, o_r1, o_m3, o_r3, o_r2, o_sum, os_r1, os_m3, os_r3, os_r2,
    d_part, d_other,
    send_sems, recv_sems, reach_sems,
):
    width, hidden = dims
    scale_in = width ** (-0.5)
    scale_out = (hidden * NX * LINE) ** (-0.5)
    tiles = width // LANES
    share = hidden // 2
    depth = width // NY
    expert = lax.axis_index("expert")
    dp = lax.axis_index("dp")
    z = expert // NX
    x = expert % NX
    block = z // LINE
    place = z % LINE
    y = dp // 2
    core = dp % 2
    rows_b = LINE * CAP
    rows_d = BLOCKS * rows_b

    right = (z * NX + (x + 1) % NX, dp)
    left = (z * NX + (x + NX - 1) % NX, dp)
    up = (expert, ((y + 1) % NY) * 2 + core)
    down = (expert, ((y + NY - 1) % NY) * 2 + core)
    mate = (expert, y * 2 + (1 - core))

    last = LINE - 1
    not_first, not_last = place > 0, place < last
    at_first, at_last = place == 0, place == last
    front = ((z + 1) % (BLOCKS * LINE) * NX + x, dp)
    back_z = ((z + BLOCKS * LINE - 1) % (BLOCKS * LINE) * NX + x, dp)

    def seat(step, at):
        return ((((block + step + BLOCKS) % BLOCKS) * LINE + at) * NX + x, dp)

    def z_step(step):
        return ((z + step + BLOCKS * LINE) % (BLOCKS * LINE) * NX + x, dp)

    barrier = pltpu.get_barrier_semaphore()
    near = (right, left, up, down, mate, front, back_z)
    for device in near:
        pl.semaphore_signal(barrier, inc=1, device_id=device, device_id_type=MESH)

    def reach(round_index):
        for step in ((1, -1), (2, -2), (4, -4))[round_index]:
            pl.semaphore_signal(
                reach_sems.at[round_index], inc=1, device_id=z_step(step), device_id_type=MESH
            )

    def reached(round_index):
        pl.semaphore_wait(reach_sems.at[round_index], 2)

    copies = Copies(send_sems, recv_sems)

    def arrive(*waiting):
        for copy in waiting:
            copy.wait_recv()

    n_tok = tok_ref.shape[0]

    def pack(rows, dst):
        n_slot = disp.shape[0]
        packed = jnp.dot(disp[...], rows, preferred_element_type=F32).astype(BF16)
        for g in range(n_slot // 16):
            stacked = jnp.concatenate(
                [packed[g * 16:(g + 1) * 16, k * LANES:(k + 1) * LANES] for k in range(tiles)], axis=0
            )
            moved = jnp.dot(perm[...], stacked, preferred_element_type=F32).astype(BF16)
            dst[g * 16:(g + 1) * 16] = moved.reshape(16, tiles, LANES)

    per = depth // LANES

    def to_wide(src, dst, half):
        def body(i, carry):
            pair = [src[half, pl.ds(i * 32 + h * 16, 16)].reshape(256, LANES) for h in range(2)]
            moved = jnp.dot(perm[...], jnp.concatenate(pair, axis=1), preferred_element_type=F32).astype(BF16)
            for h in range(2):
                at = pl.ds(pl.multiple_of(half * rows_d + i * 32 + h * 16, 16), 16)
                for k in range(tiles):
                    dst[k // per, at, (k % per) * LANES:(k % per + 1) * LANES] = moved[
                        k * 16:(k + 1) * 16, h * LANES:(h + 1) * LANES
                    ]
            return carry

        lax.fori_loop(0, rows_d // 32, body, 0, unroll=True)

    def to_narrow(src, dst, half):
        def body(i, carry):
            pair = []
            for h in range(2):
                at = pl.ds(pl.multiple_of(i * 32 + h * 16, 16), 16)
                pair.append(jnp.concatenate(
                    [src[k // per, at, (k % per) * LANES:(k % per + 1) * LANES] for k in range(tiles)], axis=0
                ))
            moved = jnp.dot(perm[...], jnp.concatenate(pair, axis=1), preferred_element_type=F32).astype(BF16)
            for h in range(2):
                dst[half, pl.ds(i * 32 + h * 16, 16)] = moved[:, h * LANES:(h + 1) * LANES].reshape(16, tiles, LANES)
            return carry

        lax.fori_loop(0, rows_d // 32, body, 0, unroll=True)

    def row_at(c, p):
        return c * rows_b + p * CAP

    mine = pl.ds(pl.multiple_of(core * share, share), share)
    other = pl.ds(pl.multiple_of((1 - core) * share, share), share)
    lanes_mine = pl.ds(pl.multiple_of(core * (depth // 2), depth // 2), depth // 2)
    lanes_other = pl.ds(pl.multiple_of((1 - core) * (depth // 2), depth // 2), depth // 2)
    w_in[y, x, :, lanes_mine] = win_ref[mine].astype(BF16)
    w_out[x, y, :, lanes_mine] = wout_ref[mine].astype(BF16)
    w_stage[0] = win_ref[other].astype(BF16)
    w_stage[1] = wout_ref[other].astype(BF16)
    pl.semaphore_wait(barrier, len(near))
    reach(0)

    def halves(count):
        return pl.ds(0, count // 2), pl.ds(count // 2, count // 2)

    X_RING = (x, right, left)
    Y_RING = (y, up, down)

    def gather_first(blk, ring):
        pos, upper, lower = ring
        return [copies.start(blk(pos), blk(pos), device) for device in (upper, lower)]

    def gather_next(sent, blk, ring):
        pos, upper, lower = ring
        low, high = halves(share)
        below, above = (pos + 3) % 4, (pos + 1) % 4
        sent[0].wait_recv()
        to_up = copies.start(blk(below).at[low], blk(below).at[low], upper)
        sent[1].wait_recv()
        to_down = copies.start(blk(above).at[high], blk(above).at[high], lower)
        return [to_up, to_down]

    def scatter_far(blk, count, buf1, ring):
        pos, upper, lower = ring
        low, high = halves(count)
        far = (pos + 2) % 4
        return {
            "u1": copies.start(blk(far).at[low], buf1.at[0], upper),
            "d1": copies.start(blk(far).at[high], buf1.at[1], lower),
        }

    def scatter_near(sent, blk, count, buf2, ring):
        pos, upper, lower = ring
        low, high = halves(count)
        sent["u2"] = copies.start(blk((pos + 1) % 4).at[high], buf2.at[0], upper)
        sent["d2"] = copies.start(blk((pos + 3) % 4).at[low], buf2.at[1], lower)

    def scatter_first(blk, count, buf1, buf2, ring):
        sent = scatter_far(blk, count, buf1, ring)
        scatter_near(sent, blk, count, buf2, ring)
        return sent

    def scatter_middle(sent, blk, count, buf1, mid, buf3, ring):
        pos, upper, lower = ring
        low, high = halves(count)
        sent["u1"].wait_recv()
        mid[0] = add16(buf1[0], blk((pos + 1) % 4).at[low][...])
        sent["u3"] = copies.start(mid.at[0], buf3.at[0], upper)
        sent["d1"].wait_recv()
        mid[1] = add16(buf1[1], blk((pos + 3) % 4).at[high][...])
        sent["d3"] = copies.start(mid.at[1], buf3.at[1], lower)

    def scatter_end(sent, blk, count, buf2, buf3, ring):
        low, high = halves(count)
        pos = ring[0]
        arrive(sent["d2"], sent["u3"])
        first = blk(pos).at[low][...].astype(F32) + buf2[1].astype(F32) + buf3[0].astype(F32)
        arrive(sent["u2"], sent["d3"])
        second = blk(pos).at[high][...].astype(F32) + buf2[0].astype(F32) + buf3[1].astype(F32)
        return first, second

    def attn_begin(sent):
        low, high = halves(n_tok)
        out = {}
        for q in (2, 1, 3, 0):
            at = (y + q) % NY
            sent[q].wait_recv()
            a_sum[at] = add16(attn_ref[at, core], a_mate[at])
            if q == 2:
                out["u1"] = copies.start(a_sum.at[at, low], a_r1.at[0], up)
                out["d1"] = copies.start(a_sum.at[at, high], a_r1.at[1], down)
            elif q == 1:
                out["u2"] = copies.start(a_sum.at[at, high], a_r2.at[0], up)
            elif q == 3:
                out["d2"] = copies.start(a_sum.at[at, low], a_r2.at[1], down)
        return out

    def chunk(j):
        return (block + BLOCKS + j) % BLOCKS

    def z_begin(packed, rows):
        here = pl.ds(row_at(block, place), CAP)
        mine_at = pl.ds(block * CAP, CAP)
        state = {"rows": rows, "edge": {}, "relay": {}}
        state["r1"] = copies.start(packed.at[mine_at], rows.at[core, here], front, not_last)
        state["l1"] = copies.start(packed.at[mine_at], rows.at[core, here], back_z, not_first)
        for step in (1, 2):
            for sign in (1, -1):
                first = copies.slots(LINE)
                sends = None if step == 1 else (place >= 2 if sign == 1 else place < 2)
                copies.start(
                    packed.at[pl.ds(chunk(sign * step) * CAP, CAP)], rows.at[core, here],
                    seat(sign * step, 0 if sign == 1 else last), sends, recv=first + place,
                )
                state["edge"][sign * step] = first
        for sign in (1, -1):
            state["relay"][sign] = (copies.slots(CHAIN), copies.send_slots(CHAIN))
        return state

    def z_line(state, n):
        rows = state["rows"]
        for key, sign, ahead, came, go in (("r", 1, front, place >= n, not_last), ("l", -1, back_z, place + n <= last, not_first)):
            state[key + str(n)].wait_recv(came)
            if n < last:
                at = pl.ds(row_at(block, jnp.clip(place - sign * n, 0, last)), CAP)
                state[key + str(n + 1)] = copies.start(rows.at[core, at], rows.at[core, at], ahead, came & go)

    directions = (
        (1, front, at_first, not_first, not_last, place), (-1, back_z, at_last, not_last, not_first, last - place),
    )

    def pair_place(sign, k):
        return 2 * (1 - k % 2) if sign == 1 else 2 * (k % 2)

    def z_chain(state, *times):
        rows = state["rows"]

        def view(sign, k):
            from_block = (block + BLOCKS - sign * (1 + k // 2)) % BLOCKS
            return rows.at[core, pl.ds(row_at(from_block, pair_place(sign, k)), 2 * CAP)]

        for t in times:
            for sign, ahead, entry, inner, go, rank in directions:
                recv, send = state["relay"][sign]
                if t < CHAIN:
                    at = view(sign, t)
                    first = state["edge"][sign * (1 + t // 2)] + pair_place(sign, t)
                    start = copies.make(at, at, ahead, recv + t, send + t)
                    half_at = rows.at[core, pl.ds(row_at(0, 0), CAP)]
                    arrivals = [copies.make(half_at, half_at, mate, first + n, 0) for n in range(2)]

                    def enter(start=start, arrivals=arrivals):
                        for copy in arrivals:
                            copy.wait_recv()
                        start.start()

                    pl.when(entry)(enter)
                k = t - LAG * rank
                safe = jnp.clip(k, 0, CHAIN - 1)
                at = view(sign, safe)
                relay = copies.make(at, at, ahead, recv + safe, send + safe)

                def pass_on(relay=relay, go=go):
                    relay.wait_recv()
                    pl.when(go)(relay.start)

                pl.when(inner & (k >= 0) & (k < CHAIN))(pass_on)
                if t == CHAIN - 1 + LAG * last:
                    for n in range(CHAIN):
                        sent = copies.make(view(sign, n), view(sign, n), ahead, recv + n, send + n)
                        copies.started.append(Copy(sent, go))

    def z_share(state, j):
        at = state["rows"].at[core, pl.ds(row_at(chunk(j), 0), rows_b)]
        return copies.start(at, at, mate)

    def back_share(j):
        at = pl.ds(row_at(chunk(j), 0), rows_b)
        return copies.start(p3.at[1 - core, at], p_mate.at[at], mate)

    def back_sum(copy, j):
        at = pl.ds(row_at(chunk(j), 0), rows_b)
        copy.wait_recv()
        q3[at] = add16(p3[core, at], p_mate[at])

    def back_chain(state, *times):
        if not state:
            for sign in (1, -1):
                state[sign] = (copies.slots(CHAIN), copies.send_slots(CHAIN), copies.slots(2), copies.send_slots(2 * CHAIN))
        for t in times:
            for (sign, ahead, entry, inner, go, rank), buf, out in zip(directions, (zr, zl), (zs_r, zs_l)):
                recv, send, end, send_end = state[sign]
                k = t - LAG * rank
                safe = jnp.clip(k, 0, CHAIN - 1)
                step = 1 + safe // 2
                to_block = (block + BLOCKS + sign * step) % BLOCKS
                first = pair_place(-sign, safe)
                relay = copies.make(out.at[safe], buf.at[safe], ahead, recv + safe, send + safe)
                leaving = [
                    copies.make(
                        out.at[safe, pl.ds(n * CAP, CAP)], slots.at[pl.ds(block * CAP, CAP)],
                        ((to_block * LINE + first + n) * NX + x, dp), end + safe // 2, send_end + 2 * safe + n,
                    )
                    for n in range(2)
                ]

                def pass_on(
                    relay=relay, leaving=leaving, inner=inner, go=go, buf=buf, out=out, safe=safe,
                    at=pl.ds(row_at(to_block, first), 2 * CAP),
                ):
                    pl.when(inner)(relay.wait_recv)
                    out[safe] = add16(q3[at], buf[safe])
                    pl.when(go)(relay.start)

                    @pl.when(jnp.logical_not(go))
                    def _():
                        for copy in leaving:
                            copy.start()

                pl.when((k >= 0) & (k < CHAIN))(pass_on)
                if t == CHAIN - 1 + LAG * last:
                    for n in range(CHAIN):
                        sent = copies.make(out.at[n], buf.at[n], ahead, recv + n, send + n)
                        copies.started.append(Copy(sent, go))
                    for n in range(2 * CHAIN):
                        at = out.at[n // 2, pl.ds(0, CAP)]
                        sent = copies.make(at, at, ahead, end, send_end + n)
                        copies.started.append(Copy(sent, jnp.logical_not(go)))

    def back_chain_end(state):
        at = slots.at[pl.ds(0, CAP)]
        for sign in (1, -1):
            end = state[sign][2]
            for n, came in ((0, None), (1, place < 2 if sign == 1 else place >= 2)):
                guarded(came, copies.make(at, at, mate, end + n, 0).wait_recv)

    def back_own():
        for n in (3, 2, 1):
            for key, sign, ahead, buf, out in (("r", 1, front, own_r, own_sr), ("l", -1, back_z, own_l, own_sl)):
                target = place + sign * n
                valid = (target >= 0) & (target <= last)
                at = pl.ds(row_at(block, jnp.clip(target, 0, last)), CAP)
                behind = (place - sign >= 0) & (place - sign <= last)
                if n < last:
                    own_state[key + str(n + 1)].wait_recv(valid & behind)
                out[n - 1] = add16(q3[at], buf[n])
                own_state[key + str(n)] = copies.start(out.at[n - 1], buf.at[n - 1], ahead, valid)

    def back_own_end():
        own_state["r1"].wait_recv(not_first)
        own_state["l1"].wait_recv(not_last)
        slots[pl.ds(block * CAP, CAP)] = add16(q3[pl.ds(row_at(block, place), CAP)], own_r[0], own_l[0])

    own_state = {}

    def in_x(i):
        return w_in.at[y, i]

    def out_y(i):
        return w_out.at[x, i]

    def in_y(s):
        return lambda i: w_in.at[i, s]

    def out_x(s):
        return lambda i: w_out.at[i, s]

    def forward(i):
        pre = None
        for k in range(NY):
            term = lax.dot_general(
                x2[k], w_in[k, i], (((1,), (1,)), ((), ())), preferred_element_type=F32
            )
            pre = term if pre is None else pre + term
        pre = pre * scale_in
        square = pre * pre
        tangent = jnp.tanh(gelu_coef * (pre + cubic_coef * square * pre))
        hid[i] = (0.5 * pre * (1.0 + tangent)).astype(BF16).T
        pre_slope[i] = scale_out * (
            0.5 * (1.0 + tangent) + 0.5 * pre * (1.0 - tangent * tangent) * gelu_coef * (1.0 + 3.0 * cubic_coef * square)
        )

    def out_grads(i):
        for k in range(NY):
            d_out[i, k] = (jnp.dot(hid[i], g2[k], preferred_element_type=F32) * scale_out).astype(BF16)

    def hidden_grads(k, begin):
        for i in range(NX):
            term = lax.dot_general(
                g2[k], w_out[i, k], (((1,), (1,)), ((), ())), preferred_element_type=F32
            )
            grad_sum[i] = term if begin else grad_sum[i] + term

    def in_grads(k):
        for i in range(NX):
            d_in[k, i] = (jnp.dot(pg_t[i], x2[k], preferred_element_type=F32) * scale_in).astype(BF16)

    order = (0, 1, 3, 2)
    w_pair = [
        copies.start(w_stage.at[0], w_in.at[y, x, :, lanes_mine], mate),
        copies.start(w_stage.at[1], w_out.at[x, y, :, lanes_mine], mate),
    ]
    attn_sent = {}
    for q in (2, 1, 3, 0):
        at = (y + q) % NY
        attn_sent[q] = copies.start(attn_ref.at[at, 1 - core], a_mate.at[at], mate)
    reached(0)
    reach(1)
    arrive(*w_pair)
    in_big, out_big, in_last, out_last = {}, {}, {}, {}
    in_first = gather_first(in_x, X_RING)
    in_big[0] = gather_first(in_y(x), Y_RING)
    out_big[0] = gather_first(out_x(y), X_RING)
    reached(1)
    reach(2)
    row_i = lax.broadcasted_iota(jnp.int32, (256, 256), 0)
    col_i = lax.broadcasted_iota(jnp.int32, (256, 256), 1)
    perm[...] = jnp.where(col_i == ((row_i & 15) << 4) + (row_i >> 4), 1.0, 0.0).astype(BF16)

    ids_row = ids_ref[...].astype(F32)
    eye_t = lax.broadcasted_iota(jnp.int32, (n_tok, n_tok), 0)
    eye_s = lax.broadcasted_iota(jnp.int32, (n_tok, n_tok), 1)
    spread_ids = jnp.broadcast_to(ids_row, (n_tok, n_tok))
    ids_col = jnp.sum(jnp.where(eye_t == eye_s, spread_ids, 0.0), axis=1, keepdims=True)
    earlier = jnp.where((ids_col == spread_ids) & (eye_t < eye_s), 1.0, 0.0)
    rank_row = jnp.sum(earlier, axis=0, keepdims=True)
    slot_row = jnp.where(rank_row < CAP, ids_row * CAP + rank_row, -1.0)
    n_slot = disp.shape[0]
    slot_i = lax.broadcasted_iota(jnp.int32, (n_slot, n_tok), 0).astype(F32)
    disp[...] = jnp.where(slot_i == jnp.broadcast_to(slot_row, (n_slot, n_tok)), 1.0, 0.0).astype(BF16)
    gate_col = jnp.sum(
        jnp.where(eye_t == eye_s, jnp.broadcast_to(gate_ref[...], (n_tok, n_tok)), 0.0),
        axis=1, keepdims=True,
    )

    attn_ring = attn_begin(attn_sent)
    out_first = gather_first(out_y, Y_RING)
    pack(tok_ref[...], pk_t)
    x3[core, pl.ds(row_at(block, place), CAP)] = pk_t[pl.ds(block * CAP, CAP)]
    reached(2)
    t_state = z_begin(pk_t, x3)
    @pl.when(at_first)
    def _():
        zr[...] = jnp.zeros_like(zr)
        own_r[...] = jnp.zeros_like(own_r)

    @pl.when(at_last)
    def _():
        zl[...] = jnp.zeros_like(zl)
        own_l[...] = jnp.zeros_like(own_l)

    slots[BLOCKS * CAP:] = jnp.zeros((slots.shape[0] - BLOCKS * CAP, tiles, LANES), BF16)

    z_line(t_state, 1)
    scatter_middle(attn_ring, lambda i: a_sum.at[i], n_tok, a_r1, a_m3, a_r3, Y_RING)
    z_chain(t_state, 0, 1)
    in_next = gather_next(in_first, in_x, X_RING)
    for q in (1, 3):
        in_big[q] = gather_first(in_y((x + q) % NX), Y_RING)
    z_chain(t_state, 2, 3)
    z_line(t_state, 2)
    z_chain(t_state, 4)
    first, second = scatter_end(attn_ring, lambda i: a_sum.at[i], n_tok, a_r2, a_r3, Y_RING)
    summed = jnp.concatenate([first, second], axis=0)
    pack((gate_col * summed).astype(BF16), pk_g)
    g3[core, pl.ds(row_at(block, place), CAP)] = pk_g[pl.ds(block * CAP, CAP)]
    g_state = z_begin(pk_g, g3)
    z_chain(t_state, 5, 6)
    z_line(t_state, 3)
    arrive(*in_next)
    in_big[2] = gather_first(in_y((x + 2) % NX), Y_RING)
    out_next = gather_next(out_first, out_y, Y_RING)
    for q in (1, 3):
        out_big[q] = gather_first(out_x((y + q) % NY), X_RING)
    z_chain(t_state, 7, 8)
    t_share = [z_share(t_state, j) for j in range(4)]
    z_line(g_state, 1)
    z_chain(g_state, 0, 1)
    to_wide(x3, x2, core)
    in_last[0] = gather_next(in_big[0], in_y(x), Y_RING)
    out_last[0] = gather_next(out_big[0], out_x(y), X_RING)
    z_chain(g_state, 2)
    z_line(g_state, 2)
    arrive(*t_share)
    to_wide(x3, x2, 1 - core)
    z_chain(g_state, 3, 4)
    arrive(*out_next)
    out_big[2] = gather_first(out_x((y + 2) % NY), X_RING)
    in_last[1] = gather_next(in_big[1], in_y((x + 1) % NX), Y_RING)
    in_last[3] = gather_next(in_big[3], in_y((x + 3) % NX), Y_RING)
    z_chain(g_state, 5)
    z_line(g_state, 3)
    arrive(*in_last[0])
    forward(x)
    z_chain(g_state, 6, 7)
    out_last[1] = gather_next(out_big[1], out_x((y + 1) % NY), X_RING)
    out_last[3] = gather_next(out_big[3], out_x((y + 3) % NY), X_RING)
    arrive(*in_last[1], *in_last[3])
    z_chain(g_state, 8)
    g_share = [z_share(g_state, j) for j in range(4)]
    in_last[2] = gather_next(in_big[2], in_y((x + 2) % NX), Y_RING)
    out_last[2] = gather_next(out_big[2], out_x((y + 2) % NY), X_RING)
    forward((x + 1) % NX)
    forward((x + 3) % NX)
    to_wide(g3, g2, core)
    arrive(*in_last[2])
    forward((x + 2) % NX)
    arrive(*g_share)
    to_wide(g3, g2, 1 - core)
    def out_block(i):
        return d_out.at[i]

    def in_block(i):
        return d_in.at[i]

    out_grads((x + 2) % NX)
    out_ring = scatter_far(out_block, NY, o_r1, X_RING)
    for q in range(4):
        arrive(*out_last[q])
        hidden_grads((y + q) % NY, q == 0)
    for i in range(NX):
        grad = (grad_sum[i] * pre_slope[i]).astype(BF16)
        pg[i] = grad
        pg_t[i] = grad.T
    in_grads((y + 2) % NY)
    in_ring = scatter_far(in_block, NX, i_r1, Y_RING)
    out_grads((x + 1) % NX)
    out_grads((x + 3) % NX)
    scatter_near(out_ring, out_block, NY, o_r2, X_RING)
    in_grads((y + 1) % NY)
    in_grads((y + 3) % NY)
    scatter_near(in_ring, in_block, NX, i_r2, Y_RING)

    back = {}
    for part_i in range(2):
        half = (1 - core) if part_i == 0 else core
        for k in range(NY):
            term = None
            for i in range(NX):
                add = jnp.dot(
                    pg[i, pl.ds(pl.multiple_of(half * rows_d, rows_d), rows_d)], w_in[k, i],
                    preferred_element_type=F32,
                )
                term = add if term is None else term + add
            p2[k] = (term * scale_in).astype(BF16)
        to_narrow(p2, p3, half)
        if part_i == 0:
            for j in order:
                back[j] = back_share(j)
    scatter_middle(out_ring, out_block, NY, o_r1, o_m3, o_r3, X_RING)
    for j in order:
        back_sum(back[j], j)
    ends = {}
    back_chain(ends, 0)
    scatter_middle(in_ring, in_block, NX, i_r1, i_m3, i_r3, Y_RING)
    back_own()
    back_chain(ends, 1)
    out_grads(x)
    in_grads(y)
    back_chain(ends, 2, 3)
    first, second = scatter_end(out_ring, out_block, NY, o_r2, o_r3, X_RING)
    o_sum[0:2] = first.astype(BF16)
    o_sum[2:4] = second.astype(BF16)
    out_small = scatter_first(lambda i: o_sum.at[i], share, os_r1, os_r2, Y_RING)
    back_chain(ends, 4, 5)
    first, second = scatter_end(in_ring, in_block, NX, i_r2, i_r3, Y_RING)
    i_sum[0:2] = first.astype(BF16)
    i_sum[2:4] = second.astype(BF16)
    in_small = scatter_first(lambda i: i_sum.at[i], share, is_r1, is_r2, X_RING)
    back_chain(ends, 6)
    scatter_middle(out_small, lambda i: o_sum.at[i], share, os_r1, os_m3, os_r3, Y_RING)
    back_chain(ends, 7)
    scatter_middle(in_small, lambda i: i_sum.at[i], share, is_r1, is_m3, is_r3, X_RING)
    back_chain(ends, 8)
    back_own_end()
    pair = []
    for t, sent, sums, buf2, buf3, ring in (
        (1, out_small, o_sum, os_r2, os_r3, Y_RING), (0, in_small, i_sum, is_r2, is_r3, X_RING),
    ):
        low, high = halves(share)
        first, second = scatter_end(sent, lambda i: sums.at[i], share, buf2, buf3, ring)
        d_part[t, low] = first.astype(BF16)
        d_part[t, high] = second.astype(BF16)
        pair.append(copies.start(d_part.at[t, :, lanes_other], d_other.at[t], mate))

    back_chain_end(ends)
    wide = []
    for g in range(n_slot // 16):
        moved = jnp.dot(
            perm[...], slots[g * 16:(g + 1) * 16].reshape(256, LANES), preferred_element_type=F32
        ).astype(BF16)
        wide.append(jnp.concatenate([moved[k * 16:(k + 1) * 16] for k in range(tiles)], axis=1))
    slots_wide = jnp.concatenate(wide, axis=0)
    tg_ref[...] = lax.dot_general(
        disp[...], slots_wide, (((0,), (0,)), ((), ())), preferred_element_type=F32
    ).astype(BF16)

    for t, copy, old, new in ((1, pair[0], wout_ref, nwout_ref), (0, pair[1], win_ref, nwin_ref)):
        new[mine] = old[mine] - step_rate * d_part[t, :, lanes_mine].astype(F32)
        copy.wait_recv()
        new[other] = old[other] - step_rate * d_other[t].astype(F32)
    copies.finish()


def hand_over(*refs):
    for source, target in zip(refs[:3], refs[3:]):
        target[...] = source[...]


def shards(tokens, attn_partials, expert_ids, gate, w_in, w_out):
    n_tok, width = tokens.shape
    w_in_t, w_out_t = w_in.T, w_out.T
    hidden = w_in_t.shape[0]
    tiles = width // LANES
    rows_b = LINE * CAP
    rows_d = BLOCKS * rows_b
    share = hidden // 2
    depth = width // NY
    slot_rows = 48
    vmem = pl.BlockSpec(memory_space=pltpu.VMEM)

    def bf16(*shape):
        return pltpu.VMEM(shape, BF16)

    def rows16(*lead):
        return bf16(*lead, tiles, LANES)

    scratch = [
        rows16(slot_rows), rows16(slot_rows), rows16(2, rows_d), rows16(2, rows_d),
        bf16(NY, 2 * rows_d, depth), bf16(NY, 2 * rows_d, depth),
        bf16(256, 256), bf16(slot_rows, n_tok),
        bf16(2, share, depth // 2), bf16(NY, NX, share, depth), bf16(NX, NY, share, depth),
        pltpu.VMEM((NX, 2 * rows_d, share), F32), pltpu.VMEM((NX, 2 * rows_d, share), F32),
        bf16(NX, 2 * rows_d, share), bf16(NX, share, 2 * rows_d), bf16(NX, share, 2 * rows_d),
        bf16(NY, rows_d, depth), rows16(2, rows_d), rows16(rows_d),
        rows16(rows_d), rows16(CHAIN, 2 * CAP), rows16(CHAIN, 2 * CAP), rows16(CHAIN, 2 * CAP), rows16(CHAIN, 2 * CAP),
        rows16(LINE, CAP), rows16(LINE, CAP), rows16(LINE, CAP), rows16(LINE, CAP), rows16(slot_rows),
        bf16(NY, n_tok, width), bf16(NY, n_tok, width),
    ]
    scratch += [bf16(2, n_tok // 2, width)] * 4
    for _ in range(2):
        scratch += [bf16(4, 4, share, depth)] + [bf16(2, 2, share, depth)] * 4
        scratch += [bf16(4, share, depth)] + [bf16(2, share // 2, depth)] * 4
    scratch += [bf16(2, share, depth), bf16(2, share, depth // 2)]
    scratch += [pltpu.SemaphoreType.DMA((N_COPIES,)), pltpu.SemaphoreType.DMA((N_COPIES,))]
    scratch += [pltpu.SemaphoreType.REGULAR((3,))]
    token_grad, new_in, new_out = pl.pallas_call(
        functools.partial(kernel, (width, hidden)),
        out_shape=(
            jax.ShapeDtypeStruct((n_tok, width), BF16),
            jax.ShapeDtypeStruct(w_in_t.shape, F32),
            jax.ShapeDtypeStruct(w_out_t.shape, F32),
        ),
        in_specs=[vmem] * 6,
        out_specs=(vmem, vmem, vmem),
        scratch_shapes=scratch,
        compiler_params=pltpu.CompilerParams(
            collective_id=0, has_side_effects=True, vmem_limit_bytes=60 * 1024 * 1024
        ),
    )(
        tokens,
        attn_partials.reshape(NY, 2, n_tok, width),
        expert_ids.reshape(1, n_tok),
        gate.reshape(1, n_tok),
        w_in_t,
        w_out_t,
    )
    results = (token_grad, new_in, new_out)
    token_grad, new_in, new_out = pl.pallas_call(
        hand_over,
        out_shape=tuple(jax.ShapeDtypeStruct(r.shape, r.dtype) for r in results),
        in_specs=[vmem] * 3,
        out_specs=(vmem, vmem, vmem),
    )(*results)
    return token_grad, new_in.T, new_out.T


def solution(mesh):
    in_specs = (
        P(("expert", "dp"), None),
        P("dp", "expert", None),
        P(("expert", "dp")),
        P(("expert", "dp")),
        P("dp", "expert"),
        P("dp", "expert"),
    )
    out_specs = (P(("expert", "dp"), None), P("dp", "expert"), P("dp", "expert"))
    return jax.shard_map(shards, mesh=mesh, in_specs=in_specs, out_specs=out_specs, check_vma=False)
```

```python
import functools

import jax
import jax.numpy as jnp
from jax import lax
from jax.experimental import pallas as pl
from jax.experimental.pallas import tpu as pltpu
from jax.sharding import PartitionSpec as P

NX = 4
NY = 4
LINE = 4
BLOCKS = 4
CAP = 10
LANES = 128
MESH = pl.DeviceIdType.MESH

gelu_coef = 0.7978845608028654
cubic_coef = 0.044715
step_rate = 0.5
F32 = jnp.float32
BF16 = jnp.bfloat16


def add16(*terms):
    total = terms[0].astype(F32)
    for term in terms[1:]:
        total = total + term.astype(F32)
    return total.astype(BF16)


class Copy:
    def __init__(self, copy, when):
        self.copy = copy
        self.when = when

    def wait_recv(self, when=None):
        guarded(when, self.copy.wait_recv)


def guarded(when, action):
    if when is None:
        action()
    else:
        pl.when(when)(action)


class Copies:
    def __init__(self, send_sems, recv_sems):
        self.send_sems = send_sems
        self.recv_sems = recv_sems
        self.sends = 0
        self.recvs = 0
        self.started = []

    def slots(self, count):
        first = self.recvs
        self.recvs += count
        return first

    def send_slots(self, count):
        first = self.sends
        self.sends += count
        return first

    def make(self, src, dst, device, recv=None, send=None):
        if recv is None:
            recv = self.slots(1)
        if send is None:
            send = self.sends
            self.sends += 1
        return pltpu.make_async_remote_copy(
            src_ref=src,
            dst_ref=dst,
            send_sem=self.send_sems.at[send],
            recv_sem=self.recv_sems.at[recv],
            device_id=device,
            device_id_type=MESH,
        )

    def start(self, src, dst, device, when=None, recv=None):
        copy = Copy(self.make(src, dst, device, recv), when)
        guarded(when, copy.copy.start)
        self.started.append(copy)
        return copy

    def finish(self):
        for copy in self.started:
            guarded(copy.when, copy.copy.wait_send)


N_COPIES = 384
CHAIN = 3
LAG = 2


def kernel(
    dims,
    tok_ref, attn_ref, ids_ref, gate_ref, win_ref, wout_ref,
    tg_ref, nwin_ref, nwout_ref,
    pk_t, pk_g, x3, g3, x2, g2, perm, disp,
    w_stage, w_in, w_out, pre_slope, grad_sum, pg, pg_t, hid, p2, p3, p_mate,
    q3, zr, zl, zs_r, zs_l, own_r, own_l, own_sr, own_sl, slots,
    a_mate, a_sum, a_r1, a_m3, a_r3, a_r2,
    d_in, i_r1, i_m3, i_r3, i_r2, i_sum, is_r1, is_m3, is_r3, is_r2,
    d_out, o_r1, o_m3, o_r3, o_r2, o_sum, os_r1, os_m3, os_r3, os_r2,
    d_part, d_other,
    send_sems, recv_sems, reach_sems,
):
    width, hidden = dims
    scale_in = width ** (-0.5)
    scale_out = (hidden * NX * LINE) ** (-0.5)
    tiles = width // LANES
    share = hidden // 2
    depth = width // NY
    expert = lax.axis_index("expert")
    dp = lax.axis_index("dp")
    z = expert // NX
    x = expert % NX
    block = z // LINE
    place = z % LINE
    y = dp // 2
    core = dp % 2
    rows_b = LINE * CAP
    rows_d = BLOCKS * rows_b

    right = (z * NX + (x + 1) % NX, dp)
    left = (z * NX + (x + NX - 1) % NX, dp)
    up = (expert, ((y + 1) % NY) * 2 + core)
    down = (expert, ((y + NY - 1) % NY) * 2 + core)
    mate = (expert, y * 2 + (1 - core))

    last = LINE - 1
    not_first, not_last = place > 0, place < last
    at_first, at_last = place == 0, place == last
    front = ((z + 1) % (BLOCKS * LINE) * NX + x, dp)
    back_z = ((z + BLOCKS * LINE - 1) % (BLOCKS * LINE) * NX + x, dp)

    def seat(step, at):
        return ((((block + step + BLOCKS) % BLOCKS) * LINE + at) * NX + x, dp)

    def z_step(step):
        return ((z + step + BLOCKS * LINE) % (BLOCKS * LINE) * NX + x, dp)

    barrier = pltpu.get_barrier_semaphore()
    near = (right, left, up, down, mate, front, back_z)
    for device in near:
        pl.semaphore_signal(barrier, inc=1, device_id=device, device_id_type=MESH)

    def reach(round_index):
        for step in ((1, -1), (2, -2), (4, -4))[round_index]:
            pl.semaphore_signal(
                reach_sems.at[round_index], inc=1, device_id=z_step(step), device_id_type=MESH
            )

    def reached(round_index):
        pl.semaphore_wait(reach_sems.at[round_index], 2)

    copies = Copies(send_sems, recv_sems)

    def arrive(*waiting):
        for copy in waiting:
            copy.wait_recv()

    n_tok = tok_ref.shape[0]

    def pack(rows, dst):
        n_slot = disp.shape[0]
        packed = jnp.dot(disp[...], rows, preferred_element_type=F32).astype(BF16)
        for g in range(n_slot // 16):
            stacked = jnp.concatenate(
                [packed[g * 16:(g + 1) * 16, k * LANES:(k + 1) * LANES] for k in range(tiles)], axis=0
            )
            moved = jnp.dot(perm[...], stacked, preferred_element_type=F32).astype(BF16)
            dst[g * 16:(g + 1) * 16] = moved.reshape(16, tiles, LANES)

    per = depth // LANES

    def to_wide(src, dst, half):
        def body(i, carry):
            pair = [src[half, pl.ds(i * 32 + h * 16, 16)].reshape(256, LANES) for h in range(2)]
            moved = jnp.dot(perm[...], jnp.concatenate(pair, axis=1), preferred_element_type=F32).astype(BF16)
            for h in range(2):
                at = pl.ds(pl.multiple_of(half * rows_d + i * 32 + h * 16, 16), 16)
                for k in range(tiles):
                    dst[k // per, at, (k % per) * LANES:(k % per + 1) * LANES] = moved[
                        k * 16:(k + 1) * 16, h * LANES:(h + 1) * LANES
                    ]
            return carry

        lax.fori_loop(0, rows_d // 32, body, 0, unroll=True)

    def to_narrow(src, dst, half):
        def body(i, carry):
            pair = []
            for h in range(2):
                at = pl.ds(pl.multiple_of(i * 32 + h * 16, 16), 16)
                pair.append(jnp.concatenate(
                    [src[k // per, at, (k % per) * LANES:(k % per + 1) * LANES] for k in range(tiles)], axis=0
                ))
            moved = jnp.dot(perm[...], jnp.concatenate(pair, axis=1), preferred_element_type=F32).astype(BF16)
            for h in range(2):
                dst[half, pl.ds(i * 32 + h * 16, 16)] = moved[:, h * LANES:(h + 1) * LANES].reshape(16, tiles, LANES)
            return carry

        lax.fori_loop(0, rows_d // 32, body, 0, unroll=True)

    def row_at(c, p):
        return c * rows_b + p * CAP

    mine = pl.ds(pl.multiple_of(core * share, share), share)
    other = pl.ds(pl.multiple_of((1 - core) * share, share), share)
    lanes_mine = pl.ds(pl.multiple_of(core * (depth // 2), depth // 2), depth // 2)
    lanes_other = pl.ds(pl.multiple_of((1 - core) * (depth // 2), depth // 2), depth // 2)
    w_in[y, x, :, lanes_mine] = win_ref[mine].astype(BF16)
    w_out[x, y, :, lanes_mine] = wout_ref[mine].astype(BF16)
    w_stage[0] = win_ref[other].astype(BF16)
    w_stage[1] = wout_ref[other].astype(BF16)
    pl.semaphore_wait(barrier, len(near))
    reach(0)

    def halves(count):
        return pl.ds(0, count // 2), pl.ds(count // 2, count // 2)

    X_RING = (x, right, left)
    Y_RING = (y, up, down)

    def gather_first(blk, ring):
        pos, upper, lower = ring
        return [copies.start(blk(pos), blk(pos), device) for device in (upper, lower)]

    def gather_next(sent, blk, ring):
        pos, upper, lower = ring
        low, high = halves(share)
        below, above = (pos + 3) % 4, (pos + 1) % 4
        sent[0].wait_recv()
        to_up = copies.start(blk(below).at[low], blk(below).at[low], upper)
        sent[1].wait_recv()
        to_down = copies.start(blk(above).at[high], blk(above).at[high], lower)
        return [to_up, to_down]

    def scatter_far(blk, count, buf1, ring):
        pos, upper, lower = ring
        low, high = halves(count)
        far = (pos + 2) % 4
        return {
            "u1": copies.start(blk(far).at[low], buf1.at[0], upper),
            "d1": copies.start(blk(far).at[high], buf1.at[1], lower),
        }

    def scatter_near(sent, blk, count, buf2, ring):
        pos, upper, lower = ring
        low, high = halves(count)
        sent["u2"] = copies.start(blk((pos + 1) % 4).at[high], buf2.at[0], upper)
        sent["d2"] = copies.start(blk((pos + 3) % 4).at[low], buf2.at[1], lower)

    def scatter_first(blk, count, buf1, buf2, ring):
        sent = scatter_far(blk, count, buf1, ring)
        scatter_near(sent, blk, count, buf2, ring)
        return sent

    def scatter_middle(sent, blk, count, buf1, mid, buf3, ring):
        pos, upper, lower = ring
        low, high = halves(count)
        sent["u1"].wait_recv()
        mid[0] = add16(buf1[0], blk((pos + 1) % 4).at[low][...])
        sent["u3"] = copies.start(mid.at[0], buf3.at[0], upper)
        sent["d1"].wait_recv()
        mid[1] = add16(buf1[1], blk((pos + 3) % 4).at[high][...])
        sent["d3"] = copies.start(mid.at[1], buf3.at[1], lower)

    def scatter_end(sent, blk, count, buf2, buf3, ring):
        low, high = halves(count)
        pos = ring[0]
        arrive(sent["d2"], sent["u3"])
        first = blk(pos).at[low][...].astype(F32) + buf2[1].astype(F32) + buf3[0].astype(F32)
        arrive(sent["u2"], sent["d3"])
        second = blk(pos).at[high][...].astype(F32) + buf2[0].astype(F32) + buf3[1].astype(F32)
        return first, second

    def attn_begin(sent):
        low, high = halves(n_tok)
        out = {}
        for q in (2, 1, 3, 0):
            at = (y + q) % NY
            sent[q].wait_recv()
            a_sum[at] = add16(attn_ref[at, core], a_mate[at])
            if q == 2:
                out["u1"] = copies.start(a_sum.at[at, low], a_r1.at[0], up)
                out["d1"] = copies.start(a_sum.at[at, high], a_r1.at[1], down)
            elif q == 1:
                out["u2"] = copies.start(a_sum.at[at, high], a_r2.at[0], up)
            elif q == 3:
                out["d2"] = copies.start(a_sum.at[at, low], a_r2.at[1], down)
        return out

    def chunk(j):
        return (block + BLOCKS + j) % BLOCKS

    def z_begin(packed, rows):
        here = pl.ds(row_at(block, place), CAP)
        mine_at = pl.ds(block * CAP, CAP)
        state = {"rows": rows, "edge": {}, "relay": {}}
        state["r1"] = copies.start(packed.at[mine_at], rows.at[core, here], front, not_last)
        state["l1"] = copies.start(packed.at[mine_at], rows.at[core, here], back_z, not_first)
        for step in (1, 2):
            for sign in (1, -1):
                first = copies.slots(LINE)
                sends = None if step == 1 else (place >= 2 if sign == 1 else place < 2)
                copies.start(
                    packed.at[pl.ds(chunk(sign * step) * CAP, CAP)], rows.at[core, here],
                    seat(sign * step, 0 if sign == 1 else last), sends, recv=first + place,
                )
                state["edge"][sign * step] = first
        for sign in (1, -1):
            state["relay"][sign] = (copies.slots(CHAIN), copies.send_slots(CHAIN))
        return state

    def z_line(state, n):
        rows = state["rows"]
        for key, sign, ahead, came, go in (("r", 1, front, place >= n, not_last), ("l", -1, back_z, place + n <= last, not_first)):
            state[key + str(n)].wait_recv(came)
            if n < last:
                at = pl.ds(row_at(block, jnp.clip(place - sign * n, 0, last)), CAP)
                state[key + str(n + 1)] = copies.start(rows.at[core, at], rows.at[core, at], ahead, came & go)

    directions = (
        (1, front, at_first, not_first, not_last, place), (-1, back_z, at_last, not_last, not_first, last - place),
    )

    def pair_place(sign, k):
        return 2 * (1 - k % 2) if sign == 1 else 2 * (k % 2)

    def z_chain(state, *times):
        rows = state["rows"]

        def view(sign, k):
            from_block = (block + BLOCKS - sign * (1 + k // 2)) % BLOCKS
            return rows.at[core, pl.ds(row_at(from_block, pair_place(sign, k)), 2 * CAP)]

        for t in times:
            for sign, ahead, entry, inner, go, rank in directions:
                recv, send = state["relay"][sign]
                if t < CHAIN:
                    at = view(sign, t)
                    first = state["edge"][sign * (1 + t // 2)] + pair_place(sign, t)
                    start = copies.make(at, at, ahead, recv + t, send + t)
                    half_at = rows.at[core, pl.ds(row_at(0, 0), CAP)]
                    arrivals = [copies.make(half_at, half_at, mate, first + n, 0) for n in range(2)]

                    def enter(start=start, arrivals=arrivals):
                        for copy in arrivals:
                            copy.wait_recv()
                        start.start()

                    pl.when(entry)(enter)
                k = t - LAG * rank
                safe = jnp.clip(k, 0, CHAIN - 1)
                at = view(sign, safe)
                relay = copies.make(at, at, ahead, recv + safe, send + safe)

                def pass_on(relay=relay, go=go):
                    relay.wait_recv()
                    pl.when(go)(relay.start)

                pl.when(inner & (k >= 0) & (k < CHAIN))(pass_on)
                if t == CHAIN - 1 + LAG * last:
                    for n in range(CHAIN):
                        sent = copies.make(view(sign, n), view(sign, n), ahead, recv + n, send + n)
                        copies.started.append(Copy(sent, go))

    def z_share(state, j):
        at = state["rows"].at[core, pl.ds(row_at(chunk(j), 0), rows_b)]
        return copies.start(at, at, mate)

    def back_share(j):
        at = pl.ds(row_at(chunk(j), 0), rows_b)
        return copies.start(p3.at[1 - core, at], p_mate.at[at], mate)

    def back_sum(copy, j):
        at = pl.ds(row_at(chunk(j), 0), rows_b)
        copy.wait_recv()
        q3[at] = add16(p3[core, at], p_mate[at])

    def back_chain(state, *times):
        if not state:
            for sign in (1, -1):
                state[sign] = (copies.slots(CHAIN), copies.send_slots(CHAIN), copies.slots(2), copies.send_slots(2 * CHAIN))
        for t in times:
            for (sign, ahead, entry, inner, go, rank), buf, out in zip(directions, (zr, zl), (zs_r, zs_l)):
                recv, send, end, send_end = state[sign]
                k = t - LAG * rank
                safe = jnp.clip(k, 0, CHAIN - 1)
                step = 1 + safe // 2
                to_block = (block + BLOCKS + sign * step) % BLOCKS
                first = pair_place(-sign, safe)
                relay = copies.make(out.at[safe], buf.at[safe], ahead, recv + safe, send + safe)
                leaving = [
                    copies.make(
                        out.at[safe, pl.ds(n * CAP, CAP)], slots.at[pl.ds(block * CAP, CAP)],
                        ((to_block * LINE + first + n) * NX + x, dp), end + safe // 2, send_end + 2 * safe + n,
                    )
                    for n in range(2)
                ]

                def pass_on(
                    relay=relay, leaving=leaving, inner=inner, go=go, buf=buf, out=out, safe=safe,
                    at=pl.ds(row_at(to_block, first), 2 * CAP),
                ):
                    pl.when(inner)(relay.wait_recv)
                    out[safe] = add16(q3[at], buf[safe])
                    pl.when(go)(relay.start)

                    @pl.when(jnp.logical_not(go))
                    def _():
                        for copy in leaving:
                            copy.start()

                pl.when((k >= 0) & (k < CHAIN))(pass_on)
                if t == CHAIN - 1 + LAG * last:
                    for n in range(CHAIN):
                        sent = copies.make(out.at[n], buf.at[n], ahead, recv + n, send + n)
                        copies.started.append(Copy(sent, go))
                    for n in range(2 * CHAIN):
                        at = out.at[n // 2, pl.ds(0, CAP)]
                        sent = copies.make(at, at, ahead, end, send_end + n)
                        copies.started.append(Copy(sent, jnp.logical_not(go)))

    def back_chain_end(state):
        at = slots.at[pl.ds(0, CAP)]
        for sign in (1, -1):
            end = state[sign][2]
            for n, came in ((0, None), (1, place < 2 if sign == 1 else place >= 2)):
                guarded(came, copies.make(at, at, mate, end + n, 0).wait_recv)

    def back_own():
        for n in (3, 2, 1):
            for key, sign, ahead, buf, out in (("r", 1, front, own_r, own_sr), ("l", -1, back_z, own_l, own_sl)):
                target = place + sign * n
                valid = (target >= 0) & (target <= last)
                at = pl.ds(row_at(block, jnp.clip(target, 0, last)), CAP)
                behind = (place - sign >= 0) & (place - sign <= last)
                if n < last:
                    own_state[key + str(n + 1)].wait_recv(valid & behind)
                out[n - 1] = add16(q3[at], buf[n])
                own_state[key + str(n)] = copies.start(out.at[n - 1], buf.at[n - 1], ahead, valid)

    def back_own_end():
        own_state["r1"].wait_recv(not_first)
        own_state["l1"].wait_recv(not_last)
        slots[pl.ds(block * CAP, CAP)] = add16(q3[pl.ds(row_at(block, place), CAP)], own_r[0], own_l[0])

    own_state = {}

    def in_x(i):
        return w_in.at[y, i]

    def out_y(i):
        return w_out.at[x, i]

    def in_y(s):
        return lambda i: w_in.at[i, s]

    def out_x(s):
        return lambda i: w_out.at[i, s]

    def forward(i):
        pre = None
        for k in range(NY):
            term = lax.dot_general(
                x2[k], w_in[k, i], (((1,), (1,)), ((), ())), preferred_element_type=F32
            )
            pre = term if pre is None else pre + term
        pre = pre * scale_in
        square = pre * pre
        tangent = jnp.tanh(gelu_coef * (pre + cubic_coef * square * pre))
        hid[i] = (0.5 * pre * (1.0 + tangent)).astype(BF16).T
        pre_slope[i] = scale_out * (
            0.5 * (1.0 + tangent) + 0.5 * pre * (1.0 - tangent * tangent) * gelu_coef * (1.0 + 3.0 * cubic_coef * square)
        )

    def out_grads(i):
        for k in range(NY):
            d_out[i, k] = (jnp.dot(hid[i], g2[k], preferred_element_type=F32) * scale_out).astype(BF16)

    def hidden_grads(k, begin):
        for i in range(NX):
            term = lax.dot_general(
                g2[k], w_out[i, k], (((1,), (1,)), ((), ())), preferred_element_type=F32
            )
            grad_sum[i] = term if begin else grad_sum[i] + term

    def in_grads(k):
        for i in range(NX):
            d_in[k, i] = (jnp.dot(pg_t[i], x2[k], preferred_element_type=F32) * scale_in).astype(BF16)

    order = (0, 1, 3, 2)
    w_pair = [
        copies.start(w_stage.at[0], w_in.at[y, x, :, lanes_mine], mate),
        copies.start(w_stage.at[1], w_out.at[x, y, :, lanes_mine], mate),
    ]
    attn_sent = {}
    for q in (2, 1, 3, 0):
        at = (y + q) % NY
        attn_sent[q] = copies.start(attn_ref.at[at, 1 - core], a_mate.at[at], mate)
    reached(0)
    reach(1)
    arrive(*w_pair)
    in_big, out_big, in_last, out_last = {}, {}, {}, {}
    in_first = gather_first(in_x, X_RING)
    in_big[0] = gather_first(in_y(x), Y_RING)
    out_big[0] = gather_first(out_x(y), X_RING)
    reached(1)
    reach(2)
    row_i = lax.broadcasted_iota(jnp.int32, (256, 256), 0)
    col_i = lax.broadcasted_iota(jnp.int32, (256, 256), 1)
    perm[...] = jnp.where(col_i == ((row_i & 15) << 4) + (row_i >> 4), 1.0, 0.0).astype(BF16)

    ids_row = ids_ref[...].astype(F32)
    eye_t = lax.broadcasted_iota(jnp.int32, (n_tok, n_tok), 0)
    eye_s = lax.broadcasted_iota(jnp.int32, (n_tok, n_tok), 1)
    spread_ids = jnp.broadcast_to(ids_row, (n_tok, n_tok))
    ids_col = jnp.sum(jnp.where(eye_t == eye_s, spread_ids, 0.0), axis=1, keepdims=True)
    earlier = jnp.where((ids_col == spread_ids) & (eye_t < eye_s), 1.0, 0.0)
    rank_row = jnp.sum(earlier, axis=0, keepdims=True)
    slot_row = jnp.where(rank_row < CAP, ids_row * CAP + rank_row, -1.0)
    n_slot = disp.shape[0]
    slot_i = lax.broadcasted_iota(jnp.int32, (n_slot, n_tok), 0).astype(F32)
    disp[...] = jnp.where(slot_i == jnp.broadcast_to(slot_row, (n_slot, n_tok)), 1.0, 0.0).astype(BF16)
    gate_col = jnp.sum(
        jnp.where(eye_t == eye_s, jnp.broadcast_to(gate_ref[...], (n_tok, n_tok)), 0.0),
        axis=1, keepdims=True,
    )

    attn_ring = attn_begin(attn_sent)
    out_first = gather_first(out_y, Y_RING)
    pack(tok_ref[...], pk_t)
    x3[core, pl.ds(row_at(block, place), CAP)] = pk_t[pl.ds(block * CAP, CAP)]
    reached(2)
    t_state = z_begin(pk_t, x3)
    @pl.when(at_first)
    def _():
        zr[...] = jnp.zeros_like(zr)
        own_r[...] = jnp.zeros_like(own_r)

    @pl.when(at_last)
    def _():
        zl[...] = jnp.zeros_like(zl)
        own_l[...] = jnp.zeros_like(own_l)

    slots[BLOCKS * CAP:] = jnp.zeros((slots.shape[0] - BLOCKS * CAP, tiles, LANES), BF16)

    z_line(t_state, 1)
    scatter_middle(attn_ring, lambda i: a_sum.at[i], n_tok, a_r1, a_m3, a_r3, Y_RING)
    z_chain(t_state, 0, 1)
    in_next = gather_next(in_first, in_x, X_RING)
    for q in (1, 3):
        in_big[q] = gather_first(in_y((x + q) % NX), Y_RING)
    z_chain(t_state, 2, 3)
    z_line(t_state, 2)
    z_chain(t_state, 4)
    first, second = scatter_end(attn_ring, lambda i: a_sum.at[i], n_tok, a_r2, a_r3, Y_RING)
    summed = jnp.concatenate([first, second], axis=0)
    pack((gate_col * summed).astype(BF16), pk_g)
    g3[core, pl.ds(row_at(block, place), CAP)] = pk_g[pl.ds(block * CAP, CAP)]
    g_state = z_begin(pk_g, g3)
    z_chain(t_state, 5, 6)
    z_line(t_state, 3)
    arrive(*in_next)
    in_big[2] = gather_first(in_y((x + 2) % NX), Y_RING)
    out_next = gather_next(out_first, out_y, Y_RING)
    for q in (1, 3):
        out_big[q] = gather_first(out_x((y + q) % NY), X_RING)
    z_chain(t_state, 7, 8)
    t_share = [z_share(t_state, j) for j in range(4)]
    z_line(g_state, 1)
    z_chain(g_state, 0, 1)
    to_wide(x3, x2, core)
    in_last[0] = gather_next(in_big[0], in_y(x), Y_RING)
    out_last[0] = gather_next(out_big[0], out_x(y), X_RING)
    z_chain(g_state, 2)
    z_line(g_state, 2)
    arrive(*t_share)
    to_wide(x3, x2, 1 - core)
    z_chain(g_state, 3, 4)
    arrive(*out_next)
    out_big[2] = gather_first(out_x((y + 2) % NY), X_RING)
    in_last[1] = gather_next(in_big[1], in_y((x + 1) % NX), Y_RING)
    in_last[3] = gather_next(in_big[3], in_y((x + 3) % NX), Y_RING)
    z_chain(g_state, 5)
    z_line(g_state, 3)
    z_chain(g_state, 6, 7)
    out_last[1] = gather_next(out_big[1], out_x((y + 1) % NY), X_RING)
    out_last[3] = gather_next(out_big[3], out_x((y + 3) % NY), X_RING)
    arrive(*in_last[0])
    forward(x)
    z_chain(g_state, 8)
    g_share = [z_share(g_state, j) for j in range(4)]
    in_last[2] = gather_next(in_big[2], in_y((x + 2) % NX), Y_RING)
    out_last[2] = gather_next(out_big[2], out_x((y + 2) % NY), X_RING)
    arrive(*in_last[1], *in_last[3])
    forward((x + 1) % NX)
    forward((x + 3) % NX)
    to_wide(g3, g2, core)
    arrive(*in_last[2])
    forward((x + 2) % NX)
    arrive(*g_share)
    to_wide(g3, g2, 1 - core)
    def out_block(i):
        return d_out.at[i]

    def in_block(i):
        return d_in.at[i]

    out_grads((x + 2) % NX)
    out_ring = scatter_far(out_block, NY, o_r1, X_RING)
    for q in range(4):
        arrive(*out_last[q])
        hidden_grads((y + q) % NY, q == 0)
    for i in range(NX):
        grad = (grad_sum[i] * pre_slope[i]).astype(BF16)
        pg[i] = grad
        pg_t[i] = grad.T
    in_grads((y + 2) % NY)
    in_ring = scatter_far(in_block, NX, i_r1, Y_RING)
    out_grads((x + 1) % NX)
    out_grads((x + 3) % NX)
    scatter_near(out_ring, out_block, NY, o_r2, X_RING)
    in_grads((y + 1) % NY)
    in_grads((y + 3) % NY)
    scatter_near(in_ring, in_block, NX, i_r2, Y_RING)

    back = {}
    for part_i in range(2):
        half = (1 - core) if part_i == 0 else core
        for k in range(NY):
            term = None
            for i in range(NX):
                add = jnp.dot(
                    pg[i, pl.ds(pl.multiple_of(half * rows_d, rows_d), rows_d)], w_in[k, i],
                    preferred_element_type=F32,
                )
                term = add if term is None else term + add
            p2[k] = (term * scale_in).astype(BF16)
        to_narrow(p2, p3, half)
        if part_i == 0:
            for j in order:
                back[j] = back_share(j)
    scatter_middle(out_ring, out_block, NY, o_r1, o_m3, o_r3, X_RING)
    for j in order:
        back_sum(back[j], j)
    ends = {}
    back_chain(ends, 0)
    scatter_middle(in_ring, in_block, NX, i_r1, i_m3, i_r3, Y_RING)
    back_own()
    back_chain(ends, 1)
    out_grads(x)
    in_grads(y)
    back_chain(ends, 2, 3)
    first, second = scatter_end(out_ring, out_block, NY, o_r2, o_r3, X_RING)
    o_sum[0:2] = first.astype(BF16)
    o_sum[2:4] = second.astype(BF16)
    out_small = scatter_first(lambda i: o_sum.at[i], share, os_r1, os_r2, Y_RING)
    back_chain(ends, 4, 5)
    first, second = scatter_end(in_ring, in_block, NX, i_r2, i_r3, Y_RING)
    i_sum[0:2] = first.astype(BF16)
    i_sum[2:4] = second.astype(BF16)
    in_small = scatter_first(lambda i: i_sum.at[i], share, is_r1, is_r2, X_RING)
    back_chain(ends, 6)
    scatter_middle(out_small, lambda i: o_sum.at[i], share, os_r1, os_m3, os_r3, Y_RING)
    back_chain(ends, 7)
    scatter_middle(in_small, lambda i: i_sum.at[i], share, is_r1, is_m3, is_r3, X_RING)
    back_chain(ends, 8)
    back_own_end()
    pair = []
    for t, sent, sums, buf2, buf3, ring in (
        (1, out_small, o_sum, os_r2, os_r3, Y_RING), (0, in_small, i_sum, is_r2, is_r3, X_RING),
    ):
        low, high = halves(share)
        first, second = scatter_end(sent, lambda i: sums.at[i], share, buf2, buf3, ring)
        d_part[t, low] = first.astype(BF16)
        d_part[t, high] = second.astype(BF16)
        pair.append(copies.start(d_part.at[t, :, lanes_other], d_other.at[t], mate))

    back_chain_end(ends)
    wide = []
    for g in range(n_slot // 16):
        moved = jnp.dot(
            perm[...], slots[g * 16:(g + 1) * 16].reshape(256, LANES), preferred_element_type=F32
        ).astype(BF16)
        wide.append(jnp.concatenate([moved[k * 16:(k + 1) * 16] for k in range(tiles)], axis=1))
    slots_wide = jnp.concatenate(wide, axis=0)
    tg_ref[...] = lax.dot_general(
        disp[...], slots_wide, (((0,), (0,)), ((), ())), preferred_element_type=F32
    ).astype(BF16)

    for t, copy, old, new in ((1, pair[0], wout_ref, nwout_ref), (0, pair[1], win_ref, nwin_ref)):
        new[mine] = old[mine] - step_rate * d_part[t, :, lanes_mine].astype(F32)
        copy.wait_recv()
        new[other] = old[other] - step_rate * d_other[t].astype(F32)
    copies.finish()


def hand_over(*refs):
    for source, target in zip(refs[:3], refs[3:]):
        target[...] = source[...]


def shards(tokens, attn_partials, expert_ids, gate, w_in, w_out):
    n_tok, width = tokens.shape
    w_in_t, w_out_t = w_in.T, w_out.T
    hidden = w_in_t.shape[0]
    tiles = width // LANES
    rows_b = LINE * CAP
    rows_d = BLOCKS * rows_b
    share = hidden // 2
    depth = width // NY
    slot_rows = 48
    vmem = pl.BlockSpec(memory_space=pltpu.VMEM)

    def bf16(*shape):
        return pltpu.VMEM(shape, BF16)

    def rows16(*lead):
        return bf16(*lead, tiles, LANES)

    scratch = [
        rows16(slot_rows), rows16(slot_rows), rows16(2, rows_d), rows16(2, rows_d),
        bf16(NY, 2 * rows_d, depth), bf16(NY, 2 * rows_d, depth),
        bf16(256, 256), bf16(slot_rows, n_tok),
        bf16(2, share, depth // 2), bf16(NY, NX, share, depth), bf16(NX, NY, share, depth),
        pltpu.VMEM((NX, 2 * rows_d, share), F32), pltpu.VMEM((NX, 2 * rows_d, share), F32),
        bf16(NX, 2 * rows_d, share), bf16(NX, share, 2 * rows_d), bf16(NX, share, 2 * rows_d),
        bf16(NY, rows_d, depth), rows16(2, rows_d), rows16(rows_d),
        rows16(rows_d), rows16(CHAIN, 2 * CAP), rows16(CHAIN, 2 * CAP), rows16(CHAIN, 2 * CAP), rows16(CHAIN, 2 * CAP),
        rows16(LINE, CAP), rows16(LINE, CAP), rows16(LINE, CAP), rows16(LINE, CAP), rows16(slot_rows),
        bf16(NY, n_tok, width), bf16(NY, n_tok, width),
    ]
    scratch += [bf16(2, n_tok // 2, width)] * 4
    for _ in range(2):
        scratch += [bf16(4, 4, share, depth)] + [bf16(2, 2, share, depth)] * 4
        scratch += [bf16(4, share, depth)] + [bf16(2, share // 2, depth)] * 4
    scratch += [bf16(2, share, depth), bf16(2, share, depth // 2)]
    scratch += [pltpu.SemaphoreType.DMA((N_COPIES,)), pltpu.SemaphoreType.DMA((N_COPIES,))]
    scratch += [pltpu.SemaphoreType.REGULAR((3,))]
    token_grad, new_in, new_out = pl.pallas_call(
        functools.partial(kernel, (width, hidden)),
        out_shape=(
            jax.ShapeDtypeStruct((n_tok, width), BF16),
            jax.ShapeDtypeStruct(w_in_t.shape, F32),
            jax.ShapeDtypeStruct(w_out_t.shape, F32),
        ),
        in_specs=[vmem] * 6,
        out_specs=(vmem, vmem, vmem),
        scratch_shapes=scratch,
        compiler_params=pltpu.CompilerParams(
            collective_id=0, has_side_effects=True, vmem_limit_bytes=60 * 1024 * 1024
        ),
    )(
        tokens,
        attn_partials.reshape(NY, 2, n_tok, width),
        expert_ids.reshape(1, n_tok),
        gate.reshape(1, n_tok),
        w_in_t,
        w_out_t,
    )
    results = (token_grad, new_in, new_out)
    token_grad, new_in, new_out = pl.pallas_call(
        hand_over,
        out_shape=tuple(jax.ShapeDtypeStruct(r.shape, r.dtype) for r in results),
        in_specs=[vmem] * 3,
        out_specs=(vmem, vmem, vmem),
    )(*results)
    return token_grad, new_in.T, new_out.T


def solution(mesh):
    in_specs = (
        P(("expert", "dp"), None),
        P("dp", "expert", None),
        P(("expert", "dp")),
        P(("expert", "dp")),
        P("dp", "expert"),
        P("dp", "expert"),
    )
    out_specs = (P(("expert", "dp"), None), P("dp", "expert"), P("dp", "expert"))
    return jax.shard_map(shards, mesh=mesh, in_specs=in_specs, out_specs=out_specs, check_vma=False)
```
